32 devices in a mesh: wide: 8 (over y, x, core), narrow: 4 (over z).
Axes of the slice: x: 2, y: 2, z: 4, core: 2. Of those that a mesh axis runs over, the one named last changes fastest.
Arguments:
- raster: int32 [512, 1024], P('narrow', 'wide'), may hold values from 0 to 1
- transmission: bfloat16 [512, 1024], P('narrow', 'wide'), may hold values from 0.5 to 1.5
- kernels: float32 [8, 2, 64, 64], replicated, may hold values from -0.09375 to 0.09375
- kernel_weight: float32 [8], replicated, may hold values from 0.1 to 1
- library: bfloat16 [65536, 256], P(('wide', 'narrow')), may hold values from -40 to 40
- clip_tile: int32 [128], replicated, may hold values from 0 to 31, as said below
- clip_corner: int32 [2, 128], replicated, may hold values from 0 to 64
Outputs:
- aerial: float32 [512, 1024], P('narrow', 'wide')
- scores: float32 [128], P(('wide', 'narrow'))
The draws below stay inside these ranges and needn't reach their ends.
Inputs may be any that keep to these rules, and one draw needn't show every extreme that they name: `clip_tile`: each tile owns at most 16 clips, and some tile owns exactly 16.
All inputs are finite; a program needn't handle non-finite values.
Results may differ from the reference program's by a relative error of at most 0.0011.
Values may be sent and summed in bfloat16 or wider, within the bound.
No kernel may reach another device: no remote copies, remote signals or barrier semaphores. Data moves between devices by JAX's collectives and lax.ppermute only.
A program may use at most 64 MiB of HBM per device.

```python
import math
import jax
import jax.numpy as jnp
from jax import lax

TILE = 128
KERNELS = 8
KSIZE = 64
CLIP = 64
KSIG = 16
LIB_DEV = 2048
CAP = 16
SIGD = 256
GRID_COLS = 8
TILES = 32
NX = 512
NY = 1024
CLIPS = 128
LIB = 65536


def clip_owners(key):
    key_hot, key_order, key_shuffle = jax.random.split(jax.random.fold_in(key, 11), 3)
    slot_count = TILES * CAP
    busiest = jax.random.randint(key_hot, (), 0, TILES)
    slot_owner = jnp.arange(slot_count, dtype=jnp.int32) // CAP
    ranking = jax.random.permutation(key_order, slot_count).astype(jnp.int32)
    priority = jnp.where(slot_owner == busiest, -1, ranking)
    chosen = jnp.argsort(priority, stable=True)[:CLIPS]
    chosen = chosen[jax.random.permutation(key_shuffle, CLIPS)]
    return (chosen // CAP).astype(jnp.int32)


def layout_draws(key):
    key_raster, key_light, key_taps, key_weight, key_corner = jax.random.split(jax.random.fold_in(key, 5), 5)
    raster = jax.random.randint(key_raster, (NX, NY), 0, 2, dtype=jnp.int32)
    transmission = jax.random.uniform(key_light, (NX, NY), jnp.float32, 0.5, 1.5).astype(jnp.bfloat16)
    kernels = jnp.clip(jax.random.normal(key_taps, (KERNELS, 2, KSIZE, KSIZE), jnp.float32), -4.0, 4.0) * (math.sqrt(2.0) / KSIZE)
    log_weight = jax.random.uniform(key_weight, (KERNELS,), jnp.float32, math.log(0.1), 0.0)
    kernel_weight = jnp.clip(jnp.exp(log_weight), 0.1, 1.0)
    clip_corner = jax.random.randint(key_corner, (2, CLIPS), 0, TILE - CLIP + 1, dtype=jnp.int32)
    return (raster, transmission, kernels, kernel_weight, clip_corner)


def dct_table():
    freq_index = jnp.arange(KSIG, dtype=jnp.float32)[:, None]
    pixel_index = jnp.arange(CLIP, dtype=jnp.float32)[None, :]
    weights = jnp.where(freq_index == 0, jnp.sqrt(jnp.float32(1.0 / CLIP)), jnp.sqrt(jnp.float32(2.0 / CLIP)))
    return weights * jnp.cos(jnp.pi * (pixel_index + 0.5) * freq_index / CLIP)


def complex_product(formula, left_real, left_imag, right_real, right_imag):
    highest = lax.Precision.HIGHEST

    def single(left_operand, right_operand):
        return jnp.einsum(formula, left_operand, right_operand, precision=highest)
    real_part = single(left_real, right_real) - single(left_imag, right_imag)
    imag_part = single(left_real, right_imag) + single(left_imag, right_real)
    return (real_part, imag_part)


def drawn_units(key, planted_count):
    raster, transmission, kernels, kernel_weight, clip_corner = layout_draws(key)
    clip_tile = clip_owners(key)
    highest = lax.Precision.HIGHEST
    half_width = KSIZE // 2
    mask_values = raster.astype(jnp.float32) * transmission.astype(jnp.float32)
    padded = jnp.pad(mask_values, ((half_width, half_width), (half_width, half_width)))
    patch_size = CLIP + KSIZE
    grid_index = jnp.arange(patch_size, dtype=jnp.int32)
    phase_angle = 2.0 * math.pi / patch_size * jnp.mod(grid_index[:, None] * grid_index[None, :], patch_size).astype(jnp.float32)
    cosine_table = jnp.cos(phase_angle)
    sine_table = jnp.sin(phase_angle)
    taps_cos = cosine_table[:, :KSIZE]
    taps_sin = sine_table[:, :KSIZE]
    section_real, section_imag = complex_product('ai,kij->kaj', taps_cos, taps_sin, kernels[:, 0], kernels[:, 1])
    gain_real, gain_imag = complex_product('kaj,bj->kab', section_real, section_imag, taps_cos, taps_sin)
    out_cos = cosine_table[:CLIP]
    out_sin = sine_table[:CLIP]
    dct_rows = dct_table()
    keep_mask = (jnp.arange(SIGD, dtype=jnp.int32) != 0).astype(jnp.float32)
    picked = jax.random.permutation(jax.random.fold_in(key, 29), CLIPS)[:planted_count]
    row_first = (clip_tile // GRID_COLS * TILE + clip_corner[0])[picked].astype(jnp.int32)
    col_first = (clip_tile % GRID_COLS * TILE + clip_corner[1])[picked].astype(jnp.int32)
    scale_factor = 1.0 / (patch_size * patch_size)

    def one_clip(corner_pair):
        patch_cells = lax.dynamic_slice(padded, (corner_pair[0], corner_pair[1]), (patch_size, patch_size))
        half_real = jnp.dot(cosine_table, patch_cells, precision=highest)
        half_imag = -jnp.dot(sine_table, patch_cells, precision=highest)
        spec_real = jnp.dot(half_real, cosine_table, precision=highest) + jnp.dot(half_imag, sine_table, precision=highest)
        spec_imag = jnp.dot(half_imag, cosine_table, precision=highest) - jnp.dot(half_real, sine_table, precision=highest)
        filt_real = spec_real[None] * gain_real - spec_imag[None] * gain_imag
        filt_imag = spec_real[None] * gain_imag + spec_imag[None] * gain_real
        left_real, left_imag = complex_product('xa,kab->kxb', out_cos, out_sin, filt_real, filt_imag)
        field_real, field_imag = complex_product('kxb,yb->kxy', left_real, left_imag, out_cos, out_sin)
        energy = (field_real * scale_factor) ** 2 + (field_imag * scale_factor) ** 2
        window = jnp.einsum('k,kxy->xy', kernel_weight, energy, precision=highest)
        halfway = jnp.dot(dct_rows, window, precision=highest)
        signature = jnp.dot(halfway, dct_rows.T, precision=highest).reshape(SIGD) * keep_mask
        return signature / jnp.sqrt(jnp.sum(signature * signature) + 1e-12)
    return lax.map(one_clip, jnp.stack([row_first, col_first], axis=1))


def draw_raster(key, part):
    return layout_draws(key)[0]


def draw_transmission(key, part):
    return layout_draws(key)[1]


def draw_kernels(key, part):
    return layout_draws(key)[2]


def draw_kernel_weight(key, part):
    return layout_draws(key)[3]


def draw_clip_corner(key, part):
    return layout_draws(key)[4]


def draw_clip_tile(key, part):
    return clip_owners(key)


def draw_library(key, part):
    planted_count = CLIPS // 4
    clip_units = drawn_units(key, planted_count)
    key_list = jax.random.split(jax.random.fold_in(key, 23), 9)
    magnitude = jnp.exp(jax.random.uniform(key_list[0], (LIB, 1), jnp.float32, math.log(4.0), math.log(40.0)))
    sign_flip = (2 * jax.random.randint(key_list[1], (LIB, 1), 0, 2) - 1).astype(jnp.float32)
    column = jnp.arange(SIGD, dtype=jnp.int32)[None, :]
    noise_part = jnp.clip(jax.random.normal(key_list[3], (LIB, SIGD), jnp.float32), -4.0, 4.0) * 0.05
    background = jnp.where(column == 0, jnp.minimum(magnitude, 40.0) * sign_flip, noise_part)
    near_ratio = jnp.exp(jax.random.uniform(key_list[4], (planted_count, 1), jnp.float32, math.log(0.02), math.log(0.25)))
    far_ratio = jnp.sqrt(near_ratio * near_ratio + jax.random.uniform(key_list[5], (planted_count, 1), jnp.float32, 1.0, 3.0) / 200.0)
    ratios = jnp.stack([near_ratio, far_ratio])
    directions = jax.random.normal(key_list[6], (2, planted_count, SIGD), jnp.float32)
    directions = directions - jnp.sum(directions * clip_units[None], axis=2, keepdims=True) * clip_units[None]
    directions = directions / jnp.sqrt(jnp.sum(directions * directions, axis=2, keepdims=True))
    amplitude = jnp.exp(jax.random.uniform(key_list[7], (2, planted_count, 1), jnp.float32, math.log(0.5), math.log(4.0)))
    copies = (amplitude * (clip_units[None] + ratios * directions)).reshape(2 * planted_count, SIGD)
    positions = jax.random.permutation(key_list[8], LIB)[:2 * planted_count]
    library_rows = background.at[positions].set(copies)
    return library_rows.astype(jnp.bfloat16)


def setup_inputs(seed: int = 0) -> dict:
    key_of = jax.random.split(jax.random.key(seed), 8)
    return {
        "raster": draw_raster(jax.random.fold_in(key_of[7], 71), 0),
        "transmission": draw_transmission(jax.random.fold_in(key_of[7], 71), 0),
        "kernels": draw_kernels(jax.random.fold_in(key_of[7], 71), 0),
        "kernel_weight": draw_kernel_weight(jax.random.fold_in(key_of[7], 71), 0),
        "library": draw_library(jax.random.fold_in(key_of[7], 71), 0),
        "clip_tile": draw_clip_tile(jax.random.fold_in(key_of[7], 71), 0),
        "clip_corner": draw_clip_corner(jax.random.fold_in(key_of[7], 71), 0),
    }


sharpness = 400.0

def dct_basis():
    freq_index = jnp.arange(KSIG, dtype=jnp.float32)[:, None]
    pixel_index = jnp.arange(CLIP, dtype=jnp.float32)[None, :]
    weights = jnp.where(freq_index == 0, jnp.sqrt(jnp.float32(1.0 / CLIP)), jnp.sqrt(jnp.float32(2.0 / CLIP)))
    return weights * jnp.cos(jnp.pi * (pixel_index + 0.5) * freq_index / CLIP)

def normalize(matrix):
    mean_square = lax.optimization_barrier(jnp.mean(matrix * matrix, axis=1, keepdims=True))
    return (matrix / (KSIG * jnp.sqrt(mean_square + 1e-06))).astype(jnp.bfloat16)

def reference(raster, transmission, kernels, kernel_weight, library, clip_tile, clip_corner):
    mask_values = raster.astype(jnp.float32) * transmission.astype(jnp.float32)
    half_width = KSIZE // 2
    padded = jnp.pad(mask_values, ((half_width, half_width), (half_width, half_width)))
    spectrum = jnp.fft.fft2(padded)
    aerial = jnp.zeros((NX, NY), jnp.float32)
    for kernel_index in range(KERNELS):
        conj_taps = kernels[kernel_index, 0] - 1j * kernels[kernel_index, 1]
        spread = jnp.zeros(padded.shape, spectrum.dtype)
        spread = spread.at[:KSIZE, :KSIZE].set(conj_taps.astype(spectrum.dtype))
        tile_field = jnp.fft.ifft2(spectrum * jnp.conj(jnp.fft.fft2(spread)))[:NX, :NY]
        aerial = aerial + kernel_weight[kernel_index] * (jnp.real(tile_field) ** 2 + jnp.imag(tile_field) ** 2)
    grid_row = clip_tile // GRID_COLS
    grid_col = clip_tile % GRID_COLS
    row_start = (grid_row * TILE + clip_corner[0]).astype(jnp.int32)
    col_start = (grid_col * TILE + clip_corner[1]).astype(jnp.int32)

    def window(row_first, col_first):
        return lax.dynamic_slice(aerial, (row_first, col_first), (CLIP, CLIP))
    windows = jax.vmap(window)(row_start, col_start)
    dct_rows = dct_basis()
    halfway = jnp.einsum('ku,cuv->ckv', dct_rows, windows, precision=lax.Precision.HIGHEST)
    signature = jnp.einsum('ckv,lv->ckl', halfway, dct_rows, precision=lax.Precision.HIGHEST).reshape(CLIPS, SIGD)
    signature = jnp.where(jnp.arange(SIGD)[None, :] == 0, 0.0, signature)
    clip_units = normalize(signature)
    blocks = library.reshape(TILES, LIB_DEV, SIGD)

    def absorb(running, lib_block):
        peak_old, total_old = running
        lib_units = normalize(lib_block.astype(jnp.float32))
        logits = sharpness * (jnp.dot(clip_units, lib_units.T, preferred_element_type=jnp.float32) - 1.0)
        peak_new = jnp.maximum(peak_old, lax.optimization_barrier(jnp.max(logits, axis=1)))
        total_new = total_old * jnp.exp(peak_old - peak_new) + lax.optimization_barrier(jnp.sum(jnp.exp(logits - peak_new[:, None]), axis=1))
        return ((peak_new, total_new), None)
    start_pair = (jnp.full((CLIPS,), -1e+30, jnp.float32), jnp.zeros((CLIPS,), jnp.float32))
    (peak_all, total_sum), unused = lax.scan(absorb, start_pair, blocks)
    scores = -(peak_all + jnp.log(total_sum)) / sharpness
    return (aerial, scores)
```

```python
import math

import jax
import jax.numpy as jnp
from jax import lax
from jax.sharding import PartitionSpec as P

KSIZE = 64
CLIP = 64
KSIG = 16
CAP = 16


sharpness = 400.0
highest = lax.Precision.HIGHEST


def extended_2(block, sides, width):
    for axis, dim in sides:
        count = lax.axis_size(axis)
        forward = [(i, i + 1) for i in range(count - 1)]
        backward = [(target, source) for source, target in forward]
        low = lax.ppermute(
            lax.slice_in_dim(block, block.shape[dim] - width, None, axis=dim), axis, forward
        )
        high = lax.ppermute(lax.slice_in_dim(block, 0, width, axis=dim), axis, backward)
        block = jnp.concatenate([low, block, high], axis=dim)
    return block


def normalize(matrix):
    mean_square = jnp.mean(matrix * matrix, axis=1, keepdims=True)
    return (matrix / (KSIG * jnp.sqrt(mean_square + 1e-06))).astype(jnp.bfloat16)


def pair_product(formula, left_pair, right_pair):

    def single(left_operand, right_operand):
        return jnp.einsum(formula, left_operand, right_operand, precision=highest)

    real_part = single(left_pair[0], right_pair[0]) - single(left_pair[1], right_pair[1])
    imag_part = single(left_pair[0], right_pair[1]) + single(left_pair[1], right_pair[0])
    return (real_part, imag_part)


def shifted_basis(corner_rows, tile_size):
    freq_index = jnp.arange(KSIG, dtype=jnp.float32)[None, :, None]
    offset = jnp.arange(tile_size, dtype=jnp.int32)[None, None, :] - corner_rows[:, None, None]
    inside = (offset >= 0) & (offset < CLIP)
    weights = jnp.where(
        freq_index == 0, jnp.sqrt(jnp.float32(1.0 / CLIP)), jnp.sqrt(jnp.float32(2.0 / CLIP))
    )
    values = weights * jnp.cos(jnp.pi * (offset.astype(jnp.float32) + 0.5) * freq_index / CLIP)
    return jnp.where(inside, values, 0.0)


def library_parts(clip_units, lib_units):
    block_rows = min(512, lib_units.shape[0])
    blocks = lib_units.reshape(-1, block_rows, lib_units.shape[1])

    def absorb(running, lib_block):
        peak_old, total_old = running
        logits = sharpness * (
            jnp.einsum("cd,jd->cj", clip_units, lib_block, preferred_element_type=jnp.float32) - 1.0
        )
        peak_new = jnp.maximum(peak_old, jnp.max(logits, axis=1))
        total_new = total_old * jnp.exp(peak_old - peak_new) + jnp.sum(
            jnp.exp(logits - peak_new[:, None]), axis=1
        )
        return ((peak_new, total_new), None)

    rows_count = clip_units.shape[0]
    start_pair = (
        jnp.full((rows_count,), -1e30, jnp.float32),
        jnp.zeros((rows_count,), jnp.float32),
    )
    (peak_all, total_sum), unused = lax.scan(absorb, start_pair, blocks)
    return (peak_all, total_sum)


def per_device(raster, transmission, kernels, kernel_weight, library, clip_tile, clip_corner):
    tile_size = raster.shape[0]
    half_width = KSIZE // 2
    mask_values = raster.astype(jnp.bfloat16) * transmission
    extended = extended_2(mask_values, (("wide", 1), ("narrow", 0)), half_width).astype(jnp.float32)
    full_size = tile_size + 2 * half_width
    grid_index = jnp.arange(full_size, dtype=jnp.float32)
    phase_angle = (
        2.0 * math.pi / full_size * jnp.mod(grid_index[:, None] * grid_index[None, :], full_size)
    )
    fourier = (jnp.cos(phase_angle), -jnp.sin(phase_angle))
    inverse = (jnp.cos(phase_angle), jnp.sin(phase_angle))
    left_pair = (
        jnp.dot(fourier[0], extended, precision=highest),
        jnp.dot(fourier[1], extended, precision=highest),
    )
    spectrum = pair_product("ab,bc->ac", left_pair, fourier)
    kernel_taps = (kernels[:, 0], kernels[:, 1])
    narrow_cols = (inverse[0][:, :KSIZE], inverse[1][:, :KSIZE])
    sectioned = pair_product("ai,kij->kaj", narrow_cols, kernel_taps)
    transfer = pair_product("kaj,bj->kab", sectioned, narrow_cols)
    filtered = (
        spectrum[0][None] * transfer[0] - spectrum[1][None] * transfer[1],
        spectrum[0][None] * transfer[1] + spectrum[1][None] * transfer[0],
    )
    tile_rows = (inverse[0][:tile_size], inverse[1][:tile_size])
    partial_field = pair_product("xa,kab->kxb", tile_rows, filtered)
    tile_field = pair_product("kxb,yb->kxy", partial_field, tile_rows)
    inverse_scale = 1.0 / (full_size * full_size)
    energy = (tile_field[0] * inverse_scale) ** 2 + (tile_field[1] * inverse_scale) ** 2
    aerial = jnp.einsum("k,kxy->xy", kernel_weight, energy, precision=highest)
    cols_wide = lax.axis_size("wide")
    rows_narrow = lax.axis_size("narrow")
    own_tile = lax.axis_index("narrow") * cols_wide + lax.axis_index("wide")
    owned_clips = clip_tile == own_tile
    slot_rank = jnp.cumsum(owned_clips.astype(jnp.int32)) - 1
    slot_ids = jnp.arange(CAP, dtype=jnp.int32)
    select = (owned_clips[None, :] & (slot_rank[None, :] == slot_ids[:, None])).astype(jnp.int32)
    corner_rows = jnp.sum(select * clip_corner[0][None, :], axis=1)
    corner_cols = jnp.sum(select * clip_corner[1][None, :], axis=1)
    row_basis = shifted_basis(corner_rows, tile_size)
    col_basis = shifted_basis(corner_cols, tile_size)
    halfway = jnp.einsum("skx,xy->sky", row_basis, aerial, precision=highest)
    signature = jnp.einsum("sky,sly->skl", halfway, col_basis, precision=highest).reshape(
        CAP, KSIG * KSIG
    )
    signature = jnp.where(jnp.arange(KSIG * KSIG)[None, :] == 0, 0.0, signature)
    slot_units = normalize(signature)
    lib_units = normalize(library.astype(jnp.float32))
    clip_count = clip_tile.shape[0]
    earlier = jnp.arange(clip_count)[None, :] < jnp.arange(clip_count)[:, None]
    same_tile = clip_tile[None, :] == clip_tile[:, None]
    rank_all = jnp.sum((earlier & same_tile).astype(jnp.int32), axis=1)
    holder = clip_tile % cols_wide * rows_narrow + clip_tile // cols_wide
    position = holder * CAP + rank_all
    both = ("wide", "narrow")
    device_count = cols_wide * rows_narrow
    copies = jnp.broadcast_to(slot_units[None], (device_count,) + slot_units.shape)
    gathered = lax.all_to_all(copies, both, 0, 0, tiled=True).reshape(-1, KSIG * KSIG)
    peak_all, total_sum = library_parts(gathered[position], lib_units)
    slab_log = (peak_all + jnp.log(total_sum)).reshape(device_count, -1)
    slab_log = lax.all_to_all(slab_log, both, 0, 0, tiled=True)
    peak_own = jnp.max(slab_log, axis=0)
    total_own = jnp.sum(jnp.exp(slab_log - peak_own[None, :]), axis=0)
    scores = -(peak_own + jnp.log(total_own)) / sharpness
    return (aerial, scores)


def solution(mesh):
    placed = (
        P("narrow", "wide"),
        P("narrow", "wide"),
        P(),
        P(),
        P(("wide", "narrow"), None),
        P(),
        P(),
    )
    return jax.shard_map(
        per_device,
        mesh=mesh,
        in_specs=placed,
        out_specs=(P("narrow", "wide"), P(("wide", "narrow"))),
        check_vma=False,
    )
```

```python
import math

import jax
import jax.numpy as jnp
import numpy as np
from jax import lax
from jax.experimental import pallas as pl
from jax.experimental.pallas import tpu as pltpu
from jax.sharding import PartitionSpec as P

KSIZE = 64
CLIP = 64
KSIG = 16
CAP = 16
SIGD = KSIG * KSIG
LANES = 128

sharpness = 400.0
f32 = jnp.float32
bf16 = jnp.bfloat16
VMEM_SPEC = pl.BlockSpec(memory_space=pltpu.VMEM)


def ceil_to(value, step):
    return -(-value // step) * step


def halves(table):
    high = table.astype(bf16)
    return high, (table - high.astype(np.float64)).astype(bf16)


def tables(tile):
    full = tile + KSIZE
    half = full // 2
    wide = ceil_to(full, 2 * LANES)
    unit = 2.0 * math.pi / full
    place = np.arange(full)
    place = np.where(place < tile + KSIZE // 2, place, place - full)
    taps = np.arange(KSIZE) - KSIZE // 2
    odd = np.arange(half) + 0.5
    freq = np.arange(full)

    def padded(table, rows, cols):
        out = np.zeros((rows, cols))
        out[: table.shape[0], : table.shape[1]] = table
        return out

    def side_by_side(angle, rows, cols):
        return np.concatenate(
            [padded(np.cos(angle), rows, cols), padded(np.sin(angle), rows, cols)], axis=1
        )

    angle = unit * odd[:, None] * place[None, :]
    rows_in = padded(np.concatenate([np.cos(angle), -np.sin(angle)]), full, wide)
    cols_in = side_by_side(unit * place[:, None] * freq[None, :], wide, wide)
    cols_out = side_by_side(unit * freq[:, None] * np.arange(tile)[None, :], wide, tile)
    angle = unit * np.arange(tile)[:, None] * odd[None, :]
    rows_out = padded(np.concatenate([np.cos(angle), -np.sin(angle)], axis=1), tile, wide)
    angle = unit * odd[:, None] * taps[None, :]
    taps_rows = np.concatenate([np.cos(angle), np.sin(angle)]) * (2.0 / (full * full))
    taps_cols = side_by_side(unit * taps[:, None] * freq[None, :], KSIZE, wide)
    high, low = halves(taps_rows)
    taps_rows = np.concatenate([high, low, high, low], axis=1)
    high, low = halves(taps_cols)
    taps_cols = np.concatenate([high, high, low, low], axis=0)
    return {
        "rows_in": halves(rows_in),
        "cols_in": halves(cols_in),
        "cols_out": halves(cols_out),
        "rows_out": halves(rows_out),
        "taps_rows": taps_rows,
        "taps_cols": taps_cols,
    }


def dot(left, right):
    return jnp.dot(left, right, preferred_element_type=f32)


def split(value):
    high = value.astype(bf16)
    return high, (value - high.astype(f32)).astype(bf16)


def dot3(left, right):
    return dot(left[0], right[0]) + dot(left[1], right[0]) + dot(left[0], right[1])


def dot3_t(left, right):
    def single(a, b):
        return lax.dot_general(a, b, (((1,), (1,)), ((), ())), preferred_element_type=f32)

    return single(left[0], right[0]) + single(left[1], right[0]) + single(left[0], right[1])


def iota(shape, dim):
    return lax.broadcasted_iota(jnp.int32, shape, dim)


def shifted_basis(corner, tile):
    shape = (CAP * KSIG, tile)
    freq = iota(shape, 0) & (KSIG - 1)
    offset = iota(shape, 1) - corner
    turn = ((2 * offset + 1) * freq) & (4 * CLIP - 1)
    fold = jnp.abs(turn.astype(f32) * (1.0 / (2 * CLIP)) - 1.0) - 0.5
    x = fold * math.pi
    square = x * x
    series = jnp.full(shape, -1.0 / math.factorial(15), f32)
    for order in (13, 11, 9, 7, 5, 3, 1):
        sign = 1.0 if order % 4 == 1 else -1.0
        series = series * square + sign / math.factorial(order)
    weight = jnp.where(freq == 0, math.sqrt(1.0 / CLIP), math.sqrt(2.0 / CLIP))
    inside = (offset >= 0) & (offset < CLIP)
    return jnp.where(inside, weight * (series * x), 0.0)


def filters_body(
    cols_wide, taps_ref, rows_ref, cols_ref, tile_ref, corner_ref, out_ref, rb_ref, cb_ref
):
    real_count = out_ref.shape[0]
    half = out_ref.shape[2]
    wide = out_ref.shape[3]

    def one(index, carry):
        taps = taps_ref[index]
        spread = jnp.concatenate([taps, taps, taps, taps], axis=1)
        high, low = split(spread)
        stacked = jnp.concatenate([high, high, low, low], axis=0)
        rows = dot(rows_ref[...], stacked)
        kept = rows.astype(bf16).astype(f32)
        is_low = (iota(rows.shape, 1) & KSIZE) != 0
        mixed = jnp.where(is_low, rows - kept, rows).astype(bf16)
        both = dot(mixed, cols_ref[...])
        out_ref[index, 0] = both[:half, :wide] - both[half:, wide:]
        out_ref[index, 1] = both[:half, wide:] + both[half:, :wide]
        return carry

    lax.fori_loop(0, real_count, one, 0, unroll=2)

    clip_count = tile_ref.shape[1]
    own_tile = lax.axis_index("narrow") * cols_wide + lax.axis_index("wide")
    owned = tile_ref[...] == own_tile
    owned8 = jnp.broadcast_to(owned.astype(f32), (8, clip_count))
    square = (clip_count, clip_count)
    earlier = (iota(square, 0) < iota(square, 1)).astype(f32).astype(bf16)
    rank = dot(owned8.astype(bf16), earlier)[:1]
    rank = jnp.where(owned, rank, -1.0)
    slot = (iota((CAP * KSIG, clip_count), 0) // KSIG).astype(f32)
    select = (slot == rank).astype(f32).astype(bf16)
    tile = rb_ref.shape[2]
    for axis, basis_ref in ((0, rb_ref), (1, cb_ref)):
        line = corner_ref[axis : axis + 1, :].astype(f32).astype(bf16)
        table = jnp.broadcast_to(line, (tile, clip_count))
        corner = lax.dot_general(
            select, table, (((1,), (1,)), ((), ())), preferred_element_type=f32
        )
        high, low = split(shifted_basis(corner.astype(jnp.int32), tile))
        basis_ref[0] = high
        basis_ref[1] = low


def image_body(
    raster_ref,
    light_ref,
    side_ref,
    after_ref,
    before_ref,
    weight_ref,
    filter_ref,
    rb_ref,
    cb_ref,
    rows_in_ref,
    cols_in_ref,
    cols_out_ref,
    rows_out_ref,
    aerial_ref,
    units_ref,
    mask_ref,
    spec_ref,
    prod_ref,
    mid_ref,
):
    tile = raster_ref.shape[0]
    half = filter_ref.shape[2]
    full = 2 * half
    wide = filter_ref.shape[3]
    border = KSIZE // 2
    mask_ref[:tile, :tile] = (raster_ref[...].astype(f32) * light_ref[...].astype(f32)).astype(bf16)
    mask_ref[:tile, tile:] = side_ref[...]
    mask_ref[tile : tile + border, :] = after_ref[...]
    mask_ref[tile + border : full, :] = before_ref[...]
    mask_ref[full:, :] = jnp.zeros((wide - full, wide), bf16)
    mask = mask_ref[...]
    rows = dot(rows_in_ref[0], mask) + dot(rows_in_ref[1], mask)
    both = dot3(split(rows), (cols_in_ref[0], cols_in_ref[1]))
    spec_ref[0] = both[:half, :wide] + both[half:, wide:]
    spec_ref[1] = both[half:, :wide] - both[:half, wide:]
    aerial_ref[...] = jnp.zeros_like(aerial_ref)
    mid_ref[:, full:, :] = jnp.zeros((2, wide - full, wide), bf16)

    def one(index, carry):
        for part in range(2):
            real = filter_ref[2 * index + part, 0]
            imag = filter_ref[2 * index + part, 1]
            base = part * full
            high, low = split(spec_ref[0] * real - spec_ref[1] * imag)
            prod_ref[0, base : base + half] = high
            prod_ref[1, base : base + half] = low
            high, low = split(spec_ref[0] * imag + spec_ref[1] * real)
            prod_ref[0, base + half : base + full] = high
            prod_ref[1, base + half : base + full] = low
        cols = dot3((prod_ref[0], prod_ref[1]), (cols_out_ref[0], cols_out_ref[1]))
        for part in range(2):
            base = part * full
            lane = part * tile
            real = cols[base : base + half]
            imag = cols[base + half : base + full]
            high, low = split(real[:, :tile] - imag[:, tile:])
            mid_ref[0, :half, lane : lane + tile] = high
            mid_ref[1, :half, lane : lane + tile] = low
            high, low = split(imag[:, :tile] + real[:, tile:])
            mid_ref[0, half:full, lane : lane + tile] = high
            mid_ref[1, half:full, lane : lane + tile] = low
        field = dot3((rows_out_ref[0], rows_out_ref[1]), (mid_ref[0], mid_ref[1]))
        energy = field * field
        aerial_ref[...] += weight_ref[index] * (energy[:, :tile] + energy[:, tile:])
        return carry

    lax.fori_loop(0, filter_ref.shape[0] // 2, one, 0, unroll=2)

    halfway = dot3((rb_ref[0], rb_ref[1]), split(aerial_ref[...]))
    crossed = dot3_t(split(halfway), (cb_ref[0], cb_ref[1]))
    shape = (CAP * KSIG, CAP * KSIG)
    crossed = jnp.where(iota(shape, 0) // KSIG == iota(shape, 1) // KSIG, crossed, 0.0)
    fold = ((iota(shape, 0) & (KSIG - 1)) == (iota(shape, 1) & (KSIG - 1))).astype(f32).astype(bf16)
    high, low = split(crossed)
    spread = dot(high, fold) + dot(low, fold)
    spread = jnp.where((iota(shape, 0) & (KSIG - 1)) == iota(shape, 1) // KSIG, spread, 0.0)
    signature = jnp.sum(spread.reshape(CAP, KSIG, SIGD), axis=1)
    signature = jnp.where(iota(signature.shape, 1) == 0, 0.0, signature)
    mean_square = jnp.mean(signature * signature, axis=1, keepdims=True)
    units = (signature / (KSIG * jnp.sqrt(mean_square + 1e-06))).astype(bf16)
    units_ref[...] = jnp.broadcast_to(units[None], units_ref.shape)


def library_body(library_ref, out_ref):
    rows = library_ref[...].astype(f32)
    mean_square = jnp.mean(rows * rows, axis=1, keepdims=True)
    out_ref[...] = (rows * (1.0 / (KSIG * jnp.sqrt(mean_square + 1e-06)))).astype(bf16)


def match_body(cols_wide, rows_narrow, tile_ref, gathered_ref, library_ref, out_ref):
    clip_count = tile_ref.shape[1]
    slot_count = gathered_ref.shape[0]
    device_count = out_ref.shape[0]
    own_count = clip_count // device_count
    row = tile_ref[...].astype(f32)
    peaks = []
    for first in range(0, clip_count, LANES):
        shape = (LANES, clip_count)
        clip = iota(shape, 0) + first
        other = iota(shape, 1)
        spread = jnp.broadcast_to(row, shape)
        column = jnp.sum(jnp.where(clip == other, spread, 0.0), axis=1, keepdims=True)
        before = (spread == column) & (other < clip)
        rank = jnp.sum(before.astype(f32), axis=1, keepdims=True)
        grid_row = jnp.floor((column + 0.5) * (1.0 / cols_wide))
        holder = (column - grid_row * cols_wide) * rows_narrow + grid_row
        place = (holder * CAP + rank).astype(jnp.int32)
        pick = (iota((LANES, slot_count), 1) == place).astype(f32).astype(bf16)
        units = dot(pick, gathered_ref[...]).astype(bf16)
        cosine = lax.dot_general(
            library_ref[...], units, (((1,), (1,)), ((), ())), preferred_element_type=f32
        )
        logits = sharpness * (cosine - 1.0)
        peak = jnp.max(logits, axis=0, keepdims=True)
        total = jnp.sum(jnp.exp(logits - peak), axis=0, keepdims=True)
        peaks.append(peak + jnp.log(total))
    slab = peaks[0] if len(peaks) == 1 else jnp.concatenate(peaks, axis=1)
    shape = (device_count, clip_count)
    spread = jnp.broadcast_to(slab, shape)
    lane = iota((device_count, LANES), 1)
    sent = jnp.zeros((device_count, LANES), f32)
    for index in range(own_count):
        mine = iota(shape, 1) == iota(shape, 0) * own_count + index
        value = jnp.sum(jnp.where(mine, spread, 0.0), axis=1, keepdims=True)
        sent = jnp.where(lane == index, value, sent)
    out_ref[...] = sent


def call(body, out_shape, operands, scratch=(), limit=24, smem=(), flops=0, name=None):
    specs = [
        pl.BlockSpec(memory_space=pltpu.SMEM) if index in smem else VMEM_SPEC
        for index in range(len(operands))
    ]
    return pl.pallas_call(
        body,
        out_shape=out_shape,
        in_specs=specs,
        out_specs=jax.tree.map(lambda _: VMEM_SPEC, out_shape),
        scratch_shapes=list(scratch),
        compiler_params=pltpu.CompilerParams(vmem_limit_bytes=limit << 20),
        cost_estimate=pl.CostEstimate(flops=flops, bytes_accessed=1 << 20, transcendentals=0),
        name=name,
    )(*operands)


def exchanged(low_edge, high_edge, axis):
    count = lax.axis_size(axis)
    forward = [(i, i + 1) for i in range(count - 1)]
    backward = [(target, source) for source, target in forward]
    return lax.ppermute(high_edge, axis, forward), lax.ppermute(low_edge, axis, backward)


def per_device(raster, transmission, kernels, kernel_weight, library, clip_tile, clip_corner):
    tile = raster.shape[0]
    border = KSIZE // 2
    full = tile + KSIZE
    half = full // 2
    wide = ceil_to(full, 2 * LANES)
    table = {
        key: jnp.stack([jnp.asarray(part) for part in value])
        if isinstance(value, tuple)
        else jnp.asarray(value)
        for key, value in tables(tile).items()
    }
    cols_wide = lax.axis_size("wide")
    rows_narrow = lax.axis_size("narrow")
    device_count = cols_wide * rows_narrow
    both = ("wide", "narrow")
    clip_count = clip_tile.shape[0]
    kernel_count = kernels.shape[0]

    def masked(rows, cols):
        return raster[rows, cols].astype(bf16) * transmission[rows, cols]

    every = slice(None)
    left, right = exchanged(
        masked(every, slice(0, border)), masked(every, slice(tile - border, tile)), "wide"
    )
    side = jnp.concatenate([right, left, jnp.zeros((tile, wide - full), bf16)], axis=1)
    top = slice(0, border)
    bottom = slice(tile - border, tile)
    before, after = exchanged(
        jnp.concatenate([masked(top, every), side[top]], axis=1),
        jnp.concatenate([masked(bottom, every), side[bottom]], axis=1),
        "narrow",
    )

    tile_line = clip_tile.reshape(1, clip_count)
    basis = jax.ShapeDtypeStruct((2, CAP * KSIG, tile), bf16)
    filters, row_basis, col_basis = call(
        lambda *refs: filters_body(cols_wide, *refs),
        (
            jax.ShapeDtypeStruct((2 * kernel_count, 2, half, wide), f32),
            basis,
            basis,
        ),
        (
            kernels.reshape(2 * kernel_count, KSIZE, KSIZE),
            table["taps_rows"],
            table["taps_cols"],
            tile_line,
            clip_corner,
        ),
        flops=3 << 30,
        name="filters",
    )
    aerial, copies = call(
        image_body,
        (
            jax.ShapeDtypeStruct((tile, tile), f32),
            jax.ShapeDtypeStruct((device_count, CAP, SIGD), bf16),
        ),
        (
            raster,
            transmission,
            side,
            after,
            before,
            kernel_weight,
            filters,
            row_basis,
            col_basis,
            table["rows_in"],
            table["cols_in"],
            table["cols_out"],
            table["rows_out"],
        ),
        scratch=(
            pltpu.VMEM((wide, wide), bf16),
            pltpu.VMEM((2, half, wide), f32),
            pltpu.VMEM((2, 2 * full, wide), bf16),
            pltpu.VMEM((2, wide, wide), bf16),
        ),
        smem=(5,),
        flops=6 << 30,
        name="image",
    )
    lib_units = call(
        library_body,
        jax.ShapeDtypeStruct(library.shape, bf16),
        (library,),
        flops=1 << 30,
        name="library",
    )
    gathered = lax.all_to_all(copies, both, 0, 0, tiled=True).reshape(device_count * CAP, SIGD)
    slab = call(
        lambda *refs: match_body(cols_wide, rows_narrow, *refs),
        jax.ShapeDtypeStruct((device_count, LANES), f32),
        (tile_line, gathered, lib_units),
        limit=40,
        flops=1 << 30,
        name="match",
    )
    slab = lax.all_to_all(slab, both, 0, 0, tiled=True)[:, : clip_count // device_count]
    peak = jnp.max(slab, axis=0)
    total = jnp.sum(jnp.exp(slab - peak[None, :]), axis=0)
    scores = -(peak + jnp.log(total)) / sharpness
    return (aerial, scores)


def solution(mesh):
    placed = (
        P("narrow", "wide"),
        P("narrow", "wide"),
        P(),
        P(),
        P(("wide", "narrow"), None),
        P(),
        P(),
    )
    return jax.shard_map(
        per_device,
        mesh=mesh,
        in_specs=placed,
        out_specs=(P("narrow", "wide"), P(("wide", "narrow"))),
        check_vma=False,
    )
```

```python
import math

import jax
import jax.numpy as jnp
import numpy as np
from jax import lax
from jax.experimental import pallas as pl
from jax.experimental.pallas import tpu as pltpu
from jax.sharding import PartitionSpec as P

KSIZE = 64
CLIP = 64
KSIG = 16
CAP = 16
SIGD = KSIG * KSIG
LANES = 128

sharpness = 400.0
f32 = jnp.float32
bf16 = jnp.bfloat16
VMEM_SPEC = pl.BlockSpec(memory_space=pltpu.VMEM)


def ceil_to(value, step):
    return -(-value // step) * step


def halves(table):
    high = table.astype(bf16)
    return high, (table - high.astype(np.float64)).astype(bf16)


def tables(tile):
    full = tile + KSIZE
    half = full // 2
    wide = ceil_to(full, 2 * LANES)
    unit = 2.0 * math.pi / full
    place = np.arange(full)
    place = np.where(place < tile + KSIZE // 2, place, place - full)
    taps = np.arange(KSIZE) - KSIZE // 2
    odd = np.arange(half) + 0.5
    freq = np.arange(full)

    def padded(table, rows, cols):
        out = np.zeros((rows, cols))
        out[: table.shape[0], : table.shape[1]] = table
        return out

    def side_by_side(angle, rows, cols):
        return np.concatenate(
            [padded(np.cos(angle), rows, cols), padded(np.sin(angle), rows, cols)], axis=1
        )

    angle = unit * odd[:, None] * place[None, :]
    rows_in = padded(np.concatenate([np.cos(angle), -np.sin(angle)]), full, wide)
    cols_in = side_by_side(unit * place[:, None] * freq[None, :], wide, wide)
    cols_out = side_by_side(unit * freq[:, None] * np.arange(tile)[None, :], wide, tile)
    angle = unit * np.arange(tile)[:, None] * odd[None, :]
    rows_out = padded(np.concatenate([np.cos(angle), -np.sin(angle)], axis=1), tile, wide)
    angle = unit * odd[:, None] * taps[None, :]
    taps_rows = np.concatenate([np.cos(angle), np.sin(angle)]) * (2.0 / (full * full))
    taps_cols = side_by_side(unit * taps[:, None] * freq[None, :], KSIZE, wide)
    high, low = halves(taps_rows)
    taps_rows = np.concatenate([high, low, high, low], axis=1)
    high, low = halves(taps_cols)
    taps_cols = np.concatenate([high, high, low, low], axis=0)
    return {
        "rows_in": halves(rows_in),
        "cols_in": halves(cols_in),
        "cols_out": halves(cols_out),
        "rows_out": halves(rows_out),
        "taps_rows": taps_rows,
        "taps_cols": taps_cols,
    }


def dot(left, right):
    return jnp.dot(left, right, preferred_element_type=f32)


def split(value):
    high = value.astype(bf16)
    return high, (value - high.astype(f32)).astype(bf16)


def dot3(left, right):
    return dot(left[0], right[0]) + dot(left[1], right[0]) + dot(left[0], right[1])


def dot3_t(left, right):
    def single(a, b):
        return lax.dot_general(a, b, (((1,), (1,)), ((), ())), preferred_element_type=f32)

    return single(left[0], right[0]) + single(left[1], right[0]) + single(left[0], right[1])


def iota(shape, dim):
    return lax.broadcasted_iota(jnp.int32, shape, dim)


def shifted_basis(corner, tile):
    shape = (CAP * KSIG, tile)
    freq = iota(shape, 0) & (KSIG - 1)
    offset = iota(shape, 1) - corner
    turn = ((2 * offset + 1) * freq) & (4 * CLIP - 1)
    fold = jnp.abs(turn.astype(f32) * (1.0 / (2 * CLIP)) - 1.0) - 0.5
    x = fold * math.pi
    square = x * x
    series = jnp.full(shape, -1.0 / math.factorial(15), f32)
    for order in (13, 11, 9, 7, 5, 3, 1):
        sign = 1.0 if order % 4 == 1 else -1.0
        series = series * square + sign / math.factorial(order)
    weight = jnp.where(freq == 0, math.sqrt(1.0 / CLIP), math.sqrt(2.0 / CLIP))
    inside = (offset >= 0) & (offset < CLIP)
    return jnp.where(inside, weight * (series * x), 0.0)


def edges_body(raster_hbm, light_hbm, mask_ref, low_ref, high_ref, raster_ref, light_ref, sems):
    tile = mask_ref.shape[0]
    border = low_ref.shape[1]
    copies = [
        pltpu.make_async_copy(raster_hbm, raster_ref, sems.at[0]),
        pltpu.make_async_copy(light_hbm, light_ref, sems.at[1]),
    ]
    for copy in copies:
        copy.start()
    for copy in copies:
        copy.wait()
    mask = (raster_ref[...].astype(f32) * light_ref[...].astype(f32)).astype(bf16)
    mask_ref[...] = mask
    low_ref[...] = mask[:, :border]
    high_ref[...] = mask[:, tile - border :]


def transform_taps(first, count, taps_ref, rows_ref, cols_ref, out_ref, mixed_ref):
    half = out_ref.shape[2]
    wide = out_ref.shape[3]

    def along_rows(index):
        taps = taps_ref[first + index]
        spread = jnp.concatenate([taps, taps, taps, taps], axis=1)
        high, low = split(spread)
        stacked = jnp.concatenate([high, high, low, low], axis=0)
        rows = dot(rows_ref[...], stacked)
        kept = rows.astype(bf16).astype(f32)
        is_low = (iota(rows.shape, 1) & KSIZE) != 0
        mixed_ref[index % 2] = jnp.where(is_low, rows - kept, rows).astype(bf16)

    def along_cols(index):
        both = dot(mixed_ref[index % 2], cols_ref[...])
        out_ref[index, 0] = both[:half, :wide] - both[half:, wide:]
        out_ref[index, 1] = both[:half, wide:] + both[half:, :wide]

    along_rows(0)
    for index in range(count):
        if index + 1 < count:
            along_rows(index + 1)
        along_cols(index)


def first_body(taps_hbm, rows_hbm, cols_hbm, out_ref, taps_ref, rows_ref, cols_ref, mixed_ref, sems):
    copies = [
        pltpu.make_async_copy(source, target, sems.at[index])
        for index, (source, target) in enumerate(
            ((taps_hbm, taps_ref), (rows_hbm, rows_ref), (cols_hbm, cols_ref))
        )
    ]
    for copy in copies:
        copy.start()
    for copy in copies:
        copy.wait()
    transform_taps(0, out_ref.shape[0], taps_ref, rows_ref, cols_ref, out_ref, mixed_ref)


def second_body(
    first,
    cols_wide,
    taps_ref,
    rows_ref,
    cols_ref,
    tile_hbm,
    corner_hbm,
    out_ref,
    rb_ref,
    cb_ref,
    mixed_ref,
    tile_ref,
    corner_ref,
    sems,
):
    copies = [
        pltpu.make_async_copy(tile_hbm, tile_ref, sems.at[0]),
        pltpu.make_async_copy(corner_hbm, corner_ref, sems.at[1]),
    ]
    for copy in copies:
        copy.start()
    transform_taps(first, out_ref.shape[0], taps_ref, rows_ref, cols_ref, out_ref, mixed_ref)
    for copy in copies:
        copy.wait()
    clip_count = tile_ref.shape[1]
    own_tile = lax.axis_index("narrow") * cols_wide + lax.axis_index("wide")
    owned = tile_ref[...] == own_tile
    owned8 = jnp.broadcast_to(owned.astype(f32), (8, clip_count))
    square = (clip_count, clip_count)
    earlier = (iota(square, 0) < iota(square, 1)).astype(f32).astype(bf16)
    rank = dot(owned8.astype(bf16), earlier)[:1]
    rank = jnp.where(owned, rank, -1.0)
    slot = (iota((CAP * KSIG, clip_count), 0) // KSIG).astype(f32)
    select = (slot == rank).astype(f32).astype(bf16)
    tile = rb_ref.shape[2]
    for axis, basis_ref in ((0, rb_ref), (1, cb_ref)):
        line = corner_ref[axis : axis + 1, :].astype(f32).astype(bf16)
        table = jnp.broadcast_to(line, (tile, clip_count))
        corner = lax.dot_general(
            select, table, (((1,), (1,)), ((), ())), preferred_element_type=f32
        )
        high, low = split(shifted_basis(corner.astype(jnp.int32), tile))
        basis_ref[0] = high
        basis_ref[1] = low


def image_body(
    own_ref,
    side_ref,
    after_ref,
    before_ref,
    weight_ref,
    early_ref,
    late_ref,
    rb_ref,
    cb_ref,
    rows_in_ref,
    cols_in_ref,
    cols_out_ref,
    rows_out_ref,
    aerial_ref,
    units_ref,
    mask_ref,
    spec_ref,
    prod_ref,
    mid_ref,
    sum_ref,
):
    tile = own_ref.shape[0]
    half = early_ref.shape[2]
    full = 2 * half
    wide = early_ref.shape[3]
    border = KSIZE // 2
    early = early_ref.shape[0]
    kernel_count = (early + late_ref.shape[0]) // 2
    mask_ref[:tile, :tile] = own_ref[...]
    mask_ref[:tile, tile:] = side_ref[...]
    mask_ref[tile : tile + border, :] = after_ref[...]
    mask_ref[tile + border : full, :] = before_ref[...]
    mask_ref[full:, :] = jnp.zeros((wide - full, wide), bf16)
    for index in range(2):
        mid_ref[index, :, full:, :] = jnp.zeros((2, wide - full, wide), bf16)
    mask = mask_ref[...]
    rows = dot(rows_in_ref[0], mask) + dot(rows_in_ref[1], mask)
    both = dot3(split(rows), (cols_in_ref[0], cols_in_ref[1]))
    spec_ref[0] = both[:half, :wide] + both[half:, wide:]
    spec_ref[1] = both[half:, :wide] - both[:half, wide:]

    def multiply(index):
        place = prod_ref.at[index % 2]
        for part in range(2):
            number = 2 * index + part
            ref = early_ref.at[number] if number < early else late_ref.at[number - early]
            base = part * full
            high, low = split(spec_ref[0] * ref[0] - spec_ref[1] * ref[1])
            place[0, base : base + half] = high
            place[1, base : base + half] = low
            high, low = split(spec_ref[0] * ref[1] + spec_ref[1] * ref[0])
            place[0, base + half : base + full] = high
            place[1, base + half : base + full] = low

    def along_cols(index):
        place = mid_ref.at[index % 2]
        source = prod_ref.at[index % 2]
        cols = dot3((source[0], source[1]), (cols_out_ref[0], cols_out_ref[1]))
        for part in range(2):
            base = part * full
            lane = part * tile
            real = cols[base : base + half]
            imag = cols[base + half : base + full]
            high, low = split(real[:, :tile] - imag[:, tile:])
            place[0, :half, lane : lane + tile] = high
            place[1, :half, lane : lane + tile] = low
            high, low = split(imag[:, :tile] + real[:, tile:])
            place[0, half:full, lane : lane + tile] = high
            place[1, half:full, lane : lane + tile] = low

    def along_rows(index):
        source = mid_ref.at[index % 2]
        field = dot3((rows_out_ref[0], rows_out_ref[1]), (source[0], source[1]))
        energy = field * field
        value = weight_ref[index] * (energy[:, :tile] + energy[:, tile:])
        if index == 0:
            sum_ref[...] = value
        elif index == kernel_count - 1:
            aerial_ref[...] = sum_ref[...] + value
        else:
            sum_ref[...] += value

    for step in range(kernel_count + 2):
        if step < kernel_count:
            multiply(step)
        if 0 <= step - 1 < kernel_count:
            along_cols(step - 1)
        if 0 <= step - 2:
            along_rows(step - 2)

    halfway = dot3((rb_ref[0], rb_ref[1]), split(aerial_ref[...]))
    crossed = dot3_t(split(halfway), (cb_ref[0], cb_ref[1]))
    shape = (CAP * KSIG, CAP * KSIG)
    crossed = jnp.where(iota(shape, 0) // KSIG == iota(shape, 1) // KSIG, crossed, 0.0)
    fold = ((iota(shape, 0) & (KSIG - 1)) == (iota(shape, 1) & (KSIG - 1))).astype(f32).astype(bf16)
    high, low = split(crossed)
    spread = dot(high, fold) + dot(low, fold)
    spread = jnp.where((iota(shape, 0) & (KSIG - 1)) == iota(shape, 1) // KSIG, spread, 0.0)
    signature = jnp.sum(spread.reshape(CAP, KSIG, SIGD), axis=1)
    signature = jnp.where(iota(signature.shape, 1) == 0, 0.0, signature)
    mean_square = jnp.mean(signature * signature, axis=1, keepdims=True)
    units = (signature / (KSIG * jnp.sqrt(mean_square + 1e-06))).astype(bf16)
    units_ref[...] = jnp.broadcast_to(units[None], units_ref.shape)


def library_body(library_ref, out_ref):
    rows = library_ref[...].astype(f32)
    mean_square = jnp.mean(rows * rows, axis=1, keepdims=True)
    out_ref[...] = (rows * (1.0 / (KSIG * jnp.sqrt(mean_square + 1e-06)))).astype(bf16)


def match_body(cols_wide, rows_narrow, tile_ref, gathered_ref, library_ref, out_ref):
    clip_count = tile_ref.shape[1]
    slot_count = gathered_ref.shape[0]
    device_count = out_ref.shape[0]
    own_count = clip_count // device_count
    row = tile_ref[...].astype(f32)
    peaks = []
    for first in range(0, clip_count, LANES):
        shape = (LANES, clip_count)
        clip = iota(shape, 0) + first
        other = iota(shape, 1)
        spread = jnp.broadcast_to(row, shape)
        column = jnp.sum(jnp.where(clip == other, spread, 0.0), axis=1, keepdims=True)
        before = (spread == column) & (other < clip)
        rank = jnp.sum(before.astype(f32), axis=1, keepdims=True)
        grid_row = jnp.floor((column + 0.5) * (1.0 / cols_wide))
        holder = (column - grid_row * cols_wide) * rows_narrow + grid_row
        place = (holder * CAP + rank).astype(jnp.int32)
        pick = (iota((LANES, slot_count), 1) == place).astype(f32).astype(bf16)
        units = dot(pick, gathered_ref[...]).astype(bf16)
        cosine = lax.dot_general(
            library_ref[...], units, (((1,), (1,)), ((), ())), preferred_element_type=f32
        )
        logits = sharpness * (cosine - 1.0)
        peak = jnp.max(logits, axis=0, keepdims=True)
        total = jnp.sum(jnp.exp(logits - peak), axis=0, keepdims=True)
        peaks.append(peak + jnp.log(total))
    slab = peaks[0] if len(peaks) == 1 else jnp.concatenate(peaks, axis=1)
    shape = (device_count, clip_count)
    spread = jnp.broadcast_to(slab, shape)
    lane = iota((device_count, LANES), 1)
    sent = jnp.zeros((device_count, LANES), f32)
    for index in range(own_count):
        mine = iota(shape, 1) == iota(shape, 0) * own_count + index
        value = jnp.sum(jnp.where(mine, spread, 0.0), axis=1, keepdims=True)
        sent = jnp.where(lane == index, value, sent)
    out_ref[...] = sent


def call(
    body, out_shape, operands, scratch=(), limit=24, smem=(), hbm=(), flops=0, name=None
):
    spaces = [
        pltpu.SMEM if index in smem else pltpu.HBM if index in hbm else pltpu.VMEM
        for index in range(len(operands))
    ]
    return pl.pallas_call(
        body,
        out_shape=out_shape,
        in_specs=[pl.BlockSpec(memory_space=space) for space in spaces],
        out_specs=jax.tree.map(lambda _: VMEM_SPEC, out_shape),
        scratch_shapes=list(scratch),
        compiler_params=pltpu.CompilerParams(vmem_limit_bytes=limit << 20),
        cost_estimate=pl.CostEstimate(flops=flops, bytes_accessed=1 << 20, transcendentals=0),
        name=name,
    )(*operands)


def exchanged(low_edge, high_edge, axis):
    count = lax.axis_size(axis)
    forward = [(i, i + 1) for i in range(count - 1)]
    backward = [(target, source) for source, target in forward]
    return lax.ppermute(high_edge, axis, forward), lax.ppermute(low_edge, axis, backward)


def per_device(raster, transmission, kernels, kernel_weight, library, clip_tile, clip_corner):
    tile = raster.shape[0]
    border = KSIZE // 2
    full = tile + KSIZE
    half = full // 2
    wide = ceil_to(full, 2 * LANES)
    table = {
        key: jnp.stack([jnp.asarray(part) for part in value])
        if isinstance(value, tuple)
        else jnp.asarray(value)
        for key, value in tables(tile).items()
    }
    cols_wide = lax.axis_size("wide")
    rows_narrow = lax.axis_size("narrow")
    device_count = cols_wide * rows_narrow
    both = ("wide", "narrow")
    clip_count = clip_tile.shape[0]
    real_count = 2 * kernels.shape[0]

    mask, low_edge, high_edge = call(
        edges_body,
        (
            jax.ShapeDtypeStruct((tile, tile), bf16),
            jax.ShapeDtypeStruct((tile, border), bf16),
            jax.ShapeDtypeStruct((tile, border), bf16),
        ),
        (raster, transmission),
        scratch=(
            pltpu.VMEM((tile, tile), jnp.int32),
            pltpu.VMEM((tile, tile), bf16),
            pltpu.SemaphoreType.DMA((2,)),
        ),
        hbm=(0, 1),
        limit=8,
        name="edges",
    )
    left, right = exchanged(low_edge, high_edge, "wide")

    early = real_count // 2
    spectrum = (2, half, wide)
    mixed = pltpu.VMEM((2, full, 4 * KSIZE), bf16)
    early_filters, taps, taps_rows, taps_cols = call(
        first_body,
        (
            jax.ShapeDtypeStruct((early,) + spectrum, f32),
            jax.ShapeDtypeStruct((real_count, KSIZE, KSIZE), f32),
            jax.ShapeDtypeStruct(table["taps_rows"].shape, bf16),
            jax.ShapeDtypeStruct(table["taps_cols"].shape, bf16),
        ),
        (
            kernels.reshape(real_count, KSIZE, KSIZE),
            table["taps_rows"],
            table["taps_cols"],
        ),
        scratch=(mixed, pltpu.SemaphoreType.DMA((3,))),
        hbm=(0, 1, 2),
        flops=2 << 30,
        name="first",
    )
    left, right, early_filters = lax.optimization_barrier((left, right, early_filters))

    side = jnp.concatenate([right, left, jnp.zeros((tile, wide - full), bf16)], axis=1)
    top = slice(0, border)
    bottom = slice(tile - border, tile)
    before, after = exchanged(
        jnp.concatenate([mask[top], side[top]], axis=1),
        jnp.concatenate([mask[bottom], side[bottom]], axis=1),
        "narrow",
    )

    tile_line = clip_tile.reshape(1, clip_count)
    basis = jax.ShapeDtypeStruct((2, CAP * KSIG, tile), bf16)
    late_filters, row_basis, col_basis = call(
        lambda *refs: second_body(early, cols_wide, *refs),
        (
            jax.ShapeDtypeStruct((real_count - early,) + spectrum, f32),
            basis,
            basis,
        ),
        (taps, taps_rows, taps_cols, tile_line, clip_corner),
        scratch=(
            mixed,
            pltpu.VMEM((1, clip_count), jnp.int32),
            pltpu.VMEM((2, clip_count), jnp.int32),
            pltpu.SemaphoreType.DMA((2,)),
        ),
        hbm=(3, 4),
        flops=2 << 30,
        name="second",
    )
    aerial, copies = call(
        image_body,
        (
            jax.ShapeDtypeStruct((tile, tile), f32),
            jax.ShapeDtypeStruct((device_count, CAP, SIGD), bf16),
        ),
        (
            mask,
            side,
            after,
            before,
            kernel_weight,
            early_filters,
            late_filters,
            row_basis,
            col_basis,
            table["rows_in"],
            table["cols_in"],
            table["cols_out"],
            table["rows_out"],
        ),
        scratch=(
            pltpu.VMEM((wide, wide), bf16),
            pltpu.VMEM(spectrum, f32),
            pltpu.VMEM((2, 2, 2 * full, wide), bf16),
            pltpu.VMEM((2, 2, wide, wide), bf16),
            pltpu.VMEM((tile, tile), f32),
        ),
        smem=(4,),
        flops=6 << 30,
        name="image",
    )
    lib_units = call(
        library_body,
        jax.ShapeDtypeStruct(library.shape, bf16),
        (library,),
        flops=1 << 30,
        name="library",
    )
    gathered = lax.all_to_all(copies, both, 0, 0, tiled=True).reshape(device_count * CAP, SIGD)
    slab = call(
        lambda *refs: match_body(cols_wide, rows_narrow, *refs),
        jax.ShapeDtypeStruct((device_count, LANES), f32),
        (tile_line, gathered, lib_units),
        limit=40,
        flops=1 << 30,
        name="match",
    )
    slab = lax.all_to_all(slab, both, 0, 0, tiled=True)[:, : clip_count // device_count]
    peak = jnp.max(slab, axis=0)
    total = jnp.sum(jnp.exp(slab - peak[None, :]), axis=0)
    scores = -(peak + jnp.log(total)) / sharpness
    return (aerial, scores)


def solution(mesh):
    placed = (
        P("narrow", "wide"),
        P("narrow", "wide"),
        P(),
        P(),
        P(("wide", "narrow"), None),
        P(),
        P(),
    )
    return jax.shard_map(
        per_device,
        mesh=mesh,
        in_specs=placed,
        out_specs=(P("narrow", "wide"), P(("wide", "narrow"))),
        check_vma=False,
    )
```

```python
import math

import jax
import jax.numpy as jnp
import numpy as np
from jax import lax
from jax.experimental import pallas as pl
from jax.experimental.pallas import tpu as pltpu
from jax.sharding import PartitionSpec as P

KSIZE = 64
CLIP = 64
KSIG = 16
CAP = 16
SIGD = KSIG * KSIG
LANES = 128
GROUP = 2

sharpness = 400.0
f32 = jnp.float32
bf16 = jnp.bfloat16
VMEM_SPEC = pl.BlockSpec(memory_space=pltpu.VMEM)


def ceil_to(value, step):
    return -(-value // step) * step


def halves(table):
    high = table.astype(bf16)
    return high, (table - high.astype(np.float64)).astype(bf16)


def tables(tile):
    full = tile + KSIZE
    half = full // 2
    wide = ceil_to(full, 2 * LANES)
    unit = 2.0 * math.pi / full
    place = np.arange(full)
    place = np.where(place < tile + KSIZE // 2, place, place - full)
    taps = np.arange(KSIZE) - KSIZE // 2
    odd = np.arange(half) + 0.5
    freq = np.arange(full)

    def padded(table, rows, cols):
        out = np.zeros((rows, cols))
        out[: table.shape[0], : table.shape[1]] = table
        return out

    def side_by_side(angle, rows, cols):
        return np.concatenate(
            [padded(np.cos(angle), rows, cols), padded(np.sin(angle), rows, cols)], axis=1
        )

    angle = unit * odd[:, None] * place[None, :]
    rows_in = padded(np.concatenate([np.cos(angle), -np.sin(angle)]), full, wide)
    cols_in = side_by_side(unit * place[:, None] * freq[None, :], wide, wide)
    cols_out = side_by_side(unit * freq[:, None] * np.arange(tile)[None, :], wide, tile)
    angle = unit * np.arange(tile)[:, None] * odd[None, :]
    rows_out = padded(np.concatenate([np.cos(angle), -np.sin(angle)], axis=1), tile, wide)
    angle = unit * odd[:, None] * taps[None, :]
    taps_rows = np.concatenate([np.cos(angle), np.sin(angle)]) * (2.0 / (full * full))
    taps_cols = side_by_side(unit * taps[:, None] * freq[None, :], KSIZE, wide)
    high, low = halves(taps_rows)
    taps_rows = np.concatenate([high, low, high, low], axis=1)
    high, low = halves(taps_cols)
    taps_cols = np.concatenate([high, high, low, low], axis=0)
    return {
        "rows_in": halves(rows_in),
        "cols_in": halves(cols_in),
        "cols_out": halves(cols_out),
        "rows_out": halves(rows_out),
        "taps_rows": taps_rows,
        "taps_cols": taps_cols,
    }


def dot(left, right):
    return jnp.dot(left, right, preferred_element_type=f32)


def split(value):
    high = value.astype(bf16)
    return high, (value - high.astype(f32)).astype(bf16)


def dot3(left, right):
    return dot(left[0], right[0]) + dot(left[1], right[0]) + dot(left[0], right[1])


def dot3_t(left, right):
    def single(a, b):
        return lax.dot_general(a, b, (((1,), (1,)), ((), ())), preferred_element_type=f32)

    return single(left[0], right[0]) + single(left[1], right[0]) + single(left[0], right[1])


def iota(shape, dim):
    return lax.broadcasted_iota(jnp.int32, shape, dim)


def shifted_basis(corner, tile):
    shape = (CAP * KSIG, tile)
    freq = iota(shape, 0) & (KSIG - 1)
    offset = iota(shape, 1) - corner
    turn = ((2 * offset + 1) * freq) & (4 * CLIP - 1)
    fold = jnp.abs(turn.astype(f32) * (1.0 / (2 * CLIP)) - 1.0) - 0.5
    x = fold * math.pi
    square = x * x
    series = jnp.full(shape, -1.0 / math.factorial(15), f32)
    for order in (13, 11, 9, 7, 5, 3, 1):
        sign = 1.0 if order % 4 == 1 else -1.0
        series = series * square + sign / math.factorial(order)
    weight = jnp.where(freq == 0, math.sqrt(1.0 / CLIP), math.sqrt(2.0 / CLIP))
    inside = (offset >= 0) & (offset < CLIP)
    return jnp.where(inside, weight * (series * x), 0.0)


def edges_body(raster_hbm, light_hbm, mask_ref, low_ref, high_ref, raster_ref, light_ref, sems):
    tile = mask_ref.shape[0]
    border = low_ref.shape[1]
    copies = [
        pltpu.make_async_copy(raster_hbm, raster_ref, sems.at[0]),
        pltpu.make_async_copy(light_hbm, light_ref, sems.at[1]),
    ]
    for copy in copies:
        copy.start()
    for copy in copies:
        copy.wait()
    mask = (raster_ref[...].astype(f32) * light_ref[...].astype(f32)).astype(bf16)
    mask_ref[...] = mask
    low_ref[...] = mask[:, :border]
    high_ref[...] = mask[:, tile - border :]


def transform_taps(first, count, taps_ref, rows_ref, cols_ref, out_ref, mixed_ref):
    half = out_ref.shape[2]
    wide = out_ref.shape[3]

    def along_rows(index):
        taps = taps_ref[first + index]
        spread = jnp.concatenate([taps, taps, taps, taps], axis=1)
        high, low = split(spread)
        stacked = jnp.concatenate([high, high, low, low], axis=0)
        rows = dot(rows_ref[...], stacked)
        kept = rows.astype(bf16).astype(f32)
        is_low = (iota(rows.shape, 1) & KSIZE) != 0
        mixed_ref[index % 2] = jnp.where(is_low, rows - kept, rows).astype(bf16)

    def along_cols(index):
        both = dot(mixed_ref[index % 2], cols_ref[...])
        out_ref[index, 0] = both[:half, :wide] - both[half:, wide:]
        out_ref[index, 1] = both[:half, wide:] + both[half:, :wide]

    along_rows(0)
    for index in range(count):
        if index + 1 < count:
            along_rows(index + 1)
        along_cols(index)


def first_body(taps_hbm, rows_hbm, cols_hbm, out_ref, taps_ref, rows_ref, cols_ref, mixed_ref, sems):
    copies = [
        pltpu.make_async_copy(source, target, sems.at[index])
        for index, (source, target) in enumerate(
            ((taps_hbm, taps_ref), (rows_hbm, rows_ref), (cols_hbm, cols_ref))
        )
    ]
    for copy in copies:
        copy.start()
    for copy in copies:
        copy.wait()
    transform_taps(0, out_ref.shape[0], taps_ref, rows_ref, cols_ref, out_ref, mixed_ref)


def second_body(
    first,
    cols_wide,
    taps_ref,
    rows_ref,
    cols_ref,
    tile_hbm,
    corner_hbm,
    out_ref,
    rb_ref,
    cb_ref,
    mixed_ref,
    tile_ref,
    corner_ref,
    sems,
):
    copies = [
        pltpu.make_async_copy(tile_hbm, tile_ref, sems.at[0]),
        pltpu.make_async_copy(corner_hbm, corner_ref, sems.at[1]),
    ]
    for copy in copies:
        copy.start()
    transform_taps(first, out_ref.shape[0], taps_ref, rows_ref, cols_ref, out_ref, mixed_ref)
    for copy in copies:
        copy.wait()
    clip_count = tile_ref.shape[1]
    own_tile = lax.axis_index("narrow") * cols_wide + lax.axis_index("wide")
    owned = tile_ref[...] == own_tile
    owned8 = jnp.broadcast_to(owned.astype(f32), (8, clip_count))
    square = (clip_count, clip_count)
    earlier = (iota(square, 0) < iota(square, 1)).astype(f32).astype(bf16)
    rank = dot(owned8.astype(bf16), earlier)[:1]
    rank = jnp.where(owned, rank, -1.0)
    slot = (iota((CAP * KSIG, clip_count), 0) // KSIG).astype(f32)
    select = (slot == rank).astype(f32).astype(bf16)
    tile = rb_ref.shape[2]
    for axis, basis_ref in ((0, rb_ref), (1, cb_ref)):
        line = corner_ref[axis : axis + 1, :].astype(f32).astype(bf16)
        table = jnp.broadcast_to(line, (tile, clip_count))
        corner = lax.dot_general(
            select, table, (((1,), (1,)), ((), ())), preferred_element_type=f32
        )
        high, low = split(shifted_basis(corner.astype(jnp.int32), tile))
        basis_ref[0] = high
        basis_ref[1] = low


def image_body(
    own_ref,
    side_ref,
    after_ref,
    before_ref,
    weight_ref,
    early_ref,
    late_ref,
    rb_ref,
    cb_ref,
    rows_in_ref,
    cols_in_ref,
    cols_out_ref,
    rows_out_ref,
    aerial_ref,
    units_ref,
    mask_ref,
    spec_ref,
    prod_ref,
    mid_ref,
    sum_ref,
):
    tile = own_ref.shape[0]
    half = early_ref.shape[2]
    full = 2 * half
    wide = early_ref.shape[3]
    border = KSIZE // 2
    early = early_ref.shape[0]
    kernel_count = (early + late_ref.shape[0]) // 2
    mask_ref[:tile, :tile] = own_ref[...]
    mask_ref[:tile, tile:] = side_ref[...]
    mask_ref[tile : tile + border, :] = after_ref[...]
    mask_ref[tile + border : full, :] = before_ref[...]
    mask_ref[full:, :] = jnp.zeros((wide - full, wide), bf16)
    for place in range(2):
        for member in range(mid_ref.shape[1]):
            mid_ref[place, member, :, full:, :] = jnp.zeros((2, wide - full, wide), bf16)
    mask = mask_ref[...]
    rows = dot(rows_in_ref[0], mask) + dot(rows_in_ref[1], mask)
    both = dot3(split(rows), (cols_in_ref[0], cols_in_ref[1]))
    spec_ref[0] = both[:half, :wide] + both[half:, wide:]
    spec_ref[1] = both[half:, :wide] - both[:half, wide:]

    group = prod_ref.shape[2] // (2 * full)

    def multiply(index):
        place = prod_ref.at[index % 2]
        for part in range(2 * group):
            number = 2 * group * index + part
            ref = early_ref.at[number] if number < early else late_ref.at[number - early]
            base = part * full
            high, low = split(spec_ref[0] * ref[0] - spec_ref[1] * ref[1])
            place[0, base : base + half] = high
            place[1, base : base + half] = low
            high, low = split(spec_ref[0] * ref[1] + spec_ref[1] * ref[0])
            place[0, base + half : base + full] = high
            place[1, base + half : base + full] = low

    def along_cols(index):
        source = prod_ref.at[index % 2]
        cols = dot3((source[0], source[1]), (cols_out_ref[0], cols_out_ref[1]))
        for part in range(2 * group):
            place = mid_ref.at[index % 2, part // 2]
            base = part * full
            lane = part % 2 * tile
            real = cols[base : base + half]
            imag = cols[base + half : base + full]
            high, low = split(real[:, :tile] - imag[:, tile:])
            place[0, :half, lane : lane + tile] = high
            place[1, :half, lane : lane + tile] = low
            high, low = split(imag[:, :tile] + real[:, tile:])
            place[0, half:full, lane : lane + tile] = high
            place[1, half:full, lane : lane + tile] = low

    def along_rows(index):
        value = None
        for member in range(group):
            source = mid_ref.at[index % 2, member]
            field = dot3((rows_out_ref[0], rows_out_ref[1]), (source[0], source[1]))
            energy = field * field
            term = weight_ref[group * index + member] * (energy[:, :tile] + energy[:, tile:])
            value = term if value is None else value + term
        if index == 0:
            sum_ref[...] = value
        elif index == kernel_count // group - 1:
            aerial_ref[...] = sum_ref[...] + value
        else:
            sum_ref[...] += value

    for step in range(kernel_count // group + 2):
        if step < kernel_count // group:
            multiply(step)
        if 0 <= step - 1 < kernel_count // group:
            along_cols(step - 1)
        if 0 <= step - 2:
            along_rows(step - 2)

    halfway = dot3((rb_ref[0], rb_ref[1]), split(aerial_ref[...]))
    crossed = dot3_t(split(halfway), (cb_ref[0], cb_ref[1]))
    shape = (CAP * KSIG, CAP * KSIG)
    crossed = jnp.where(iota(shape, 0) // KSIG == iota(shape, 1) // KSIG, crossed, 0.0)
    fold = ((iota(shape, 0) & (KSIG - 1)) == (iota(shape, 1) & (KSIG - 1))).astype(f32).astype(bf16)
    high, low = split(crossed)
    spread = dot(high, fold) + dot(low, fold)
    spread = jnp.where((iota(shape, 0) & (KSIG - 1)) == iota(shape, 1) // KSIG, spread, 0.0)
    signature = jnp.sum(spread.reshape(CAP, KSIG, SIGD), axis=1)
    signature = jnp.where(iota(signature.shape, 1) == 0, 0.0, signature)
    mean_square = jnp.mean(signature * signature, axis=1, keepdims=True)
    units = (signature / (KSIG * jnp.sqrt(mean_square + 1e-06))).astype(bf16)
    units_ref[...] = jnp.broadcast_to(units[None], units_ref.shape)


def library_body(library_ref, out_ref):
    rows = library_ref[...].astype(f32)
    mean_square = jnp.mean(rows * rows, axis=1, keepdims=True)
    out_ref[...] = (rows * (1.0 / (KSIG * jnp.sqrt(mean_square + 1e-06)))).astype(bf16)


def match_body(cols_wide, rows_narrow, tile_ref, gathered_ref, library_ref, out_ref):
    clip_count = tile_ref.shape[1]
    slot_count = gathered_ref.shape[0]
    device_count = out_ref.shape[0]
    own_count = clip_count // device_count
    row = tile_ref[...].astype(f32)
    peaks = []
    for first in range(0, clip_count, LANES):
        shape = (LANES, clip_count)
        clip = iota(shape, 0) + first
        other = iota(shape, 1)
        spread = jnp.broadcast_to(row, shape)
        column = jnp.sum(jnp.where(clip == other, spread, 0.0), axis=1, keepdims=True)
        before = (spread == column) & (other < clip)
        rank = jnp.sum(before.astype(f32), axis=1, keepdims=True)
        grid_row = jnp.floor((column + 0.5) * (1.0 / cols_wide))
        holder = (column - grid_row * cols_wide) * rows_narrow + grid_row
        place = (holder * CAP + rank).astype(jnp.int32)
        pick = (iota((LANES, slot_count), 1) == place).astype(f32).astype(bf16)
        units = dot(pick, gathered_ref[...]).astype(bf16)
        cosine = lax.dot_general(
            library_ref[...], units, (((1,), (1,)), ((), ())), preferred_element_type=f32
        )
        logits = sharpness * (cosine - 1.0)
        peak = jnp.max(logits, axis=0, keepdims=True)
        total = jnp.sum(jnp.exp(logits - peak), axis=0, keepdims=True)
        peaks.append(peak + jnp.log(total))
    slab = peaks[0] if len(peaks) == 1 else jnp.concatenate(peaks, axis=1)
    shape = (device_count, clip_count)
    spread = jnp.broadcast_to(slab, shape)
    lane = iota((device_count, LANES), 1)
    sent = jnp.zeros((device_count, LANES), f32)
    for index in range(own_count):
        mine = iota(shape, 1) == iota(shape, 0) * own_count + index
        value = jnp.sum(jnp.where(mine, spread, 0.0), axis=1, keepdims=True)
        sent = jnp.where(lane == index, value, sent)
    out_ref[...] = sent


def call(
    body, out_shape, operands, scratch=(), limit=24, smem=(), hbm=(), flops=0, name=None
):
    spaces = [
        pltpu.SMEM if index in smem else pltpu.HBM if index in hbm else pltpu.VMEM
        for index in range(len(operands))
    ]
    return pl.pallas_call(
        body,
        out_shape=out_shape,
        in_specs=[pl.BlockSpec(memory_space=space) for space in spaces],
        out_specs=jax.tree.map(lambda _: VMEM_SPEC, out_shape),
        scratch_shapes=list(scratch),
        compiler_params=pltpu.CompilerParams(vmem_limit_bytes=limit << 20),
        cost_estimate=pl.CostEstimate(flops=flops, bytes_accessed=1 << 20, transcendentals=0),
        name=name,
    )(
        *(
            pltpu.with_memory_space_constraint(value, pltpu.HBM) if index in hbm else value
            for index, value in enumerate(operands)
        )
    )


def exchanged(low_edge, high_edge, axis):
    count = lax.axis_size(axis)
    forward = [(i, i + 1) for i in range(count - 1)]
    backward = [(target, source) for source, target in forward]
    return lax.ppermute(high_edge, axis, forward), lax.ppermute(low_edge, axis, backward)


def per_device(raster, transmission, kernels, kernel_weight, library, clip_tile, clip_corner):
    tile = raster.shape[0]
    border = KSIZE // 2
    full = tile + KSIZE
    half = full // 2
    wide = ceil_to(full, 2 * LANES)
    table = {
        key: jnp.stack([jnp.asarray(part) for part in value])
        if isinstance(value, tuple)
        else jnp.asarray(value)
        for key, value in tables(tile).items()
    }
    cols_wide = lax.axis_size("wide")
    rows_narrow = lax.axis_size("narrow")
    device_count = cols_wide * rows_narrow
    both = ("wide", "narrow")
    clip_count = clip_tile.shape[0]
    real_count = 2 * kernels.shape[0]

    mask, low_edge, high_edge = call(
        edges_body,
        (
            jax.ShapeDtypeStruct((tile, tile), bf16),
            jax.ShapeDtypeStruct((tile, border), bf16),
            jax.ShapeDtypeStruct((tile, border), bf16),
        ),
        (raster, transmission),
        scratch=(
            pltpu.VMEM((tile, tile), jnp.int32),
            pltpu.VMEM((tile, tile), bf16),
            pltpu.SemaphoreType.DMA((2,)),
        ),
        hbm=(0, 1),
        limit=8,
        name="edges",
    )
    left, right = exchanged(low_edge, high_edge, "wide")

    early = real_count // 2
    spectrum = (2, half, wide)
    mixed = pltpu.VMEM((2, full, 4 * KSIZE), bf16)
    early_filters, taps, taps_rows, taps_cols = call(
        first_body,
        (
            jax.ShapeDtypeStruct((early,) + spectrum, f32),
            jax.ShapeDtypeStruct((real_count, KSIZE, KSIZE), f32),
            jax.ShapeDtypeStruct(table["taps_rows"].shape, bf16),
            jax.ShapeDtypeStruct(table["taps_cols"].shape, bf16),
        ),
        (
            kernels.reshape(real_count, KSIZE, KSIZE),
            table["taps_rows"],
            table["taps_cols"],
        ),
        scratch=(mixed, pltpu.SemaphoreType.DMA((3,))),
        hbm=(0, 1, 2),
        flops=2 << 30,
        name="first",
    )
    left, right, early_filters = lax.optimization_barrier((left, right, early_filters))

    side = jnp.concatenate([right, left, jnp.zeros((tile, wide - full), bf16)], axis=1)
    top = slice(0, border)
    bottom = slice(tile - border, tile)
    before, after = exchanged(
        jnp.concatenate([mask[top], side[top]], axis=1),
        jnp.concatenate([mask[bottom], side[bottom]], axis=1),
        "narrow",
    )

    tile_line = clip_tile.reshape(1, clip_count)
    basis = jax.ShapeDtypeStruct((2, CAP * KSIG, tile), bf16)
    late_filters, row_basis, col_basis = call(
        lambda *refs: second_body(early, cols_wide, *refs),
        (
            jax.ShapeDtypeStruct((real_count - early,) + spectrum, f32),
            basis,
            basis,
        ),
        (taps, taps_rows, taps_cols, tile_line, clip_corner),
        scratch=(
            mixed,
            pltpu.VMEM((1, clip_count), jnp.int32),
            pltpu.VMEM((2, clip_count), jnp.int32),
            pltpu.SemaphoreType.DMA((2,)),
        ),
        hbm=(3, 4),
        flops=2 << 30,
        name="second",
    )
    aerial, copies = call(
        image_body,
        (
            jax.ShapeDtypeStruct((tile, tile), f32),
            jax.ShapeDtypeStruct((device_count, CAP, SIGD), bf16),
        ),
        (
            mask,
            side,
            after,
            before,
            kernel_weight,
            early_filters,
            late_filters,
            row_basis,
            col_basis,
            table["rows_in"],
            table["cols_in"],
            table["cols_out"],
            table["rows_out"],
        ),
        scratch=(
            pltpu.VMEM((wide, wide), bf16),
            pltpu.VMEM(spectrum, f32),
            pltpu.VMEM((2, 2, GROUP * 2 * full, wide), bf16),
            pltpu.VMEM((2, GROUP, 2, wide, wide), bf16),
            pltpu.VMEM((tile, tile), f32),
        ),
        smem=(4,),
        flops=6 << 30,
        name="image",
    )
    lib_units = call(
        library_body,
        jax.ShapeDtypeStruct(library.shape, bf16),
        (library,),
        flops=1 << 30,
        name="library",
    )
    gathered = lax.all_to_all(copies, both, 0, 0, tiled=True).reshape(device_count * CAP, SIGD)
    slab = call(
        lambda *refs: match_body(cols_wide, rows_narrow, *refs),
        jax.ShapeDtypeStruct((device_count, LANES), f32),
        (tile_line, gathered, lib_units),
        limit=40,
        flops=1 << 30,
        name="match",
    )
    slab = lax.all_to_all(slab, both, 0, 0, tiled=True)[:, : clip_count // device_count]
    peak = jnp.max(slab, axis=0)
    total = jnp.sum(jnp.exp(slab - peak[None, :]), axis=0)
    scores = -(peak + jnp.log(total)) / sharpness
    return (aerial, scores)


def solution(mesh):
    placed = (
        P("narrow", "wide"),
        P("narrow", "wide"),
        P(),
        P(),
        P(("wide", "narrow"), None),
        P(),
        P(),
    )
    return jax.shard_map(
        per_device,
        mesh=mesh,
        in_specs=placed,
        out_specs=(P("narrow", "wide"), P(("wide", "narrow"))),
        check_vma=False,
    )
```

```python
import math

import jax
import jax.numpy as jnp
import numpy as np
from jax import lax
from jax.experimental import pallas as pl
from jax.experimental.pallas import tpu as pltpu
from jax.sharding import PartitionSpec as P

KSIZE = 64
CLIP = 64
KSIG = 16
CAP = 16
SIGD = KSIG * KSIG
LANES = 128
GROUP = 2

sharpness = 400.0
f32 = jnp.float32
bf16 = jnp.bfloat16
VMEM_SPEC = pl.BlockSpec(memory_space=pltpu.VMEM)


def ceil_to(value, step):
    return -(-value // step) * step


def halves(table):
    high = table.astype(bf16)
    return high, (table - high.astype(np.float64)).astype(bf16)


def tables(tile):
    full = tile + KSIZE
    half = full // 2
    wide = ceil_to(full, 2 * LANES)
    unit = 2.0 * math.pi / full
    place = np.arange(full)
    place = np.where(place < tile + KSIZE // 2, place, place - full)
    taps = np.arange(KSIZE) - KSIZE // 2
    odd = np.arange(half) + 0.5
    freq = np.arange(full)

    def padded(table, rows, cols):
        out = np.zeros((rows, cols))
        out[: table.shape[0], : table.shape[1]] = table
        return out

    def side_by_side(angle, rows, cols):
        return np.concatenate(
            [padded(np.cos(angle), rows, cols), padded(np.sin(angle), rows, cols)], axis=1
        )

    angle = unit * odd[:, None] * place[None, :]
    rows_in = padded(np.concatenate([np.cos(angle), -np.sin(angle)]), full, wide)
    cols_in = side_by_side(unit * place[:, None] * freq[None, :], wide, wide)
    cols_out = side_by_side(unit * freq[:, None] * np.arange(tile)[None, :], wide, tile)
    angle = unit * np.arange(tile)[:, None] * odd[None, :]
    rows_out = padded(np.concatenate([np.cos(angle), -np.sin(angle)], axis=1), tile, wide)
    angle = unit * odd[:, None] * taps[None, :]
    taps_rows = np.concatenate([np.cos(angle), np.sin(angle)]) * (2.0 / (full * full))
    taps_cols = side_by_side(unit * taps[:, None] * freq[None, :], KSIZE, wide)
    high, low = halves(taps_rows)
    taps_rows = np.concatenate([high, low, high, low], axis=1)
    high, low = halves(taps_cols)
    taps_cols = np.concatenate([high, high, low, low], axis=0)
    return {
        "rows_in": halves(rows_in),
        "cols_in": halves(cols_in),
        "cols_out": halves(cols_out),
        "rows_out": halves(rows_out),
        "taps_rows": taps_rows,
        "taps_cols": taps_cols,
    }


def dot(left, right):
    return jnp.dot(left, right, preferred_element_type=f32)


def split(value):
    high = value.astype(bf16)
    return high, (value - high.astype(f32)).astype(bf16)


def dot3(left, right):
    return dot(left[0], right[0]) + dot(left[1], right[0]) + dot(left[0], right[1])


def dot3_t(left, right):
    def single(a, b):
        return lax.dot_general(a, b, (((1,), (1,)), ((), ())), preferred_element_type=f32)

    return single(left[0], right[0]) + single(left[1], right[0]) + single(left[0], right[1])


def iota(shape, dim):
    return lax.broadcasted_iota(jnp.int32, shape, dim)


def shifted_basis(corner, tile):
    shape = (CAP * KSIG, tile)
    freq = iota(shape, 0) & (KSIG - 1)
    offset = iota(shape, 1) - corner
    turn = ((2 * offset + 1) * freq) & (4 * CLIP - 1)
    fold = jnp.abs(turn.astype(f32) * (1.0 / (2 * CLIP)) - 1.0) - 0.5
    x = fold * math.pi
    square = x * x
    series = jnp.full(shape, -1.0 / math.factorial(15), f32)
    for order in (13, 11, 9, 7, 5, 3, 1):
        sign = 1.0 if order % 4 == 1 else -1.0
        series = series * square + sign / math.factorial(order)
    weight = jnp.where(freq == 0, math.sqrt(1.0 / CLIP), math.sqrt(2.0 / CLIP))
    inside = (offset >= 0) & (offset < CLIP)
    return jnp.where(inside, weight * (series * x), 0.0)


def neighbours():
    return [(dw, dz) for dw in (-1, 0, 1) for dz in (-1, 0, 1) if dw or dz]


def fetched(pairs, sems):
    copies = [
        pltpu.make_async_copy(source, target, sems.at[index])
        for index, (source, target) in enumerate(pairs)
    ]
    for copy in copies:
        copy.start()
    return copies


def edges_body(cols_wide, rows_narrow, raster_hbm, light_hbm, mask_ref, sent_ref, raster_ref, light_ref, sems):
    tile = mask_ref.shape[0]
    border = sent_ref.shape[1]
    copies = fetched(((raster_hbm, raster_ref), (light_hbm, light_ref)), sems)
    sent_ref[...] = jnp.zeros_like(sent_ref)
    for copy in copies:
        copy.wait()
    mask = raster_ref[...].astype(f32) * light_ref[...].astype(f32)
    mask_ref[...] = mask.astype(bf16)
    lane = iota((border, tile), 1)

    def folded(first):
        out = jnp.zeros((border, tile), f32)
        for block in range(tile // border):
            low = block * border
            moved = pltpu.roll(mask[low : low + border], (low - first) % tile, 1)
            out = jnp.where((lane >= low) & (lane < low + border), moved, out)
        return out.astype(bf16)

    top = mask[:border].astype(bf16)
    bottom = mask[tile - border :].astype(bf16)
    low_cols = folded(0)
    high_cols = folded(tile - border)
    col = lax.axis_index("wide")
    row = lax.axis_index("narrow")
    for dw, dz in neighbours():
        strip = top if dz < 0 else bottom if dz > 0 else low_cols if dw < 0 else high_cols
        there = (col + dw >= 0) & (col + dw < cols_wide)
        there &= (row + dz >= 0) & (row + dz < rows_narrow)

        @pl.when(there)
        def _():
            sent_ref[(col + dw) * rows_narrow + row + dz] = strip


def transform_taps(taps_ref, rows_ref, cols_ref, out_ref, mixed_ref, finished):
    count = out_ref.shape[0]
    half = out_ref.shape[2]
    wide = out_ref.shape[3]

    def along_rows(index):
        taps = taps_ref[index]
        spread = jnp.concatenate([taps, taps, taps, taps], axis=1)
        high, low = split(spread)
        stacked = jnp.concatenate([high, high, low, low], axis=0)
        rows = dot(rows_ref[...], stacked)
        kept = rows.astype(bf16).astype(f32)
        is_low = (iota(rows.shape, 1) & KSIZE) != 0
        mixed_ref[index % 2] = jnp.where(is_low, rows - kept, rows).astype(bf16)

    def along_cols(index):
        both = dot(mixed_ref[index % 2], cols_ref[...])
        out_ref[index, 0] = both[:half, :wide] - both[half:, wide:]
        out_ref[index, 1] = both[:half, wide:] + both[half:, :wide]
        finished[index].start()

    along_rows(0)
    for index in range(count):
        if index + 1 < count:
            along_rows(index + 1)
        along_cols(index)


def filters_body(
    cols_wide,
    taps_hbm,
    rows_hbm,
    cols_hbm,
    tile_hbm,
    corner_hbm,
    out_hbm,
    rb_ref,
    cb_ref,
    out_ref,
    mixed_ref,
    taps_ref,
    rows_ref,
    cols_ref,
    tile_ref,
    corner_ref,
    sems,
    out_sems,
):
    pairs = (
        (taps_hbm, taps_ref),
        (rows_hbm, rows_ref),
        (cols_hbm, cols_ref),
        (tile_hbm, tile_ref),
        (corner_hbm, corner_ref),
    )
    for copy in fetched(pairs, sems):
        copy.wait()
    finished = [
        pltpu.make_async_copy(out_ref.at[index], out_hbm.at[index], out_sems.at[index])
        for index in range(out_ref.shape[0])
    ]
    transform_taps(taps_ref, rows_ref, cols_ref, out_ref, mixed_ref, finished)
    clip_count = tile_ref.shape[1]
    own_tile = lax.axis_index("narrow") * cols_wide + lax.axis_index("wide")
    owned = tile_ref[...] == own_tile
    owned8 = jnp.broadcast_to(owned.astype(f32), (8, clip_count))
    square = (clip_count, clip_count)
    earlier = (iota(square, 0) < iota(square, 1)).astype(f32).astype(bf16)
    rank = dot(owned8.astype(bf16), earlier)[:1]
    rank = jnp.where(owned, rank, -1.0)
    slot = (iota((CAP * KSIG, clip_count), 0) // KSIG).astype(f32)
    select = (slot == rank).astype(f32).astype(bf16)
    tile = rb_ref.shape[2]
    for axis, basis_ref in ((0, rb_ref), (1, cb_ref)):
        line = corner_ref[axis : axis + 1, :].astype(f32).astype(bf16)
        table = jnp.broadcast_to(line, (tile, clip_count))
        corner = lax.dot_general(
            select, table, (((1,), (1,)), ((), ())), preferred_element_type=f32
        )
        high, low = split(shifted_basis(corner.astype(jnp.int32), tile))
        basis_ref[0] = high
        basis_ref[1] = low
    for copy in finished:
        copy.wait()


def image_body(
    cols_wide,
    rows_narrow,
    own_ref,
    got_ref,
    weight_ref,
    filter_hbm,
    rb_ref,
    cb_ref,
    rows_in_ref,
    cols_in_ref,
    cols_out_ref,
    rows_out_ref,
    aerial_ref,
    units_ref,
    mask_ref,
    spec_ref,
    prod_ref,
    mid_ref,
    sum_ref,
    filter_ref,
    sems,
):
    tile = own_ref.shape[0]
    half = filter_ref.shape[2]
    full = 2 * half
    wide = filter_ref.shape[3]
    border = KSIZE // 2
    kernel_count = filter_ref.shape[0] // 2
    group = prod_ref.shape[2] // (2 * full)
    parts = [
        (filter_hbm.at[pl.ds(first, 2 * group)], filter_ref.at[pl.ds(first, 2 * group)])
        for first in range(0, 2 * kernel_count, 2 * group)
    ]
    arriving = fetched(parts, sems)
    col = lax.axis_index("wide")
    row = lax.axis_index("narrow")
    lane = iota((border, tile), 1)

    def from_neighbour(dw, dz):
        there = (col + dw >= 0) & (col + dw < cols_wide)
        there &= (row + dz >= 0) & (row + dz < rows_narrow)
        place = jnp.where(there, (col + dw) * rows_narrow + row + dz, 0)
        return jnp.where(there, got_ref[place].astype(f32), 0.0)

    def beside(right, right_shift, left, left_shift):
        right = pltpu.roll(right, right_shift % tile, 1)
        left = pltpu.roll(left, left_shift % tile, 1)
        return jnp.where(lane < border, right, jnp.where(lane < 2 * border, left, 0.0)).astype(bf16)

    mask_ref[:tile, :tile] = own_ref[...]
    right = from_neighbour(1, 0)
    left = from_neighbour(-1, 0)
    for low in range(0, tile, border):
        mask_ref[low : low + border, tile:] = beside(right, -low, left, border - low)
    for low, dz in ((tile, 1), (tile + border, -1)):
        mask_ref[low : low + border, :tile] = from_neighbour(0, dz).astype(bf16)
        mask_ref[low : low + border, tile:] = beside(
            from_neighbour(1, dz), 0, from_neighbour(-1, dz), 2 * border
        )
    mask_ref[full:, :] = jnp.zeros((wide - full, wide), bf16)
    for place in range(2):
        for member in range(mid_ref.shape[1]):
            mid_ref[place, member, :, full:, :] = jnp.zeros((2, wide - full, wide), bf16)
    mask = mask_ref[...]
    rows = dot(rows_in_ref[0], mask) + dot(rows_in_ref[1], mask)
    both = dot3(split(rows), (cols_in_ref[0], cols_in_ref[1]))
    spec_ref[0] = both[:half, :wide] + both[half:, wide:]
    spec_ref[1] = both[half:, :wide] - both[:half, wide:]

    def multiply(index):
        arriving[index].wait()
        place = prod_ref.at[index % 2]
        for part in range(2 * group):
            number = 2 * group * index + part
            ref = filter_ref.at[number]
            base = part * full
            high, low = split(spec_ref[0] * ref[0] - spec_ref[1] * ref[1])
            place[0, base : base + half] = high
            place[1, base : base + half] = low
            high, low = split(spec_ref[0] * ref[1] + spec_ref[1] * ref[0])
            place[0, base + half : base + full] = high
            place[1, base + half : base + full] = low

    def along_cols(index):
        source = prod_ref.at[index % 2]
        cols = dot3((source[0], source[1]), (cols_out_ref[0], cols_out_ref[1]))
        for part in range(2 * group):
            place = mid_ref.at[index % 2, part // 2]
            base = part * full
            lane = part % 2 * tile
            real = cols[base : base + half]
            imag = cols[base + half : base + full]
            high, low = split(real[:, :tile] - imag[:, tile:])
            place[0, :half, lane : lane + tile] = high
            place[1, :half, lane : lane + tile] = low
            high, low = split(imag[:, :tile] + real[:, tile:])
            place[0, half:full, lane : lane + tile] = high
            place[1, half:full, lane : lane + tile] = low

    def along_rows(index):
        value = None
        for member in range(group):
            source = mid_ref.at[index % 2, member]
            field = dot3((rows_out_ref[0], rows_out_ref[1]), (source[0], source[1]))
            energy = field * field
            term = weight_ref[group * index + member] * (energy[:, :tile] + energy[:, tile:])
            value = term if value is None else value + term
        if index == 0:
            sum_ref[...] = value
        elif index == kernel_count // group - 1:
            aerial_ref[...] = sum_ref[...] + value
        else:
            sum_ref[...] += value

    for step in range(kernel_count // group + 2):
        if step < kernel_count // group:
            multiply(step)
        if 0 <= step - 1 < kernel_count // group:
            along_cols(step - 1)
        if 0 <= step - 2:
            along_rows(step - 2)

    halfway = dot3((rb_ref[0], rb_ref[1]), split(aerial_ref[...]))
    crossed = dot3_t(split(halfway), (cb_ref[0], cb_ref[1]))
    shape = (CAP * KSIG, CAP * KSIG)
    crossed = jnp.where(iota(shape, 0) // KSIG == iota(shape, 1) // KSIG, crossed, 0.0)
    fold = ((iota(shape, 0) & (KSIG - 1)) == (iota(shape, 1) & (KSIG - 1))).astype(f32).astype(bf16)
    high, low = split(crossed)
    spread = dot(high, fold) + dot(low, fold)
    spread = jnp.where((iota(shape, 0) & (KSIG - 1)) == iota(shape, 1) // KSIG, spread, 0.0)
    signature = jnp.sum(spread.reshape(CAP, KSIG, SIGD), axis=1)
    signature = jnp.where(iota(signature.shape, 1) == 0, 0.0, signature)
    mean_square = jnp.mean(signature * signature, axis=1, keepdims=True)
    units = (signature / (KSIG * jnp.sqrt(mean_square + 1e-06))).astype(bf16)
    units_ref[...] = jnp.broadcast_to(units[None], units_ref.shape)


def library_body(library_ref, out_ref):
    rows = library_ref[...].astype(f32)
    mean_square = jnp.mean(rows * rows, axis=1, keepdims=True)
    out_ref[...] = (rows * (1.0 / (KSIG * jnp.sqrt(mean_square + 1e-06)))).astype(bf16)


def match_body(cols_wide, rows_narrow, tile_ref, gathered_ref, library_ref, out_ref):
    clip_count = tile_ref.shape[1]
    slot_count = gathered_ref.shape[0]
    device_count = out_ref.shape[0]
    own_count = clip_count // device_count
    row = tile_ref[...].astype(f32)
    peaks = []
    for first in range(0, clip_count, LANES):
        shape = (LANES, clip_count)
        clip = iota(shape, 0) + first
        other = iota(shape, 1)
        spread = jnp.broadcast_to(row, shape)
        column = jnp.sum(jnp.where(clip == other, spread, 0.0), axis=1, keepdims=True)
        before = (spread == column) & (other < clip)
        rank = jnp.sum(before.astype(f32), axis=1, keepdims=True)
        grid_row = jnp.floor((column + 0.5) * (1.0 / cols_wide))
        holder = (column - grid_row * cols_wide) * rows_narrow + grid_row
        place = (holder * CAP + rank).astype(jnp.int32)
        pick = (iota((LANES, slot_count), 1) == place).astype(f32).astype(bf16)
        units = dot(pick, gathered_ref[...]).astype(bf16)
        cosine = lax.dot_general(
            library_ref[...], units, (((1,), (1,)), ((), ())), preferred_element_type=f32
        )
        logits = sharpness * (cosine - 1.0)
        peak = jnp.max(logits, axis=0, keepdims=True)
        total = jnp.sum(jnp.exp(logits - peak), axis=0, keepdims=True)
        peaks.append(peak + jnp.log(total))
    slab = peaks[0] if len(peaks) == 1 else jnp.concatenate(peaks, axis=1)
    shape = (device_count, clip_count)
    spread = jnp.broadcast_to(slab, shape)
    lane = iota((device_count, LANES), 1)
    sent = jnp.zeros((device_count, LANES), f32)
    for index in range(own_count):
        mine = iota(shape, 1) == iota(shape, 0) * own_count + index
        value = jnp.sum(jnp.where(mine, spread, 0.0), axis=1, keepdims=True)
        sent = jnp.where(lane == index, value, sent)
    out_ref[...] = sent


def call(
    body, out_shape, operands, scratch=(), limit=24, smem=(), hbm=(), out=None, flops=0, name=None
):
    spaces = [
        pltpu.SMEM if index in smem else pltpu.HBM if index in hbm else pltpu.VMEM
        for index in range(len(operands))
    ]
    return pl.pallas_call(
        body,
        out_shape=out_shape,
        in_specs=[pl.BlockSpec(memory_space=space) for space in spaces],
        out_specs=jax.tree.map(lambda _: VMEM_SPEC, out_shape) if out is None else out,
        scratch_shapes=list(scratch),
        compiler_params=pltpu.CompilerParams(vmem_limit_bytes=limit << 20),
        cost_estimate=pl.CostEstimate(flops=flops, bytes_accessed=1 << 20, transcendentals=0),
        name=name,
    )(
        *(
            pltpu.with_memory_space_constraint(value, pltpu.HBM) if index in hbm else value
            for index, value in enumerate(operands)
        )
    )


def per_device(raster, transmission, kernels, kernel_weight, library, clip_tile, clip_corner):
    tile = raster.shape[0]
    border = KSIZE // 2
    full = tile + KSIZE
    half = full // 2
    wide = ceil_to(full, 2 * LANES)
    table = {
        key: jnp.stack([jnp.asarray(part) for part in value])
        if isinstance(value, tuple)
        else jnp.asarray(value)
        for key, value in tables(tile).items()
    }
    cols_wide = lax.axis_size("wide")
    rows_narrow = lax.axis_size("narrow")
    device_count = cols_wide * rows_narrow
    both = ("wide", "narrow")
    clip_count = clip_tile.shape[0]
    real_count = 2 * kernels.shape[0]

    mask, sent = call(
        lambda *refs: edges_body(cols_wide, rows_narrow, *refs),
        (
            jax.ShapeDtypeStruct((tile, tile), bf16),
            jax.ShapeDtypeStruct((device_count, border, tile), bf16),
        ),
        (raster, transmission),
        scratch=(
            pltpu.VMEM((tile, tile), jnp.int32),
            pltpu.VMEM((tile, tile), bf16),
            pltpu.SemaphoreType.DMA((2,)),
        ),
        hbm=(0, 1),
        name="edges",
    )
    got = lax.all_to_all(sent, both, 0, 0, tiled=True)

    tile_line = clip_tile.reshape(1, clip_count)
    spectrum = (2, half, wide)
    basis = jax.ShapeDtypeStruct((2, CAP * KSIG, tile), bf16)
    filters, row_basis, col_basis = call(
        lambda *refs: filters_body(cols_wide, *refs),
        (pltpu.HBM((real_count,) + spectrum, f32), basis, basis),
        (
            kernels.reshape(real_count, KSIZE, KSIZE),
            table["taps_rows"],
            table["taps_cols"],
            tile_line,
            clip_corner,
        ),
        scratch=(
            pltpu.VMEM((real_count,) + spectrum, f32),
            pltpu.VMEM((2, full, 4 * KSIZE), bf16),
            pltpu.VMEM((real_count, KSIZE, KSIZE), f32),
            pltpu.VMEM(table["taps_rows"].shape, bf16),
            pltpu.VMEM(table["taps_cols"].shape, bf16),
            pltpu.VMEM((1, clip_count), jnp.int32),
            pltpu.VMEM((2, clip_count), jnp.int32),
            pltpu.SemaphoreType.DMA((5,)),
            pltpu.SemaphoreType.DMA((real_count,)),
        ),
        hbm=(0, 1, 2, 3, 4),
        out=(pl.BlockSpec(memory_space=pltpu.HBM), VMEM_SPEC, VMEM_SPEC),
        flops=4 << 30,
        name="filters",
    )
    aerial, copies = call(
        lambda *refs: image_body(cols_wide, rows_narrow, *refs),
        (
            jax.ShapeDtypeStruct((tile, tile), f32),
            jax.ShapeDtypeStruct((device_count, CAP, SIGD), bf16),
        ),
        (
            mask,
            got,
            kernel_weight,
            filters,
            row_basis,
            col_basis,
            table["rows_in"],
            table["cols_in"],
            table["cols_out"],
            table["rows_out"],
        ),
        scratch=(
            pltpu.VMEM((wide, wide), bf16),
            pltpu.VMEM(spectrum, f32),
            pltpu.VMEM((2, 2, GROUP * 2 * full, wide), bf16),
            pltpu.VMEM((2, GROUP, 2, wide, wide), bf16),
            pltpu.VMEM((tile, tile), f32),
            pltpu.VMEM((real_count,) + spectrum, f32),
            pltpu.SemaphoreType.DMA((real_count // (2 * GROUP),)),
        ),
        smem=(2,),
        hbm=(3,),
        flops=6 << 30,
        name="image",
    )
    lib_units = call(
        library_body,
        jax.ShapeDtypeStruct(library.shape, bf16),
        (library,),
        flops=1 << 30,
        name="library",
    )
    gathered = lax.all_to_all(copies, both, 0, 0, tiled=True).reshape(device_count * CAP, SIGD)
    slab = call(
        lambda *refs: match_body(cols_wide, rows_narrow, *refs),
        jax.ShapeDtypeStruct((device_count, LANES), f32),
        (tile_line, gathered, lib_units),
        limit=40,
        flops=1 << 30,
        name="match",
    )
    slab = lax.all_to_all(slab, both, 0, 0, tiled=True)[:, : clip_count // device_count]
    peak = jnp.max(slab, axis=0)
    total = jnp.sum(jnp.exp(slab - peak[None, :]), axis=0)
    scores = -(peak + jnp.log(total)) / sharpness
    return (aerial, scores)


def solution(mesh):
    placed = (
        P("narrow", "wide"),
        P("narrow", "wide"),
        P(),
        P(),
        P(("wide", "narrow"), None),
        P(),
        P(),
    )
    return jax.shard_map(
        per_device,
        mesh=mesh,
        in_specs=placed,
        out_specs=(P("narrow", "wide"), P(("wide", "narrow"))),
        check_vma=False,
    )
```

```python
import math

import jax
import jax.numpy as jnp
import numpy as np
from jax import lax
from jax.experimental import pallas as pl
from jax.experimental.pallas import tpu as pltpu
from jax.sharding import PartitionSpec as P

KSIZE = 64
CLIP = 64
KSIG = 16
CAP = 16
SIGD = KSIG * KSIG
LANES = 128
GROUP = 2

sharpness = 400.0
f32 = jnp.float32
bf16 = jnp.bfloat16
VMEM_SPEC = pl.BlockSpec(memory_space=pltpu.VMEM)


def ceil_to(value, step):
    return -(-value // step) * step


def halves(table):
    high = table.astype(bf16)
    return high, (table - high.astype(np.float64)).astype(bf16)


def tables(tile):
    full = tile + KSIZE
    half = full // 2
    wide = ceil_to(full, 2 * LANES)
    unit = 2.0 * math.pi / full
    place = np.arange(full)
    place = np.where(place < tile + KSIZE // 2, place, place - full)
    taps = np.arange(KSIZE) - KSIZE // 2
    odd = np.arange(half) + 0.5
    freq = np.arange(full)

    def padded(table, rows, cols):
        out = np.zeros((rows, cols))
        out[: table.shape[0], : table.shape[1]] = table
        return out

    def side_by_side(angle, rows, cols):
        return np.concatenate(
            [padded(np.cos(angle), rows, cols), padded(np.sin(angle), rows, cols)], axis=1
        )

    angle = unit * odd[:, None] * place[None, :]
    rows_in = padded(np.concatenate([np.cos(angle), -np.sin(angle)]), full, wide)
    cols_in = side_by_side(unit * place[:, None] * freq[None, :], wide, wide)
    cols_out = side_by_side(unit * freq[:, None] * np.arange(tile)[None, :], wide, tile)
    angle = unit * np.arange(tile)[:, None] * odd[None, :]
    rows_out = padded(np.concatenate([np.cos(angle), -np.sin(angle)], axis=1), tile, wide)
    angle = unit * odd[:, None] * taps[None, :]
    taps_rows = np.concatenate([np.cos(angle), np.sin(angle)]) * (2.0 / (full * full))
    taps_cols = side_by_side(unit * taps[:, None] * freq[None, :], KSIZE, wide)
    high, low = halves(taps_rows)
    taps_rows = np.concatenate([high, low, high, low], axis=1)
    high, low = halves(taps_cols)
    taps_cols = np.concatenate([high, high, low, low], axis=0)
    return {
        "rows_in": halves(rows_in),
        "cols_in": halves(cols_in),
        "cols_out": halves(cols_out),
        "rows_out": halves(rows_out),
        "taps_rows": taps_rows,
        "taps_cols": taps_cols,
    }


def dot(left, right):
    return jnp.dot(left, right, preferred_element_type=f32)


def split(value):
    high = value.astype(bf16)
    return high, (value - high.astype(f32)).astype(bf16)


def dot3(left, right):
    return dot(left[0], right[0]) + dot(left[1], right[0]) + dot(left[0], right[1])


def dot3_t(left, right):
    def single(a, b):
        return lax.dot_general(a, b, (((1,), (1,)), ((), ())), preferred_element_type=f32)

    return single(left[0], right[0]) + single(left[1], right[0]) + single(left[0], right[1])


def iota(shape, dim):
    return lax.broadcasted_iota(jnp.int32, shape, dim)


def shifted_basis(corner, tile):
    shape = (CAP * KSIG, tile)
    freq = iota(shape, 0) & (KSIG - 1)
    offset = iota(shape, 1) - corner
    turn = ((2 * offset + 1) * freq) & (4 * CLIP - 1)
    fold = jnp.abs(turn.astype(f32) * (1.0 / (2 * CLIP)) - 1.0) - 0.5
    x = fold * math.pi
    square = x * x
    series = jnp.full(shape, -1.0 / math.factorial(15), f32)
    for order in (13, 11, 9, 7, 5, 3, 1):
        sign = 1.0 if order % 4 == 1 else -1.0
        series = series * square + sign / math.factorial(order)
    weight = jnp.where(freq == 0, math.sqrt(1.0 / CLIP), math.sqrt(2.0 / CLIP))
    inside = (offset >= 0) & (offset < CLIP)
    return jnp.where(inside, weight * (series * x), 0.0)


def neighbours():
    return [(dw, dz) for dw in (-1, 0, 1) for dz in (-1, 0, 1) if dw or dz]


def fetched(pairs, sems):
    copies = [
        pltpu.make_async_copy(source, target, sems.at[index])
        for index, (source, target) in enumerate(pairs)
    ]
    for copy in copies:
        copy.start()
    return copies


def edges_body(
    cols_wide,
    rows_narrow,
    raster_hbm,
    light_hbm,
    mask_ref,
    sent_hbm,
    raster_ref,
    light_ref,
    strip_ref,
    sems,
    sent_sems,
):
    tile = mask_ref.shape[0]
    border = sent_hbm.shape[1]
    copies = fetched(((raster_hbm, raster_ref), (light_hbm, light_ref)), sems)
    for copy in copies:
        copy.wait()
    mask = raster_ref[...].astype(f32) * light_ref[...].astype(f32)
    mask_ref[...] = mask.astype(bf16)
    lane = iota((border, tile), 1)

    def folded(first):
        out = jnp.zeros((border, tile), f32)
        for block in range(tile // border):
            low = block * border
            moved = pltpu.roll(mask[low : low + border], (low - first) % tile, 1)
            out = jnp.where((lane >= low) & (lane < low + border), moved, out)
        return out.astype(bf16)

    strip_ref[0] = mask[:border].astype(bf16)
    strip_ref[1] = mask[tile - border :].astype(bf16)
    strip_ref[2] = folded(0)
    strip_ref[3] = folded(tile - border)
    col = lax.axis_index("wide")
    row = lax.axis_index("narrow")
    sends = []
    for index, (dw, dz) in enumerate(neighbours()):
        strip = 0 if dz < 0 else 1 if dz > 0 else 2 if dw < 0 else 3
        there = (col + dw >= 0) & (col + dw < cols_wide)
        there &= (row + dz >= 0) & (row + dz < rows_narrow)
        place = jnp.where(there, (col + dw) * rows_narrow + row + dz, 0)
        copy = pltpu.make_async_copy(
            strip_ref.at[strip], sent_hbm.at[place], sent_sems.at[index]
        )
        sends.append((there, copy))
    for there, copy in sends:
        pl.when(there)(copy.start)
    for there, copy in sends:
        pl.when(there)(copy.wait)


def transform_taps(weight_ref, taps_ref, rows_ref, cols_ref, out_ref, mixed_ref, finished):
    count = out_ref.shape[0]
    half = out_ref.shape[2]
    wide = out_ref.shape[3]

    def along_rows(index):
        taps = taps_ref[index]
        taps = taps * jnp.sqrt(jnp.full(taps.shape, weight_ref[index // 2], f32))
        spread = jnp.concatenate([taps, taps, taps, taps], axis=1)
        high, low = split(spread)
        stacked = jnp.concatenate([high, high, low, low], axis=0)
        rows = dot(rows_ref[...], stacked)
        kept = rows.astype(bf16).astype(f32)
        is_low = (iota(rows.shape, 1) & KSIZE) != 0
        mixed_ref[index % 2] = jnp.where(is_low, rows - kept, rows).astype(bf16)

    def along_cols(index):
        both = dot(mixed_ref[index % 2], cols_ref[...])
        out_ref[index, 0] = both[:half, :wide] - both[half:, wide:]
        out_ref[index, 1] = both[:half, wide:] + both[half:, :wide]
        finished[index].start()

    along_rows(0)
    for index in range(count):
        if index + 1 < count:
            along_rows(index + 1)
        along_cols(index)


def filters_body(
    cols_wide,
    weight_ref,
    taps_hbm,
    rows_hbm,
    cols_hbm,
    tile_hbm,
    corner_hbm,
    out_hbm,
    rb_ref,
    cb_ref,
    out_ref,
    mixed_ref,
    taps_ref,
    rows_ref,
    cols_ref,
    tile_ref,
    corner_ref,
    sems,
    out_sems,
):
    pairs = (
        (taps_hbm, taps_ref),
        (rows_hbm, rows_ref),
        (cols_hbm, cols_ref),
        (tile_hbm, tile_ref),
        (corner_hbm, corner_ref),
    )
    for copy in fetched(pairs, sems):
        copy.wait()
    finished = [
        pltpu.make_async_copy(out_ref.at[index], out_hbm.at[index], out_sems.at[index])
        for index in range(out_ref.shape[0])
    ]
    transform_taps(weight_ref, taps_ref, rows_ref, cols_ref, out_ref, mixed_ref, finished)
    clip_count = tile_ref.shape[1]
    own_tile = lax.axis_index("narrow") * cols_wide + lax.axis_index("wide")
    owned = tile_ref[...] == own_tile
    owned8 = jnp.broadcast_to(owned.astype(f32), (8, clip_count))
    square = (clip_count, clip_count)
    earlier = (iota(square, 0) < iota(square, 1)).astype(f32).astype(bf16)
    rank = dot(owned8.astype(bf16), earlier)[:1]
    rank = jnp.where(owned, rank, -1.0)
    slot = (iota((CAP * KSIG, clip_count), 0) // KSIG).astype(f32)
    select = (slot == rank).astype(f32).astype(bf16)
    tile = rb_ref.shape[2]
    for axis, basis_ref in ((0, rb_ref), (1, cb_ref)):
        line = corner_ref[axis : axis + 1, :].astype(f32).astype(bf16)
        table = jnp.broadcast_to(line, (tile, clip_count))
        corner = lax.dot_general(
            select, table, (((1,), (1,)), ((), ())), preferred_element_type=f32
        )
        high, low = split(shifted_basis(corner.astype(jnp.int32), tile))
        basis_ref[0] = high
        basis_ref[1] = low
    for copy in finished:
        copy.wait()


def image_body(
    cols_wide,
    rows_narrow,
    own_ref,
    got_ref,
    filter_hbm,
    rb_ref,
    cb_ref,
    rows_in_ref,
    cols_in_ref,
    cols_out_ref,
    rows_out_ref,
    aerial_ref,
    units_ref,
    mask_ref,
    spec_ref,
    prod_ref,
    mid_ref,
    sum_ref,
    filter_ref,
    sems,
):
    tile = own_ref.shape[0]
    half = filter_ref.shape[2]
    full = 2 * half
    wide = filter_ref.shape[3]
    border = KSIZE // 2
    kernel_count = filter_ref.shape[0] // 2
    group = prod_ref.shape[2] // (2 * full)

    def arriving(index):
        part = pl.ds(index * 2 * group, 2 * group)
        return pltpu.make_async_copy(filter_hbm.at[part], filter_ref.at[part], sems.at[index])

    def request(index, carry):
        arriving(index).start()
        return carry

    lax.fori_loop(0, kernel_count // group, request, 0)
    col = lax.axis_index("wide")
    row = lax.axis_index("narrow")
    lane = iota((border, tile), 1)

    def from_neighbour(dw, dz):
        there = (col + dw >= 0) & (col + dw < cols_wide)
        there &= (row + dz >= 0) & (row + dz < rows_narrow)
        place = jnp.where(there, (col + dw) * rows_narrow + row + dz, 0)
        return jnp.where(there, got_ref[place].astype(f32), 0.0)

    def beside(right, right_shift, left, left_shift):
        right = pltpu.roll(right, right_shift % tile, 1)
        left = pltpu.roll(left, left_shift % tile, 1)
        return jnp.where(lane < border, right, jnp.where(lane < 2 * border, left, 0.0)).astype(bf16)

    mask_ref[:tile, :tile] = own_ref[...]
    right = from_neighbour(1, 0)
    left = from_neighbour(-1, 0)
    for low in range(0, tile, border):
        mask_ref[low : low + border, tile:] = beside(right, -low, left, border - low)
    for low, dz in ((tile, 1), (tile + border, -1)):
        mask_ref[low : low + border, :tile] = from_neighbour(0, dz).astype(bf16)
        mask_ref[low : low + border, tile:] = beside(
            from_neighbour(1, dz), 0, from_neighbour(-1, dz), 2 * border
        )
    mask_ref[full:, :] = jnp.zeros((wide - full, wide), bf16)
    for place in range(2):
        for member in range(mid_ref.shape[1]):
            mid_ref[place, member, :, full:, :] = jnp.zeros((2, wide - full, wide), bf16)
    mask = mask_ref[...]
    rows = dot(rows_in_ref[0], mask) + dot(rows_in_ref[1], mask)
    both = dot3(split(rows), (cols_in_ref[0], cols_in_ref[1]))
    spec_ref[0] = both[:half, :wide] + both[half:, wide:]
    spec_ref[1] = both[half:, :wide] - both[:half, wide:]

    def multiply(index):
        arriving(index).wait()
        place = prod_ref.at[index % 2]
        for part in range(2 * group):
            number = 2 * group * index + part
            ref = filter_ref.at[number]
            base = part * full
            high, low = split(spec_ref[0] * ref[0] - spec_ref[1] * ref[1])
            place[0, base : base + half] = high
            place[1, base : base + half] = low
            high, low = split(spec_ref[0] * ref[1] + spec_ref[1] * ref[0])
            place[0, base + half : base + full] = high
            place[1, base + half : base + full] = low

    def along_cols(index):
        source = prod_ref.at[index % 2]
        cols = dot3((source[0], source[1]), (cols_out_ref[0], cols_out_ref[1]))
        for part in range(2 * group):
            place = mid_ref.at[index % 2, part // 2]
            base = part * full
            lane = part % 2 * tile
            real = cols[base : base + half]
            imag = cols[base + half : base + full]
            high, low = split(real[:, :tile] - imag[:, tile:])
            place[0, :half, lane : lane + tile] = high
            place[1, :half, lane : lane + tile] = low
            high, low = split(imag[:, :tile] + real[:, tile:])
            place[0, half:full, lane : lane + tile] = high
            place[1, half:full, lane : lane + tile] = low

    def along_rows(index):
        value = None
        for member in range(group):
            source = mid_ref.at[index % 2, member]
            field = dot3((rows_out_ref[0], rows_out_ref[1]), (source[0], source[1]))
            energy = field * field
            term = energy[:, :tile] + energy[:, tile:]
            value = term if value is None else value + term
        if index == 0:
            sum_ref[...] = value
        elif index == kernel_count // group - 1:
            aerial_ref[...] = sum_ref[...] + value
        else:
            sum_ref[...] += value

    for step in range(kernel_count // group + 2):
        if step < kernel_count // group:
            multiply(step)
        if 0 <= step - 1 < kernel_count // group:
            along_cols(step - 1)
        if 0 <= step - 2:
            along_rows(step - 2)

    halfway = dot3((rb_ref[0], rb_ref[1]), split(aerial_ref[...]))
    crossed = dot3_t(split(halfway), (cb_ref[0], cb_ref[1]))
    shape = (CAP * KSIG, CAP * KSIG)
    crossed = jnp.where(iota(shape, 0) // KSIG == iota(shape, 1) // KSIG, crossed, 0.0)
    fold = ((iota(shape, 0) & (KSIG - 1)) == (iota(shape, 1) & (KSIG - 1))).astype(f32).astype(bf16)
    high, low = split(crossed)
    spread = dot(high, fold) + dot(low, fold)
    spread = jnp.where((iota(shape, 0) & (KSIG - 1)) == iota(shape, 1) // KSIG, spread, 0.0)
    signature = jnp.sum(spread.reshape(CAP, KSIG, SIGD), axis=1)
    signature = jnp.where(iota(signature.shape, 1) == 0, 0.0, signature)
    mean_square = jnp.mean(signature * signature, axis=1, keepdims=True)
    units = (signature / (KSIG * jnp.sqrt(mean_square + 1e-06))).astype(bf16)
    units_ref[...] = jnp.broadcast_to(units[None], units_ref.shape)


def library_body(library_ref, out_ref):
    rows = library_ref[...].astype(f32)
    mean_square = jnp.mean(rows * rows, axis=1, keepdims=True)
    out_ref[...] = (rows * (1.0 / (KSIG * jnp.sqrt(mean_square + 1e-06)))).astype(bf16)


def match_body(cols_wide, rows_narrow, tile_ref, gathered_ref, library_ref, out_ref):
    clip_count = tile_ref.shape[1]
    slot_count = gathered_ref.shape[0]
    device_count = out_ref.shape[0]
    own_count = clip_count // device_count
    row = tile_ref[...].astype(f32)
    peaks = []
    for first in range(0, clip_count, LANES):
        shape = (LANES, clip_count)
        clip = iota(shape, 0) + first
        other = iota(shape, 1)
        spread = jnp.broadcast_to(row, shape)
        column = jnp.sum(jnp.where(clip == other, spread, 0.0), axis=1, keepdims=True)
        before = (spread == column) & (other < clip)
        rank = jnp.sum(before.astype(f32), axis=1, keepdims=True)
        grid_row = jnp.floor((column + 0.5) * (1.0 / cols_wide))
        holder = (column - grid_row * cols_wide) * rows_narrow + grid_row
        place = (holder * CAP + rank).astype(jnp.int32)
        pick = (iota((LANES, slot_count), 1) == place).astype(f32).astype(bf16)
        units = dot(pick, gathered_ref[...]).astype(bf16)
        cosine = lax.dot_general(
            library_ref[...], units, (((1,), (1,)), ((), ())), preferred_element_type=f32
        )
        logits = sharpness * (cosine - 1.0)
        peak = jnp.max(logits, axis=0, keepdims=True)
        total = jnp.sum(jnp.exp(logits - peak), axis=0, keepdims=True)
        peaks.append(peak + jnp.log(total))
    slab = peaks[0] if len(peaks) == 1 else jnp.concatenate(peaks, axis=1)
    shape = (device_count, clip_count)
    spread = jnp.broadcast_to(slab, shape)
    lane = iota((device_count, LANES), 1)
    sent = jnp.zeros((device_count, LANES), f32)
    for index in range(own_count):
        mine = iota(shape, 1) == iota(shape, 0) * own_count + index
        value = jnp.sum(jnp.where(mine, spread, 0.0), axis=1, keepdims=True)
        sent = jnp.where(lane == index, value, sent)
    out_ref[...] = sent


def call(
    body, out_shape, operands, scratch=(), limit=24, smem=(), hbm=(), out=None, flops=0, name=None
):
    spaces = [
        pltpu.SMEM if index in smem else pltpu.HBM if index in hbm else pltpu.VMEM
        for index in range(len(operands))
    ]
    return pl.pallas_call(
        body,
        out_shape=out_shape,
        in_specs=[pl.BlockSpec(memory_space=space) for space in spaces],
        out_specs=jax.tree.map(lambda _: VMEM_SPEC, out_shape) if out is None else out,
        scratch_shapes=list(scratch),
        compiler_params=pltpu.CompilerParams(vmem_limit_bytes=limit << 20),
        cost_estimate=pl.CostEstimate(flops=flops, bytes_accessed=1 << 20, transcendentals=0),
        name=name,
    )(
        *(
            pltpu.with_memory_space_constraint(value, pltpu.HBM) if index in hbm else value
            for index, value in enumerate(operands)
        )
    )


def per_device(raster, transmission, kernels, kernel_weight, library, clip_tile, clip_corner):
    tile = raster.shape[0]
    border = KSIZE // 2
    full = tile + KSIZE
    half = full // 2
    wide = ceil_to(full, 2 * LANES)
    table = {
        key: jnp.stack([jnp.asarray(part) for part in value])
        if isinstance(value, tuple)
        else jnp.asarray(value)
        for key, value in tables(tile).items()
    }
    cols_wide = lax.axis_size("wide")
    rows_narrow = lax.axis_size("narrow")
    device_count = cols_wide * rows_narrow
    both = ("wide", "narrow")
    clip_count = clip_tile.shape[0]
    real_count = 2 * kernels.shape[0]

    mask, sent = call(
        lambda *refs: edges_body(cols_wide, rows_narrow, *refs),
        (
            jax.ShapeDtypeStruct((tile, tile), bf16),
            pltpu.HBM((device_count, border, tile), bf16),
        ),
        (raster, transmission),
        scratch=(
            pltpu.VMEM((tile, tile), jnp.int32),
            pltpu.VMEM((tile, tile), bf16),
            pltpu.VMEM((4, border, tile), bf16),
            pltpu.SemaphoreType.DMA((2,)),
            pltpu.SemaphoreType.DMA((8,)),
        ),
        out=(VMEM_SPEC, pl.BlockSpec(memory_space=pltpu.HBM)),
        hbm=(0, 1),
        name="edges",
    )
    got = lax.all_to_all(sent, both, 0, 0, tiled=True)

    tile_line = clip_tile.reshape(1, clip_count)
    spectrum = (2, half, wide)
    basis = jax.ShapeDtypeStruct((2, CAP * KSIG, tile), bf16)
    filters, row_basis, col_basis = call(
        lambda *refs: filters_body(cols_wide, *refs),
        (pltpu.HBM((real_count,) + spectrum, f32), basis, basis),
        (
            kernel_weight,
            kernels.reshape(real_count, KSIZE, KSIZE),
            table["taps_rows"],
            table["taps_cols"],
            tile_line,
            clip_corner,
        ),
        scratch=(
            pltpu.VMEM((real_count,) + spectrum, f32),
            pltpu.VMEM((2, full, 4 * KSIZE), bf16),
            pltpu.VMEM((real_count, KSIZE, KSIZE), f32),
            pltpu.VMEM(table["taps_rows"].shape, bf16),
            pltpu.VMEM(table["taps_cols"].shape, bf16),
            pltpu.VMEM((1, clip_count), jnp.int32),
            pltpu.VMEM((2, clip_count), jnp.int32),
            pltpu.SemaphoreType.DMA((5,)),
            pltpu.SemaphoreType.DMA((real_count,)),
        ),
        smem=(0,),
        hbm=(1, 2, 3, 4, 5),
        out=(pl.BlockSpec(memory_space=pltpu.HBM), VMEM_SPEC, VMEM_SPEC),
        flops=4 << 30,
        name="filters",
    )
    aerial, copies = call(
        lambda *refs: image_body(cols_wide, rows_narrow, *refs),
        (
            jax.ShapeDtypeStruct((tile, tile), f32),
            jax.ShapeDtypeStruct((device_count, CAP, SIGD), bf16),
        ),
        (
            mask,
            got,
            filters,
            row_basis,
            col_basis,
            table["rows_in"],
            table["cols_in"],
            table["cols_out"],
            table["rows_out"],
        ),
        scratch=(
            pltpu.VMEM((wide, wide), bf16),
            pltpu.VMEM(spectrum, f32),
            pltpu.VMEM((2, 2, GROUP * 2 * full, wide), bf16),
            pltpu.VMEM((2, GROUP, 2, wide, wide), bf16),
            pltpu.VMEM((tile, tile), f32),
            pltpu.VMEM((real_count,) + spectrum, f32),
            pltpu.SemaphoreType.DMA((real_count // (2 * GROUP),)),
        ),
        hbm=(2,),
        flops=6 << 30,
        name="image",
    )
    lib_units = call(
        library_body,
        jax.ShapeDtypeStruct(library.shape, bf16),
        (library,),
        flops=1 << 30,
        name="library",
    )
    gathered = lax.all_to_all(copies, both, 0, 0, tiled=True).reshape(device_count * CAP, SIGD)
    slab = call(
        lambda *refs: match_body(cols_wide, rows_narrow, *refs),
        jax.ShapeDtypeStruct((device_count, LANES), f32),
        (tile_line, gathered, lib_units),
        limit=40,
        flops=1 << 30,
        name="match",
    )
    slab = lax.all_to_all(slab, both, 0, 0, tiled=True)[:, : clip_count // device_count]
    peak = jnp.max(slab, axis=0)
    total = jnp.sum(jnp.exp(slab - peak[None, :]), axis=0)
    scores = -(peak + jnp.log(total)) / sharpness
    return (aerial, scores)


def solution(mesh):
    placed = (
        P("narrow", "wide"),
        P("narrow", "wide"),
        P(),
        P(),
        P(("wide", "narrow"), None),
        P(),
        P(),
    )
    return jax.shard_map(
        per_device,
        mesh=mesh,
        in_specs=placed,
        out_specs=(P("narrow", "wide"), P(("wide", "narrow"))),
        check_vma=False,
    )
```

```python
import math

import jax
import jax.numpy as jnp
import numpy as np
from jax import lax
from jax.experimental import pallas as pl
from jax.experimental.pallas import tpu as pltpu
from jax.sharding import PartitionSpec as P

KSIZE = 64
CLIP = 64
KSIG = 16
CAP = 16
SIGD = KSIG * KSIG
LANES = 128
GROUP = 2

sharpness = 400.0
f32 = jnp.float32
bf16 = jnp.bfloat16
VMEM_SPEC = pl.BlockSpec(memory_space=pltpu.VMEM)


def ceil_to(value, step):
    return -(-value // step) * step


def halves(table):
    high = table.astype(bf16)
    return high, (table - high.astype(np.float64)).astype(bf16)


def thirds(table):
    high, rest = table.astype(bf16), table - table.astype(bf16).astype(np.float64)
    middle = rest.astype(bf16)
    return high, middle, (rest - middle.astype(np.float64)).astype(bf16)


def tables(tile):
    full = tile + KSIZE
    half = full // 2
    lanes = ceil_to(half, LANES)
    wide = 2 * lanes
    unit = 2.0 * math.pi / full
    place = np.arange(full)
    place = np.where(place < tile + KSIZE // 2, place, place - full)
    taps = np.arange(KSIZE) - KSIZE // 2
    odd = np.arange(half) + 0.5

    def padded(table, rows, cols):
        out = np.zeros((rows, cols))
        out[: table.shape[0], : table.shape[1]] = table
        return out

    def side_by_side(angle, rows):
        return np.concatenate(
            [padded(np.cos(angle), rows, lanes), padded(np.sin(angle), rows, lanes)], axis=1
        )

    angle = unit * odd[:, None] * place[None, :]
    rows_in = padded(np.concatenate([np.cos(angle), -np.sin(angle)]), full, wide)
    cols_in = side_by_side(unit * place[:, None] * odd[None, :], wide)
    angle = unit * odd[:, None] * np.arange(tile)[None, :]
    cols_out = np.concatenate(
        [padded(np.cos(angle), lanes, tile), padded(np.sin(angle), lanes, tile)]
    )
    angle = unit * np.arange(tile)[:, None] * odd[None, :]
    rows_out = padded(np.concatenate([np.cos(angle), -np.sin(angle)], axis=1), tile, wide)
    angle = unit * odd[:, None] * taps[None, :]
    taps_rows = np.concatenate([np.cos(angle), np.sin(angle)]) * (2.0 / (full * full))
    taps_cols = side_by_side(unit * taps[:, None] * odd[None, :], KSIZE)
    high, middle, low = thirds(taps_rows)
    taps_rows = np.concatenate([high, middle, low, high, middle, high], axis=1)
    high, middle, low = thirds(taps_cols)
    taps_cols = np.concatenate([high, middle, low, high, middle, high], axis=0)
    return {
        "rows_in": thirds(rows_in),
        "cols_in": thirds(cols_in),
        "cols_out": np.concatenate(halves(cols_out), axis=1),
        "rows_out": halves(rows_out),
        "taps_rows": taps_rows,
        "taps_cols": taps_cols,
    }


def dot(left, right):
    return jnp.dot(left, right, preferred_element_type=f32)


def split(value):
    high = value.astype(bf16)
    return high, (value - high.astype(f32)).astype(bf16)


def split3(value):
    high = value.astype(bf16)
    middle, low = split(value - high.astype(f32))
    return high, middle, low


def dot3(left, right):
    return dot(left[0], right[0]) + dot(left[1], right[0]) + dot(left[0], right[1])


def dot3_t(left, right):
    def single(a, b):
        return lax.dot_general(a, b, (((1,), (1,)), ((), ())), preferred_element_type=f32)

    return single(left[0], right[0]) + single(left[1], right[0]) + single(left[0], right[1])


def iota(shape, dim):
    return lax.broadcasted_iota(jnp.int32, shape, dim)


def shifted_basis(corner, tile):
    shape = (CAP * KSIG, tile)
    freq = iota(shape, 0) & (KSIG - 1)
    offset = iota(shape, 1) - corner
    turn = ((2 * offset + 1) * freq) & (4 * CLIP - 1)
    fold = jnp.abs(turn.astype(f32) * (1.0 / (2 * CLIP)) - 1.0) - 0.5
    x = fold * math.pi
    square = x * x
    series = jnp.full(shape, -1.0 / math.factorial(15), f32)
    for order in (13, 11, 9, 7, 5, 3, 1):
        sign = 1.0 if order % 4 == 1 else -1.0
        series = series * square + sign / math.factorial(order)
    weight = jnp.where(freq == 0, math.sqrt(1.0 / CLIP), math.sqrt(2.0 / CLIP))
    inside = (offset >= 0) & (offset < CLIP)
    return jnp.where(inside, weight * (series * x), 0.0)


def neighbours():
    return [(dw, dz) for dw in (-1, 0, 1) for dz in (-1, 0, 1) if dw or dz]


def fetched(pairs, sems):
    copies = [
        pltpu.make_async_copy(source, target, sems.at[index])
        for index, (source, target) in enumerate(pairs)
    ]
    for copy in copies:
        copy.start()
    return copies


def edges_body(
    cols_wide,
    rows_narrow,
    raster_hbm,
    light_hbm,
    mask_ref,
    sent_hbm,
    raster_ref,
    light_ref,
    strip_ref,
    sems,
    sent_sems,
):
    tile = mask_ref.shape[0]
    border = sent_hbm.shape[1]
    copies = fetched(((raster_hbm, raster_ref), (light_hbm, light_ref)), sems)
    for copy in copies:
        copy.wait()
    mask = raster_ref[...].astype(f32) * light_ref[...].astype(f32)
    mask_ref[...] = mask.astype(bf16)
    lane = iota((border, tile), 1)

    def folded(first):
        out = jnp.zeros((border, tile), f32)
        for block in range(tile // border):
            low = block * border
            moved = pltpu.roll(mask[low : low + border], (low - first) % tile, 1)
            out = jnp.where((lane >= low) & (lane < low + border), moved, out)
        return out.astype(bf16)

    strip_ref[0] = mask[:border].astype(bf16)
    strip_ref[1] = mask[tile - border :].astype(bf16)
    strip_ref[2] = folded(0)
    strip_ref[3] = folded(tile - border)
    col = lax.axis_index("wide")
    row = lax.axis_index("narrow")
    sends = []
    for index, (dw, dz) in enumerate(neighbours()):
        strip = 0 if dz < 0 else 1 if dz > 0 else 2 if dw < 0 else 3
        there = (col + dw >= 0) & (col + dw < cols_wide)
        there &= (row + dz >= 0) & (row + dz < rows_narrow)
        place = jnp.where(there, (col + dw) * rows_narrow + row + dz, 0)
        copy = pltpu.make_async_copy(
            strip_ref.at[strip], sent_hbm.at[place], sent_sems.at[index]
        )
        sends.append((there, copy))
    for there, copy in sends:
        pl.when(there)(copy.start)
    for there, copy in sends:
        pl.when(there)(copy.wait)


def transform_taps(weight_ref, taps_ref, rows_ref, cols_ref, out_ref, mixed_ref, finished):
    count = out_ref.shape[0]
    half = out_ref.shape[2]
    lanes = out_ref.shape[3] // 2

    def along_rows(index):
        taps = taps_ref[index]
        taps = taps * jnp.sqrt(jnp.full(taps.shape, weight_ref[index // 2], f32))
        high, middle, low = split3(jnp.concatenate([taps, taps], axis=1))
        stacked = jnp.concatenate([high, high, high, middle, middle, low], axis=0)
        rows = dot(rows_ref[...], stacked)
        high, middle, low = split3(rows)
        first = iota(rows.shape, 1) < KSIZE
        pairs = ((high, high), (high, middle), (middle, low))
        for place, (left, right) in enumerate(pairs):
            value = jnp.where(first, left.astype(f32), right.astype(f32)).astype(bf16)
            mixed_ref[index % 2, :, place * 2 * KSIZE : (place + 1) * 2 * KSIZE] = value

    def along_cols(index):
        both = dot(mixed_ref[index % 2], cols_ref[...])
        out_ref[index, 0, :, :lanes] = both[:half, :lanes] - both[half:, lanes:]
        out_ref[index, 0, :, lanes:] = both[:half, :lanes] + both[half:, lanes:]
        out_ref[index, 1, :, :lanes] = both[half:, :lanes] + both[:half, lanes:]
        out_ref[index, 1, :, lanes:] = both[half:, :lanes] - both[:half, lanes:]
        finished[index].start()

    along_rows(0)
    for index in range(count):
        if index + 1 < count:
            along_rows(index + 1)
        along_cols(index)


def filters_body(
    cols_wide,
    weight_ref,
    taps_hbm,
    rows_hbm,
    cols_hbm,
    tile_hbm,
    corner_hbm,
    out_hbm,
    rb_ref,
    cb_ref,
    out_ref,
    mixed_ref,
    taps_ref,
    rows_ref,
    cols_ref,
    tile_ref,
    corner_ref,
    sems,
    out_sems,
):
    pairs = (
        (taps_hbm, taps_ref),
        (rows_hbm, rows_ref),
        (cols_hbm, cols_ref),
        (tile_hbm, tile_ref),
        (corner_hbm, corner_ref),
    )
    for copy in fetched(pairs, sems):
        copy.wait()
    finished = [
        pltpu.make_async_copy(out_ref.at[index], out_hbm.at[index], out_sems.at[index])
        for index in range(out_ref.shape[0])
    ]
    transform_taps(weight_ref, taps_ref, rows_ref, cols_ref, out_ref, mixed_ref, finished)
    clip_count = tile_ref.shape[1]
    own_tile = lax.axis_index("narrow") * cols_wide + lax.axis_index("wide")
    owned = tile_ref[...] == own_tile
    owned8 = jnp.broadcast_to(owned.astype(f32), (8, clip_count))
    square = (clip_count, clip_count)
    earlier = (iota(square, 0) < iota(square, 1)).astype(f32).astype(bf16)
    rank = dot(owned8.astype(bf16), earlier)[:1]
    rank = jnp.where(owned, rank, -1.0)
    slot = (iota((CAP * KSIG, clip_count), 0) // KSIG).astype(f32)
    select = (slot == rank).astype(f32).astype(bf16)
    tile = rb_ref.shape[2]
    for axis, basis_ref in ((0, rb_ref), (1, cb_ref)):
        line = corner_ref[axis : axis + 1, :].astype(f32).astype(bf16)
        table = jnp.broadcast_to(line, (tile, clip_count))
        corner = lax.dot_general(
            select, table, (((1,), (1,)), ((), ())), preferred_element_type=f32
        )
        high, low = split(shifted_basis(corner.astype(jnp.int32), tile))
        basis_ref[0] = high
        basis_ref[1] = low
    for copy in finished:
        copy.wait()


def image_body(
    cols_wide,
    rows_narrow,
    own_ref,
    got_ref,
    filter_hbm,
    rb_ref,
    cb_ref,
    rows_in_ref,
    cols_in_ref,
    cols_out_ref,
    rows_out_ref,
    aerial_ref,
    units_ref,
    mask_ref,
    spec_ref,
    prod_ref,
    mid_ref,
    sum_ref,
    filter_ref,
    sems,
):
    tile = own_ref.shape[0]
    half = filter_ref.shape[2]
    full = 2 * half
    wide = filter_ref.shape[3]
    border = KSIZE // 2
    kernel_count = filter_ref.shape[0] // 2
    group = prod_ref.shape[2] // (2 * full)

    def arriving(index):
        part = pl.ds(index * kernel_count, kernel_count)
        return pltpu.make_async_copy(filter_hbm.at[part], filter_ref.at[part], sems.at[index])

    def request(index, carry):
        arriving(index).start()
        return carry

    lax.fori_loop(0, 2, request, 0)
    col = lax.axis_index("wide")
    row = lax.axis_index("narrow")
    lane = iota((border, tile), 1)

    def from_neighbour(dw, dz):
        there = (col + dw >= 0) & (col + dw < cols_wide)
        there &= (row + dz >= 0) & (row + dz < rows_narrow)
        place = jnp.where(there, (col + dw) * rows_narrow + row + dz, 0)
        return jnp.where(there, got_ref[place].astype(f32), 0.0)

    def beside(right, right_shift, left, left_shift):
        right = pltpu.roll(right, right_shift % tile, 1)
        left = pltpu.roll(left, left_shift % tile, 1)
        return jnp.where(lane < border, right, jnp.where(lane < 2 * border, left, 0.0)).astype(bf16)

    mask_ref[:tile, :tile] = own_ref[...]
    right = from_neighbour(1, 0)
    left = from_neighbour(-1, 0)
    for low in range(0, tile, border):
        mask_ref[low : low + border, tile:] = beside(right, -low, left, border - low)
    for low, dz in ((tile, 1), (tile + border, -1)):
        mask_ref[low : low + border, :tile] = from_neighbour(0, dz).astype(bf16)
        mask_ref[low : low + border, tile:] = beside(
            from_neighbour(1, dz), 0, from_neighbour(-1, dz), 2 * border
        )
    mask_ref[full:, :] = jnp.zeros((wide - full, wide), bf16)
    for place in range(2):
        for member in range(mid_ref.shape[1]):
            mid_ref[place, member, :, full:, :] = jnp.zeros((2, wide - full, wide), bf16)
    mask = mask_ref[...]
    rows = (dot(rows_in_ref[2], mask) + dot(rows_in_ref[1], mask)) + dot(rows_in_ref[0], mask)
    high, middle, low = split3(rows)
    both = dot(low, cols_in_ref[0]) + dot(high, cols_in_ref[2]) + dot(middle, cols_in_ref[1])
    both = (both + dot(middle, cols_in_ref[0]) + dot(high, cols_in_ref[1])) + dot(high, cols_in_ref[0])
    lanes = wide // 2
    spec_ref[0, :, :lanes] = both[:half, :lanes] + both[half:, lanes:]
    spec_ref[0, :, lanes:] = both[:half, :lanes] - both[half:, lanes:]
    spec_ref[1, :, :lanes] = both[half:, :lanes] - both[:half, lanes:]
    spec_ref[1, :, lanes:] = both[half:, :lanes] + both[:half, lanes:]

    def multiply(index):
        place = prod_ref.at[index % 2]
        for part in range(2 * group):
            ref = filter_ref.at[2 * group * index + part]
            base = part * full
            real = spec_ref[0] * ref[0] - spec_ref[1] * ref[1]
            imag = spec_ref[0] * ref[1] + spec_ref[1] * ref[0]
            pieces = (
                (0, 0, real[:, :lanes] + real[:, lanes:]),
                (0, lanes, imag[:, lanes:] - imag[:, :lanes]),
                (half, 0, imag[:, :lanes] + imag[:, lanes:]),
                (half, lanes, real[:, :lanes] - real[:, lanes:]),
            )
            for down, lane, piece in pieces:
                for order, value in enumerate(split3(piece)):
                    place[order, base + down : base + down + half, lane : lane + lanes] = value

    def along_cols(index):
        source = prod_ref.at[index % 2]
        table = cols_out_ref[...]
        cols = dot(source[2], table) + dot(source[1], table) + dot(source[0], table)
        for part in range(2 * group):
            place = mid_ref.at[index % 2, part // 2]
            base = part * full
            lane = part % 2 * tile
            high, low = split(cols[base : base + full, :tile] + cols[base : base + full, tile:])
            place[0, :full, lane : lane + tile] = high
            place[1, :full, lane : lane + tile] = low

    def along_rows(index):
        value = None
        for member in range(group):
            source = mid_ref.at[index % 2, member]
            field = dot3((rows_out_ref[0], rows_out_ref[1]), (source[0], source[1]))
            energy = field * field
            term = energy[:, :tile] + energy[:, tile:]
            value = term if value is None else value + term
        if index == 0:
            sum_ref[...] = value
        elif index == kernel_count // group - 1:
            aerial_ref[...] = sum_ref[...] + value
        else:
            sum_ref[...] += value

    for step in range(kernel_count // group + 2):
        if step % (kernel_count // (2 * group)) == 0 and step < kernel_count // group:
            arriving(step // (kernel_count // (2 * group))).wait()
        if step < kernel_count // group:
            multiply(step)
        if 0 <= step - 1 < kernel_count // group:
            along_cols(step - 1)
        if 0 <= step - 2:
            along_rows(step - 2)

    halfway = dot3((rb_ref[0], rb_ref[1]), split(aerial_ref[...]))
    crossed = dot3_t(split(halfway), (cb_ref[0], cb_ref[1]))
    shape = (CAP * KSIG, CAP * KSIG)
    crossed = jnp.where(iota(shape, 0) // KSIG == iota(shape, 1) // KSIG, crossed, 0.0)
    fold = ((iota(shape, 0) & (KSIG - 1)) == (iota(shape, 1) & (KSIG - 1))).astype(f32).astype(bf16)
    high = crossed.astype(bf16)
    middle, low = split(crossed - high.astype(f32))
    spread = (dot(low, fold) + dot(middle, fold)) + dot(high, fold)
    spread = jnp.where((iota(shape, 0) & (KSIG - 1)) == iota(shape, 1) // KSIG, spread, 0.0)
    signature = jnp.sum(spread.reshape(CAP, KSIG, SIGD), axis=1)
    signature = jnp.where(iota(signature.shape, 1) == 0, 0.0, signature)
    mean_square = jnp.mean(signature * signature, axis=1, keepdims=True)
    units = (signature / (KSIG * jnp.sqrt(mean_square + 1e-06))).astype(bf16)
    units_ref[...] = jnp.broadcast_to(units[None], units_ref.shape)


def library_body(library_ref, out_ref):
    rows = library_ref[...].astype(f32)
    mean_square = jnp.mean(rows * rows, axis=1, keepdims=True)
    out_ref[...] = (rows * (1.0 / (KSIG * jnp.sqrt(mean_square + 1e-06)))).astype(bf16)


def match_body(cols_wide, rows_narrow, tile_ref, gathered_ref, library_ref, out_ref):
    clip_count = tile_ref.shape[1]
    slot_count = gathered_ref.shape[0]
    device_count = out_ref.shape[0]
    own_count = clip_count // device_count
    row = tile_ref[...].astype(f32)
    peaks = []
    for first in range(0, clip_count, LANES):
        shape = (LANES, clip_count)
        clip = iota(shape, 0) + first
        other = iota(shape, 1)
        spread = jnp.broadcast_to(row, shape)
        column = jnp.sum(jnp.where(clip == other, spread, 0.0), axis=1, keepdims=True)
        before = (spread == column) & (other < clip)
        rank = jnp.sum(before.astype(f32), axis=1, keepdims=True)
        grid_row = jnp.floor((column + 0.5) * (1.0 / cols_wide))
        holder = (column - grid_row * cols_wide) * rows_narrow + grid_row
        place = (holder * CAP + rank).astype(jnp.int32)
        pick = (iota((LANES, slot_count), 1) == place).astype(f32).astype(bf16)
        units = dot(pick, gathered_ref[...]).astype(bf16)
        cosine = lax.dot_general(
            library_ref[...], units, (((1,), (1,)), ((), ())), preferred_element_type=f32
        )
        logits = sharpness * (cosine - 1.0)
        peak = jnp.max(logits, axis=0, keepdims=True)
        total = jnp.sum(jnp.exp(logits - peak), axis=0, keepdims=True)
        peaks.append(peak + jnp.log(total))
    slab = peaks[0] if len(peaks) == 1 else jnp.concatenate(peaks, axis=1)
    shape = (device_count, clip_count)
    spread = jnp.broadcast_to(slab, shape)
    lane = iota((device_count, LANES), 1)
    sent = jnp.zeros((device_count, LANES), f32)
    for index in range(own_count):
        mine = iota(shape, 1) == iota(shape, 0) * own_count + index
        value = jnp.sum(jnp.where(mine, spread, 0.0), axis=1, keepdims=True)
        sent = jnp.where(lane == index, value, sent)
    out_ref[...] = sent


def call(
    body, out_shape, operands, scratch=(), limit=24, smem=(), hbm=(), out=None, flops=0, name=None
):
    spaces = [
        pltpu.SMEM if index in smem else pltpu.HBM if index in hbm else pltpu.VMEM
        for index in range(len(operands))
    ]
    return pl.pallas_call(
        body,
        out_shape=out_shape,
        in_specs=[pl.BlockSpec(memory_space=space) for space in spaces],
        out_specs=jax.tree.map(lambda _: VMEM_SPEC, out_shape) if out is None else out,
        scratch_shapes=list(scratch),
        compiler_params=pltpu.CompilerParams(vmem_limit_bytes=limit << 20),
        cost_estimate=pl.CostEstimate(flops=flops, bytes_accessed=1 << 20, transcendentals=0),
        name=name,
    )(
        *(
            pltpu.with_memory_space_constraint(value, pltpu.HBM) if index in hbm else value
            for index, value in enumerate(operands)
        )
    )


def per_device(raster, transmission, kernels, kernel_weight, library, clip_tile, clip_corner):
    tile = raster.shape[0]
    border = KSIZE // 2
    full = tile + KSIZE
    half = full // 2
    wide = 2 * ceil_to(half, LANES)
    table = {
        key: jnp.stack([jnp.asarray(part) for part in value])
        if isinstance(value, tuple)
        else jnp.asarray(value)
        for key, value in tables(tile).items()
    }
    cols_wide = lax.axis_size("wide")
    rows_narrow = lax.axis_size("narrow")
    device_count = cols_wide * rows_narrow
    both = ("wide", "narrow")
    clip_count = clip_tile.shape[0]
    real_count = 2 * kernels.shape[0]

    mask, sent = call(
        lambda *refs: edges_body(cols_wide, rows_narrow, *refs),
        (
            jax.ShapeDtypeStruct((tile, tile), bf16),
            pltpu.HBM((device_count, border, tile), bf16),
        ),
        (raster, transmission),
        scratch=(
            pltpu.VMEM((tile, tile), jnp.int32),
            pltpu.VMEM((tile, tile), bf16),
            pltpu.VMEM((4, border, tile), bf16),
            pltpu.SemaphoreType.DMA((2,)),
            pltpu.SemaphoreType.DMA((8,)),
        ),
        out=(VMEM_SPEC, pl.BlockSpec(memory_space=pltpu.HBM)),
        hbm=(0, 1),
        name="edges",
    )
    got = lax.all_to_all(sent, both, 0, 0, tiled=True)

    tile_line = clip_tile.reshape(1, clip_count)
    spectrum = (2, half, wide)
    basis = jax.ShapeDtypeStruct((2, CAP * KSIG, tile), bf16)
    filters, row_basis, col_basis = call(
        lambda *refs: filters_body(cols_wide, *refs),
        (pltpu.HBM((real_count,) + spectrum, f32), basis, basis),
        (
            kernel_weight,
            kernels.reshape(real_count, KSIZE, KSIZE),
            table["taps_rows"],
            table["taps_cols"],
            tile_line,
            clip_corner,
        ),
        scratch=(
            pltpu.VMEM((real_count,) + spectrum, f32),
            pltpu.VMEM((2, full, 6 * KSIZE), bf16),
            pltpu.VMEM((real_count, KSIZE, KSIZE), f32),
            pltpu.VMEM(table["taps_rows"].shape, bf16),
            pltpu.VMEM(table["taps_cols"].shape, bf16),
            pltpu.VMEM((1, clip_count), jnp.int32),
            pltpu.VMEM((2, clip_count), jnp.int32),
            pltpu.SemaphoreType.DMA((5,)),
            pltpu.SemaphoreType.DMA((real_count,)),
        ),
        smem=(0,),
        hbm=(1, 2, 3, 4, 5),
        out=(pl.BlockSpec(memory_space=pltpu.HBM), VMEM_SPEC, VMEM_SPEC),
        flops=4 << 30,
        name="filters",
    )
    lib_units = call(
        library_body,
        jax.ShapeDtypeStruct(library.shape, bf16),
        (library,),
        flops=1 << 30,
        name="library",
    )
    filters, lib_units = lax.optimization_barrier((filters, lib_units))
    aerial, copies = call(
        lambda *refs: image_body(cols_wide, rows_narrow, *refs),
        (
            jax.ShapeDtypeStruct((tile, tile), f32),
            jax.ShapeDtypeStruct((device_count, CAP, SIGD), bf16),
        ),
        (
            mask,
            got,
            filters,
            row_basis,
            col_basis,
            table["rows_in"],
            table["cols_in"],
            table["cols_out"],
            table["rows_out"],
        ),
        scratch=(
            pltpu.VMEM((wide, wide), bf16),
            pltpu.VMEM(spectrum, f32),
            pltpu.VMEM((2, 3, GROUP * 2 * full, wide), bf16),
            pltpu.VMEM((2, GROUP, 2, wide, wide), bf16),
            pltpu.VMEM((tile, tile), f32),
            pltpu.VMEM((real_count,) + spectrum, f32),
            pltpu.SemaphoreType.DMA((2,)),
        ),
        hbm=(2,),
        flops=6 << 30,
        name="image",
    )
    gathered = lax.all_to_all(copies, both, 0, 0, tiled=True).reshape(device_count * CAP, SIGD)
    slab = call(
        lambda *refs: match_body(cols_wide, rows_narrow, *refs),
        jax.ShapeDtypeStruct((device_count, LANES), f32),
        (tile_line, gathered, lib_units),
        limit=40,
        flops=1 << 30,
        name="match",
    )
    slab = lax.all_to_all(slab, both, 0, 0, tiled=True)[:, : clip_count // device_count]
    peak = jnp.max(slab, axis=0)
    total = jnp.sum(jnp.exp(slab - peak[None, :]), axis=0)
    scores = -(peak + jnp.log(total)) / sharpness
    return (aerial, scores)


def solution(mesh):
    placed = (
        P("narrow", "wide"),
        P("narrow", "wide"),
        P(),
        P(),
        P(("wide", "narrow"), None),
        P(),
        P(),
    )
    return jax.shard_map(
        per_device,
        mesh=mesh,
        in_specs=placed,
        out_specs=(P("narrow", "wide"), P(("wide", "narrow"))),
        check_vma=False,
    )
```

```python
import math

import jax
import jax.numpy as jnp
import numpy as np
from jax import lax
from jax.experimental import pallas as pl
from jax.experimental.pallas import tpu as pltpu
from jax.sharding import PartitionSpec as P

KSIZE = 64
CLIP = 64
KSIG = 16
CAP = 16
SIGD = KSIG * KSIG
LANES = 128
GROUP = 2

sharpness = 400.0
f32 = jnp.float32
bf16 = jnp.bfloat16
VMEM_SPEC = pl.BlockSpec(memory_space=pltpu.VMEM)


def ceil_to(value, step):
    return -(-value // step) * step


def thirds(table):
    high, rest = table.astype(bf16), table - table.astype(bf16).astype(np.float64)
    middle = rest.astype(bf16)
    return high, middle, (rest - middle.astype(np.float64)).astype(bf16)


def tables(tile):
    full = tile + KSIZE
    half = full // 2
    lanes = ceil_to(half, LANES)
    wide = 2 * lanes
    unit = 2.0 * math.pi / full
    place = np.arange(full)
    place = np.where(place < tile + KSIZE // 2, place, place - full)
    taps = np.arange(KSIZE) - KSIZE // 2
    odd = np.arange(half) + 0.5
    extra = (lanes - half) // 2
    again = np.concatenate([odd, odd[:extra], odd[:extra]])

    def padded(table, rows, cols):
        out = np.zeros((rows, cols))
        out[: table.shape[0], : table.shape[1]] = table
        return out

    def side_by_side(angle, rows):
        return np.concatenate(
            [padded(np.cos(angle), rows, lanes), padded(np.sin(angle), rows, lanes)], axis=1
        )

    angle = unit * odd[:, None] * place[None, :]
    rows_in = padded(np.concatenate([np.cos(angle), -np.sin(angle)]), full, wide)
    cols_in = side_by_side(unit * place[:, None] * again[None, :], wide)
    angle = unit * odd[:, None] * np.arange(tile)[None, :]
    cols_out = []
    for part in (np.cos(angle), np.sin(angle)):
        high, middle, low = thirds(part)
        empty = np.zeros_like(low[:extra])
        cols_out.append(np.concatenate([high, middle], axis=1))
        cols_out.append(np.concatenate([low[:extra], empty], axis=1))
        cols_out.append(np.concatenate([high[:extra], middle[:extra]], axis=1))
    cols_out = np.concatenate(cols_out)
    angle = unit * np.arange(tile)[:, None] * odd[None, :]
    pieces = [thirds(np.cos(angle)), thirds(-np.sin(angle))]
    firsts = [piece[0] for piece in pieces]
    lows = [piece[2][:, :extra] for piece in pieces]
    heads = [piece[0][:, :extra] for piece in pieces]
    seconds = [piece[1] for piece in pieces]
    empty = np.zeros((tile, wide - full), bf16)
    rows_out = (
        np.concatenate(firsts + lows + heads, axis=1),
        np.concatenate(seconds + [empty], axis=1),
    )
    angle = unit * odd[:, None] * taps[None, :]
    taps_rows = np.concatenate([np.cos(angle), np.sin(angle)]) * (2.0 / (full * full))
    taps_cols = side_by_side(unit * taps[:, None] * again[None, :], KSIZE)
    high, middle, low = thirds(taps_rows)
    taps_rows = np.concatenate([high, middle, low, high, middle, high], axis=1)
    high, middle, low = thirds(taps_cols)
    taps_cols = np.concatenate([high, middle, low, high, middle, high], axis=0)
    return {
        "rows_in": thirds(rows_in),
        "cols_in": thirds(cols_in),
        "cols_out": cols_out,
        "rows_out": rows_out,
        "taps_rows": taps_rows,
        "taps_cols": taps_cols,
    }


def dot(left, right):
    return jnp.dot(left, right, preferred_element_type=f32)


def split(value):
    high = value.astype(bf16)
    return high, (value - high.astype(f32)).astype(bf16)


def split3(value):
    high = value.astype(bf16)
    middle, low = split(value - high.astype(f32))
    return high, middle, low


def dot3(left, right):
    return dot(left[0], right[0]) + dot(left[1], right[0]) + dot(left[0], right[1])


def dot3_t(left, right):
    def single(a, b):
        return lax.dot_general(a, b, (((1,), (1,)), ((), ())), preferred_element_type=f32)

    return single(left[0], right[0]) + single(left[1], right[0]) + single(left[0], right[1])


def iota(shape, dim):
    return lax.broadcasted_iota(jnp.int32, shape, dim)


def shifted_basis(corner, tile):
    shape = (CAP * KSIG, tile)
    freq = iota(shape, 0) & (KSIG - 1)
    offset = iota(shape, 1) - corner
    turn = ((2 * offset + 1) * freq) & (4 * CLIP - 1)
    fold = jnp.abs(turn.astype(f32) * (1.0 / (2 * CLIP)) - 1.0) - 0.5
    x = fold * math.pi
    square = x * x
    series = jnp.full(shape, -1.0 / math.factorial(15), f32)
    for order in (13, 11, 9, 7, 5, 3, 1):
        sign = 1.0 if order % 4 == 1 else -1.0
        series = series * square + sign / math.factorial(order)
    weight = jnp.where(freq == 0, math.sqrt(1.0 / CLIP), math.sqrt(2.0 / CLIP))
    inside = (offset >= 0) & (offset < CLIP)
    return jnp.where(inside, weight * (series * x), 0.0)


def neighbours():
    return [(dw, dz) for dw in (-1, 0, 1) for dz in (-1, 0, 1) if dw or dz]


def fetched(pairs, sems):
    copies = [
        pltpu.make_async_copy(source, target, sems.at[index])
        for index, (source, target) in enumerate(pairs)
    ]
    for copy in copies:
        copy.start()
    return copies


def edges_body(
    cols_wide,
    rows_narrow,
    raster_hbm,
    light_hbm,
    mask_ref,
    sent_hbm,
    raster_ref,
    light_ref,
    strip_ref,
    sems,
    sent_sems,
):
    tile = mask_ref.shape[0]
    border = sent_hbm.shape[1]
    copies = fetched(((raster_hbm, raster_ref), (light_hbm, light_ref)), sems)
    for copy in copies:
        copy.wait()
    mask = raster_ref[...].astype(f32) * light_ref[...].astype(f32)
    mask_ref[...] = mask.astype(bf16)
    lane = iota((border, tile), 1)

    def folded(first):
        out = jnp.zeros((border, tile), f32)
        for block in range(tile // border):
            low = block * border
            moved = pltpu.roll(mask[low : low + border], (low - first) % tile, 1)
            out = jnp.where((lane >= low) & (lane < low + border), moved, out)
        return out.astype(bf16)

    strip_ref[0] = mask[:border].astype(bf16)
    strip_ref[1] = mask[tile - border :].astype(bf16)
    strip_ref[2] = folded(0)
    strip_ref[3] = folded(tile - border)
    col = lax.axis_index("wide")
    row = lax.axis_index("narrow")
    sends = []
    for index, (dw, dz) in enumerate(neighbours()):
        strip = 0 if dz < 0 else 1 if dz > 0 else 2 if dw < 0 else 3
        there = (col + dw >= 0) & (col + dw < cols_wide)
        there &= (row + dz >= 0) & (row + dz < rows_narrow)
        place = jnp.where(there, (col + dw) * rows_narrow + row + dz, 0)
        copy = pltpu.make_async_copy(
            strip_ref.at[strip], sent_hbm.at[place], sent_sems.at[index]
        )
        sends.append((there, copy))
    for there, copy in sends:
        pl.when(there)(copy.start)
    for there, copy in sends:
        pl.when(there)(copy.wait)


def transform_taps(weight_ref, taps_ref, rows_ref, cols_ref, out_ref, mixed_ref, finished):
    count = out_ref.shape[0]
    half = out_ref.shape[2]
    lanes = out_ref.shape[3] // 2

    def along_rows(index):
        taps = taps_ref[index]
        taps = taps * jnp.sqrt(jnp.full(taps.shape, weight_ref[index // 2], f32))
        high, middle, low = split3(jnp.concatenate([taps, taps], axis=1))
        stacked = jnp.concatenate([high, high, high, middle, middle, low], axis=0)
        rows = dot(rows_ref[...], stacked)
        high, middle, low = split3(rows)
        first = iota(rows.shape, 1) < KSIZE
        pairs = ((high, high), (high, middle), (middle, low))
        for place, (left, right) in enumerate(pairs):
            value = jnp.where(first, left.astype(f32), right.astype(f32)).astype(bf16)
            mixed_ref[index % 2, :, place * 2 * KSIZE : (place + 1) * 2 * KSIZE] = value

    def along_cols(index):
        both = dot(mixed_ref[index % 2], cols_ref[...])
        out_ref[index, 0, :, :lanes] = both[:half, :lanes] - both[half:, lanes:]
        out_ref[index, 0, :, lanes:] = both[:half, :lanes] + both[half:, lanes:]
        out_ref[index, 1, :, :lanes] = both[half:, :lanes] + both[:half, lanes:]
        out_ref[index, 1, :, lanes:] = both[half:, :lanes] - both[:half, lanes:]
        finished[index].start()

    along_rows(0)
    for index in range(count):
        if index + 1 < count:
            along_rows(index + 1)
        along_cols(index)


def filters_body(
    cols_wide,
    weight_ref,
    taps_hbm,
    rows_hbm,
    cols_hbm,
    tile_hbm,
    corner_hbm,
    library_hbm,
    out_hbm,
    rb_ref,
    cb_ref,
    units_ref,
    out_ref,
    mixed_ref,
    taps_ref,
    rows_ref,
    cols_ref,
    tile_ref,
    corner_ref,
    library_ref,
    sems,
    out_sems,
    library_sem,
):
    pairs = (
        (taps_hbm, taps_ref),
        (rows_hbm, rows_ref),
        (cols_hbm, cols_ref),
        (tile_hbm, tile_ref),
        (corner_hbm, corner_ref),
    )
    needed = fetched(pairs, sems)
    library = pltpu.make_async_copy(library_hbm, library_ref, library_sem)
    library.start()
    for copy in needed:
        copy.wait()
    finished = [
        pltpu.make_async_copy(out_ref.at[index], out_hbm.at[index], out_sems.at[index])
        for index in range(out_ref.shape[0])
    ]
    transform_taps(weight_ref, taps_ref, rows_ref, cols_ref, out_ref, mixed_ref, finished)
    clip_count = tile_ref.shape[1]
    own_tile = lax.axis_index("narrow") * cols_wide + lax.axis_index("wide")
    owned = tile_ref[...] == own_tile
    owned8 = jnp.broadcast_to(owned.astype(f32), (8, clip_count))
    square = (clip_count, clip_count)
    earlier = (iota(square, 0) < iota(square, 1)).astype(f32).astype(bf16)
    rank = dot(owned8.astype(bf16), earlier)[:1]
    rank = jnp.where(owned, rank, -1.0)
    slot = (iota((CAP * KSIG, clip_count), 0) // KSIG).astype(f32)
    select = (slot == rank).astype(f32).astype(bf16)
    tile = rb_ref.shape[2]
    for axis, basis_ref in ((0, rb_ref), (1, cb_ref)):
        line = corner_ref[axis : axis + 1, :].astype(f32).astype(bf16)
        table = jnp.broadcast_to(line, (tile, clip_count))
        corner = lax.dot_general(
            select, table, (((1,), (1,)), ((), ())), preferred_element_type=f32
        )
        high, low = split(shifted_basis(corner.astype(jnp.int32), tile))
        basis_ref[0] = high
        basis_ref[1] = low
    library.wait()
    rows = library_ref[...].astype(f32)
    mean_square = jnp.mean(rows * rows, axis=1, keepdims=True)
    units_ref[...] = (rows * (1.0 / (KSIG * jnp.sqrt(mean_square + 1e-06)))).astype(bf16)
    for copy in finished:
        copy.wait()


def image_body(
    cols_wide,
    rows_narrow,
    own_ref,
    got_ref,
    filter_hbm,
    rb_ref,
    cb_ref,
    rows_in_ref,
    cols_in_ref,
    cols_out_ref,
    rows_out_ref,
    aerial_ref,
    units_ref,
    mask_ref,
    spec_ref,
    prod_ref,
    mid_ref,
    sum_ref,
    filter_ref,
    sems,
):
    tile = own_ref.shape[0]
    half = filter_ref.shape[2]
    full = 2 * half
    wide = filter_ref.shape[3]
    border = KSIZE // 2
    kernel_count = filter_ref.shape[0] // 2
    group = prod_ref.shape[2] // (2 * full)

    def arriving(index):
        part = pl.ds(index * kernel_count, kernel_count)
        return pltpu.make_async_copy(filter_hbm.at[part], filter_ref.at[part], sems.at[index])

    def request(index, carry):
        arriving(index).start()
        return carry

    lax.fori_loop(0, 2, request, 0)
    col = lax.axis_index("wide")
    row = lax.axis_index("narrow")
    lane = iota((border, tile), 1)

    def from_neighbour(dw, dz):
        there = (col + dw >= 0) & (col + dw < cols_wide)
        there &= (row + dz >= 0) & (row + dz < rows_narrow)
        place = jnp.where(there, (col + dw) * rows_narrow + row + dz, 0)
        return jnp.where(there, got_ref[place].astype(f32), 0.0)

    def beside(right, right_shift, left, left_shift):
        right = pltpu.roll(right, right_shift % tile, 1)
        left = pltpu.roll(left, left_shift % tile, 1)
        return jnp.where(lane < border, right, jnp.where(lane < 2 * border, left, 0.0)).astype(bf16)

    mask_ref[:tile, :tile] = own_ref[...]
    right = from_neighbour(1, 0)
    left = from_neighbour(-1, 0)
    for low in range(0, tile, border):
        mask_ref[low : low + border, tile:] = beside(right, -low, left, border - low)
    for low, dz in ((tile, 1), (tile + border, -1)):
        mask_ref[low : low + border, :tile] = from_neighbour(0, dz).astype(bf16)
        mask_ref[low : low + border, tile:] = beside(
            from_neighbour(1, dz), 0, from_neighbour(-1, dz), 2 * border
        )
    mask_ref[full:, :] = jnp.zeros((wide - full, wide), bf16)
    for place in range(2):
        for member in range(mid_ref.shape[1]):
            mid_ref[place, member, 1, full:, :] = jnp.zeros((wide - full, wide), bf16)
    mask = mask_ref[...]
    rows = (dot(rows_in_ref[2], mask) + dot(rows_in_ref[1], mask)) + dot(rows_in_ref[0], mask)
    high, middle, low = split3(rows)
    both = dot(low, cols_in_ref[0]) + dot(high, cols_in_ref[2]) + dot(middle, cols_in_ref[1])
    both = (both + dot(middle, cols_in_ref[0]) + dot(high, cols_in_ref[1])) + dot(high, cols_in_ref[0])
    lanes = wide // 2
    spec_ref[0, :, :lanes] = both[:half, :lanes] + both[half:, lanes:]
    spec_ref[0, :, lanes:] = both[:half, :lanes] - both[half:, lanes:]
    spec_ref[1, :, :lanes] = both[half:, :lanes] - both[:half, lanes:]
    spec_ref[1, :, lanes:] = both[half:, :lanes] + both[:half, lanes:]

    extra = (lanes - half) // 2
    column = iota((half, lanes), 1)

    def multiply(index):
        place = prod_ref.at[index % 2]
        for part in range(2 * group):
            ref = filter_ref.at[2 * group * index + part]
            base = part * full
            real = spec_ref[0] * ref[0] - spec_ref[1] * ref[1]
            imag = spec_ref[0] * ref[1] + spec_ref[1] * ref[0]
            pieces = (
                (0, 0, real[:, :lanes] + real[:, lanes:]),
                (0, lanes, imag[:, lanes:] - imag[:, :lanes]),
                (half, 0, imag[:, :lanes] + imag[:, lanes:]),
                (half, lanes, real[:, :lanes] - real[:, lanes:]),
            )
            for down, lane, piece in pieces:
                high, middle, low = split3(piece)
                value = jnp.where(column < half + extra, high.astype(f32), low.astype(f32))
                place[0, base + down : base + down + half, lane : lane + lanes] = value.astype(bf16)
                value = jnp.where(column < half, middle.astype(f32), 0.0)
                place[1, base + down : base + down + half, lane : lane + lanes] = value.astype(bf16)

    def along_cols(index):
        source = prod_ref.at[index % 2]
        table = cols_out_ref[...]
        cols = dot(source[1], table) + dot(source[0], table)
        for part in range(2 * group):
            place = mid_ref.at[index % 2, part // 2]
            base = part * full
            lane = part % 2 * tile
            value = cols[base : base + full, tile:] + cols[base : base + full, :tile]
            high, low = split(value)
            place[0, :full, lane : lane + tile] = high
            place[1, :full, lane : lane + tile] = low
            for order, first in enumerate((0, half)):
                slow = slice(first, first + extra)
                down = full + order * extra
                place[0, down : down + extra, lane : lane + tile] = high[slow]
                rest = split3(value[slow])[2]
                down += 2 * extra
                place[0, down : down + extra, lane : lane + tile] = rest

    def along_rows(index):
        value = None
        for member in range(group):
            source = mid_ref.at[index % 2, member]
            field = dot3((rows_out_ref[0], rows_out_ref[1]), (source[0], source[1]))
            energy = field * field
            term = energy[:, :tile] + energy[:, tile:]
            value = term if value is None else value + term
        if index == 0:
            sum_ref[...] = value
        elif index == kernel_count // group - 1:
            aerial_ref[...] = sum_ref[...] + value
        else:
            sum_ref[...] += value

    for step in range(kernel_count // group + 2):
        if step % (kernel_count // (2 * group)) == 0 and step < kernel_count // group:
            arriving(step // (kernel_count // (2 * group))).wait()
        if step < kernel_count // group:
            multiply(step)
        if 0 <= step - 1 < kernel_count // group:
            along_cols(step - 1)
        if 0 <= step - 2:
            along_rows(step - 2)

    halfway = dot3((rb_ref[0], rb_ref[1]), split(aerial_ref[...]))
    crossed = dot3_t(split(halfway), (cb_ref[0], cb_ref[1]))
    shape = (CAP * KSIG, CAP * KSIG)
    crossed = jnp.where(iota(shape, 0) // KSIG == iota(shape, 1) // KSIG, crossed, 0.0)
    fold = ((iota(shape, 0) & (KSIG - 1)) == (iota(shape, 1) & (KSIG - 1))).astype(f32).astype(bf16)
    high = crossed.astype(bf16)
    middle, low = split(crossed - high.astype(f32))
    spread = (dot(low, fold) + dot(middle, fold)) + dot(high, fold)
    spread = jnp.where((iota(shape, 0) & (KSIG - 1)) == iota(shape, 1) // KSIG, spread, 0.0)
    signature = jnp.sum(spread.reshape(CAP, KSIG, SIGD), axis=1)
    signature = jnp.where(iota(signature.shape, 1) == 0, 0.0, signature)
    mean_square = jnp.mean(signature * signature, axis=1, keepdims=True)
    units = (signature / (KSIG * jnp.sqrt(mean_square + 1e-06))).astype(bf16)
    units_ref[...] = jnp.broadcast_to(units[None], units_ref.shape)


def match_body(cols_wide, rows_narrow, tile_ref, gathered_ref, library_ref, out_ref):
    clip_count = tile_ref.shape[1]
    slot_count = gathered_ref.shape[0]
    device_count = out_ref.shape[0]
    own_count = clip_count // device_count
    row = tile_ref[...].astype(f32)
    peaks = []
    for first in range(0, clip_count, LANES):
        shape = (LANES, clip_count)
        clip = iota(shape, 0) + first
        other = iota(shape, 1)
        spread = jnp.broadcast_to(row, shape)
        column = jnp.sum(jnp.where(clip == other, spread, 0.0), axis=1, keepdims=True)
        before = (spread == column) & (other < clip)
        rank = jnp.sum(before.astype(f32), axis=1, keepdims=True)
        grid_row = jnp.floor((column + 0.5) * (1.0 / cols_wide))
        holder = (column - grid_row * cols_wide) * rows_narrow + grid_row
        place = (holder * CAP + rank).astype(jnp.int32)
        pick = (iota((LANES, slot_count), 1) == place).astype(f32).astype(bf16)
        units = dot(pick, gathered_ref[...]).astype(bf16)
        cosine = lax.dot_general(
            library_ref[...], units, (((1,), (1,)), ((), ())), preferred_element_type=f32
        )
        logits = sharpness * (cosine - 1.0)
        peak = jnp.max(logits, axis=0, keepdims=True)
        total = jnp.sum(jnp.exp(logits - peak), axis=0, keepdims=True)
        peaks.append(peak + jnp.log(total))
    slab = peaks[0] if len(peaks) == 1 else jnp.concatenate(peaks, axis=1)
    shape = (device_count, clip_count)
    spread = jnp.broadcast_to(slab, shape)
    lane = iota((device_count, LANES), 1)
    sent = jnp.zeros((device_count, LANES), f32)
    for index in range(own_count):
        mine = iota(shape, 1) == iota(shape, 0) * own_count + index
        value = jnp.sum(jnp.where(mine, spread, 0.0), axis=1, keepdims=True)
        sent = jnp.where(lane == index, value, sent)
    out_ref[...] = sent


def call(
    body, out_shape, operands, scratch=(), limit=24, smem=(), hbm=(), out=None, flops=0, name=None
):
    spaces = [
        pltpu.SMEM if index in smem else pltpu.HBM if index in hbm else pltpu.VMEM
        for index in range(len(operands))
    ]
    return pl.pallas_call(
        body,
        out_shape=out_shape,
        in_specs=[pl.BlockSpec(memory_space=space) for space in spaces],
        out_specs=jax.tree.map(lambda _: VMEM_SPEC, out_shape) if out is None else out,
        scratch_shapes=list(scratch),
        compiler_params=pltpu.CompilerParams(vmem_limit_bytes=limit << 20),
        cost_estimate=pl.CostEstimate(flops=flops, bytes_accessed=1 << 20, transcendentals=0),
        name=name,
    )(
        *(
            pltpu.with_memory_space_constraint(value, pltpu.HBM) if index in hbm else value
            for index, value in enumerate(operands)
        )
    )


def per_device(raster, transmission, kernels, kernel_weight, library, clip_tile, clip_corner):
    tile = raster.shape[0]
    border = KSIZE // 2
    full = tile + KSIZE
    half = full // 2
    wide = 2 * ceil_to(half, LANES)
    table = {
        key: jnp.stack([jnp.asarray(part) for part in value])
        if isinstance(value, tuple)
        else jnp.asarray(value)
        for key, value in tables(tile).items()
    }
    cols_wide = lax.axis_size("wide")
    rows_narrow = lax.axis_size("narrow")
    device_count = cols_wide * rows_narrow
    both = ("wide", "narrow")
    clip_count = clip_tile.shape[0]
    real_count = 2 * kernels.shape[0]

    mask, sent = call(
        lambda *refs: edges_body(cols_wide, rows_narrow, *refs),
        (
            jax.ShapeDtypeStruct((tile, tile), bf16),
            pltpu.HBM((device_count, border, tile), bf16),
        ),
        (raster, transmission),
        scratch=(
            pltpu.VMEM((tile, tile), jnp.int32),
            pltpu.VMEM((tile, tile), bf16),
            pltpu.VMEM((4, border, tile), bf16),
            pltpu.SemaphoreType.DMA((2,)),
            pltpu.SemaphoreType.DMA((8,)),
        ),
        out=(VMEM_SPEC, pl.BlockSpec(memory_space=pltpu.HBM)),
        hbm=(0, 1),
        name="edges",
    )
    got = lax.all_to_all(sent, both, 0, 0, tiled=True)

    tile_line = clip_tile.reshape(1, clip_count)
    spectrum = (2, half, wide)
    basis = jax.ShapeDtypeStruct((2, CAP * KSIG, tile), bf16)
    filters, row_basis, col_basis, lib_units = call(
        lambda *refs: filters_body(cols_wide, *refs),
        (
            pltpu.HBM((real_count,) + spectrum, f32),
            basis,
            basis,
            jax.ShapeDtypeStruct(library.shape, bf16),
        ),
        (
            kernel_weight,
            kernels.reshape(real_count, KSIZE, KSIZE),
            table["taps_rows"],
            table["taps_cols"],
            tile_line,
            clip_corner,
            library,
        ),
        scratch=(
            pltpu.VMEM((real_count,) + spectrum, f32),
            pltpu.VMEM((2, full, 6 * KSIZE), bf16),
            pltpu.VMEM((real_count, KSIZE, KSIZE), f32),
            pltpu.VMEM(table["taps_rows"].shape, bf16),
            pltpu.VMEM(table["taps_cols"].shape, bf16),
            pltpu.VMEM((1, clip_count), jnp.int32),
            pltpu.VMEM((2, clip_count), jnp.int32),
            pltpu.VMEM(library.shape, bf16),
            pltpu.SemaphoreType.DMA((5,)),
            pltpu.SemaphoreType.DMA((real_count,)),
            pltpu.SemaphoreType.DMA(()),
        ),
        smem=(0,),
        hbm=(1, 2, 3, 4, 5, 6),
        out=(pl.BlockSpec(memory_space=pltpu.HBM), VMEM_SPEC, VMEM_SPEC, VMEM_SPEC),
        flops=4 << 30,
        name="filters",
    )
    aerial, copies = call(
        lambda *refs: image_body(cols_wide, rows_narrow, *refs),
        (
            jax.ShapeDtypeStruct((tile, tile), f32),
            jax.ShapeDtypeStruct((device_count, CAP, SIGD), bf16),
        ),
        (
            mask,
            got,
            filters,
            row_basis,
            col_basis,
            table["rows_in"],
            table["cols_in"],
            table["cols_out"],
            table["rows_out"],
        ),
        scratch=(
            pltpu.VMEM((wide, wide), bf16),
            pltpu.VMEM(spectrum, f32),
            pltpu.VMEM((2, 2, GROUP * 2 * full, wide), bf16),
            pltpu.VMEM((2, GROUP, 2, wide, wide), bf16),
            pltpu.VMEM((tile, tile), f32),
            pltpu.VMEM((real_count,) + spectrum, f32),
            pltpu.SemaphoreType.DMA((2,)),
        ),
        hbm=(2,),
        flops=6 << 30,
        name="image",
    )
    gathered = lax.all_to_all(copies, both, 0, 0, tiled=True).reshape(device_count * CAP, SIGD)
    slab = call(
        lambda *refs: match_body(cols_wide, rows_narrow, *refs),
        jax.ShapeDtypeStruct((device_count, LANES), f32),
        (tile_line, gathered, lib_units),
        limit=40,
        flops=1 << 30,
        name="match",
    )
    slab = lax.all_to_all(slab, both, 0, 0, tiled=True)[:, : clip_count // device_count]
    peak = jnp.max(slab, axis=0)
    total = jnp.sum(jnp.exp(slab - peak[None, :]), axis=0)
    scores = -(peak + jnp.log(total)) / sharpness
    return (aerial, scores)


def solution(mesh):
    placed = (
        P("narrow", "wide"),
        P("narrow", "wide"),
        P(),
        P(),
        P(("wide", "narrow"), None),
        P(),
        P(),
    )
    return jax.shard_map(
        per_device,
        mesh=mesh,
        in_specs=placed,
        out_specs=(P("narrow", "wide"), P(("wide", "narrow"))),
        check_vma=False,
    )
```

```python
import math

import jax
import jax.numpy as jnp
import numpy as np
from jax import lax
from jax.experimental import pallas as pl
from jax.experimental.pallas import tpu as pltpu
from jax.sharding import PartitionSpec as P

KSIZE = 64
CLIP = 64
KSIG = 16
CAP = 16
SIGD = KSIG * KSIG
LANES = 128
GROUP = 4

sharpness = 400.0
f32 = jnp.float32
bf16 = jnp.bfloat16
VMEM_SPEC = pl.BlockSpec(memory_space=pltpu.VMEM)


def ceil_to(value, step):
    return -(-value // step) * step


def thirds(table):
    high, rest = table.astype(bf16), table - table.astype(bf16).astype(np.float64)
    middle = rest.astype(bf16)
    return high, middle, (rest - middle.astype(np.float64)).astype(bf16)


def tables(tile):
    full = tile + KSIZE
    half = full // 2
    lanes = ceil_to(half, LANES)
    wide = 2 * lanes
    unit = 2.0 * math.pi / full
    place = np.arange(full)
    place = np.where(place < tile + KSIZE // 2, place, place - full)
    taps = np.arange(KSIZE) - KSIZE // 2
    odd = np.arange(half) + 0.5
    extra = (lanes - half) // 2
    again = np.concatenate([odd, odd[:extra], odd[:extra]])

    def padded(table, rows, cols):
        out = np.zeros((rows, cols))
        out[: table.shape[0], : table.shape[1]] = table
        return out

    def side_by_side(angle, rows):
        return np.concatenate(
            [padded(np.cos(angle), rows, lanes), padded(np.sin(angle), rows, lanes)], axis=1
        )

    angle = unit * odd[:, None] * place[None, :]
    rows_in = padded(np.concatenate([np.cos(angle), -np.sin(angle)]), full, wide)
    cols_in = side_by_side(unit * place[:, None] * again[None, :], wide)
    angle = unit * odd[:, None] * np.arange(tile)[None, :]
    cols_out = []
    for part in (np.cos(angle), np.sin(angle)):
        high, middle, low = thirds(part)
        empty = np.zeros_like(low[:extra])
        cols_out.append(np.concatenate([high, middle], axis=1))
        cols_out.append(np.concatenate([low[:extra], empty], axis=1))
        cols_out.append(np.concatenate([high[:extra], middle[:extra]], axis=1))
    cols_out = np.concatenate(cols_out)
    angle = unit * np.arange(tile)[:, None] * odd[None, :]
    pieces = [thirds(np.cos(angle)), thirds(-np.sin(angle))]
    firsts = [piece[0] for piece in pieces]
    lows = [piece[2][:, :extra] for piece in pieces]
    heads = [piece[0][:, :extra] for piece in pieces]
    seconds = [piece[1] for piece in pieces]
    empty = np.zeros((tile, wide - full), bf16)
    rows_out = (
        np.concatenate(firsts + lows + heads, axis=1),
        np.concatenate(seconds + [empty], axis=1),
    )
    angle = unit * odd[:, None] * taps[None, :]
    taps_rows = np.concatenate([np.cos(angle), np.sin(angle)]) * (2.0 / (full * full))
    taps_cols = side_by_side(unit * taps[:, None] * again[None, :], KSIZE)
    high, middle, low = thirds(taps_rows)
    taps_rows = np.concatenate([high, middle, low, high, middle, high], axis=1)
    high, middle, low = thirds(taps_cols)
    taps_cols = np.concatenate([high, middle, low, high, middle, high], axis=0)
    return {
        "rows_in": thirds(rows_in),
        "cols_in": thirds(cols_in),
        "cols_out": cols_out,
        "rows_out": rows_out,
        "taps_rows": taps_rows,
        "taps_cols": taps_cols,
    }


def dot(left, right):
    return jnp.dot(left, right, preferred_element_type=f32)


def split(value):
    high = value.astype(bf16)
    return high, (value - high.astype(f32)).astype(bf16)


def split3(value):
    high = value.astype(bf16)
    middle, low = split(value - high.astype(f32))
    return high, middle, low


def dot3(left, right):
    return dot(left[0], right[0]) + dot(left[1], right[0]) + dot(left[0], right[1])


def dot3_t(left, right):
    def single(a, b):
        return lax.dot_general(a, b, (((1,), (1,)), ((), ())), preferred_element_type=f32)

    return single(left[0], right[0]) + single(left[1], right[0]) + single(left[0], right[1])


def iota(shape, dim):
    return lax.broadcasted_iota(jnp.int32, shape, dim)


def shifted_basis(corner, tile):
    shape = (CAP * KSIG, tile)
    freq = iota(shape, 0) & (KSIG - 1)
    offset = iota(shape, 1) - corner
    turn = ((2 * offset + 1) * freq) & (4 * CLIP - 1)
    fold = jnp.abs(turn.astype(f32) * (1.0 / (2 * CLIP)) - 1.0) - 0.5
    x = fold * math.pi
    square = x * x
    series = jnp.full(shape, -1.0 / math.factorial(15), f32)
    for order in (13, 11, 9, 7, 5, 3, 1):
        sign = 1.0 if order % 4 == 1 else -1.0
        series = series * square + sign / math.factorial(order)
    weight = jnp.where(freq == 0, math.sqrt(1.0 / CLIP), math.sqrt(2.0 / CLIP))
    inside = (offset >= 0) & (offset < CLIP)
    return jnp.where(inside, weight * (series * x), 0.0)


def neighbours():
    return [(dw, dz) for dw in (-1, 0, 1) for dz in (-1, 0, 1) if dw or dz]


def fetched(pairs, sems):
    copies = [
        pltpu.make_async_copy(source, target, sems.at[index])
        for index, (source, target) in enumerate(pairs)
    ]
    for copy in copies:
        copy.start()
    return copies


def edges_body(
    cols_wide,
    rows_narrow,
    raster_hbm,
    light_hbm,
    mask_ref,
    sent_hbm,
    raster_ref,
    light_ref,
    strip_ref,
    sems,
    sent_sems,
):
    tile = mask_ref.shape[0]
    border = sent_hbm.shape[1]
    copies = fetched(((raster_hbm, raster_ref), (light_hbm, light_ref)), sems)
    for copy in copies:
        copy.wait()
    mask = raster_ref[...].astype(f32) * light_ref[...].astype(f32)
    mask_ref[...] = mask.astype(bf16)
    lane = iota((border, tile), 1)

    def folded(first):
        out = jnp.zeros((border, tile), f32)
        for block in range(tile // border):
            low = block * border
            moved = pltpu.roll(mask[low : low + border], (low - first) % tile, 1)
            out = jnp.where((lane >= low) & (lane < low + border), moved, out)
        return out.astype(bf16)

    strip_ref[0] = mask[:border].astype(bf16)
    strip_ref[1] = mask[tile - border :].astype(bf16)
    strip_ref[2] = folded(0)
    strip_ref[3] = folded(tile - border)
    col = lax.axis_index("wide")
    row = lax.axis_index("narrow")
    sends = []
    for index, (dw, dz) in enumerate(neighbours()):
        strip = 0 if dz < 0 else 1 if dz > 0 else 2 if dw < 0 else 3
        there = (col + dw >= 0) & (col + dw < cols_wide)
        there &= (row + dz >= 0) & (row + dz < rows_narrow)
        place = jnp.where(there, (col + dw) * rows_narrow + row + dz, 0)
        copy = pltpu.make_async_copy(
            strip_ref.at[strip], sent_hbm.at[place], sent_sems.at[index]
        )
        sends.append((there, copy))
    for there, copy in sends:
        pl.when(there)(copy.start)
    for there, copy in sends:
        pl.when(there)(copy.wait)


def transform_taps(weight_ref, taps_ref, rows_ref, cols_ref, out_ref, mixed_ref, finished):
    count = out_ref.shape[0]
    half = out_ref.shape[2]
    lanes = out_ref.shape[3] // 2

    def along_rows(index):
        taps = taps_ref[index]
        taps = taps * jnp.sqrt(jnp.full(taps.shape, weight_ref[index // 2], f32))
        high, middle, low = split3(jnp.concatenate([taps, taps], axis=1))
        stacked = jnp.concatenate([high, high, high, middle, middle, low], axis=0)
        rows = dot(rows_ref[...], stacked)
        high, middle, low = split3(rows)
        first = iota(rows.shape, 1) < KSIZE
        pairs = ((high, high), (high, middle), (middle, low))
        for place, (left, right) in enumerate(pairs):
            value = jnp.where(first, left.astype(f32), right.astype(f32)).astype(bf16)
            mixed_ref[index % 2, :, place * 2 * KSIZE : (place + 1) * 2 * KSIZE] = value

    def along_cols(index):
        both = dot(mixed_ref[index % 2], cols_ref[...])
        out_ref[index, 0, :, :lanes] = both[:half, :lanes] - both[half:, lanes:]
        out_ref[index, 0, :, lanes:] = both[:half, :lanes] + both[half:, lanes:]
        out_ref[index, 1, :, :lanes] = both[half:, :lanes] + both[:half, lanes:]
        out_ref[index, 1, :, lanes:] = both[half:, :lanes] - both[:half, lanes:]
        finished[index].start()

    along_rows(0)
    for index in range(count):
        if index + 1 < count:
            along_rows(index + 1)
        along_cols(index)


def filters_body(
    cols_wide,
    weight_ref,
    taps_hbm,
    rows_hbm,
    cols_hbm,
    tile_hbm,
    corner_hbm,
    library_hbm,
    out_hbm,
    rb_ref,
    cb_ref,
    units_ref,
    out_ref,
    mixed_ref,
    taps_ref,
    rows_ref,
    cols_ref,
    tile_ref,
    corner_ref,
    library_ref,
    sems,
    out_sems,
    library_sem,
):
    pairs = (
        (taps_hbm, taps_ref),
        (rows_hbm, rows_ref),
        (cols_hbm, cols_ref),
        (tile_hbm, tile_ref),
        (corner_hbm, corner_ref),
    )
    needed = fetched(pairs, sems)
    library = pltpu.make_async_copy(library_hbm, library_ref, library_sem)
    library.start()
    for copy in needed:
        copy.wait()
    finished = [
        pltpu.make_async_copy(out_ref.at[index], out_hbm.at[index], out_sems.at[index])
        for index in range(out_ref.shape[0])
    ]
    transform_taps(weight_ref, taps_ref, rows_ref, cols_ref, out_ref, mixed_ref, finished)
    clip_count = tile_ref.shape[1]
    own_tile = lax.axis_index("narrow") * cols_wide + lax.axis_index("wide")
    owned = tile_ref[...] == own_tile
    owned8 = jnp.broadcast_to(owned.astype(f32), (8, clip_count))
    square = (clip_count, clip_count)
    earlier = (iota(square, 0) < iota(square, 1)).astype(f32).astype(bf16)
    rank = dot(owned8.astype(bf16), earlier)[:1]
    rank = jnp.where(owned, rank, -1.0)
    slot = (iota((CAP * KSIG, clip_count), 0) // KSIG).astype(f32)
    select = (slot == rank).astype(f32).astype(bf16)
    tile = rb_ref.shape[2]
    for axis, basis_ref in ((0, rb_ref), (1, cb_ref)):
        line = corner_ref[axis : axis + 1, :].astype(f32).astype(bf16)
        table = jnp.broadcast_to(line, (tile, clip_count))
        corner = lax.dot_general(
            select, table, (((1,), (1,)), ((), ())), preferred_element_type=f32
        )
        high, low = split(shifted_basis(corner.astype(jnp.int32), tile))
        basis_ref[0] = high
        basis_ref[1] = low
    library.wait()
    rows = library_ref[...].astype(f32)
    mean_square = jnp.mean(rows * rows, axis=1, keepdims=True)
    units_ref[...] = (rows * (1.0 / (KSIG * jnp.sqrt(mean_square + 1e-06)))).astype(bf16)
    for copy in finished:
        copy.wait()


def image_body(
    cols_wide,
    rows_narrow,
    own_ref,
    got_ref,
    filter_hbm,
    rb_ref,
    cb_ref,
    rows_in_ref,
    cols_in_ref,
    cols_out_ref,
    rows_out_ref,
    aerial_ref,
    units_ref,
    mask_ref,
    spec_ref,
    prod_ref,
    mid_ref,
    sum_ref,
    filter_ref,
    sems,
):
    tile = own_ref.shape[0]
    half = filter_ref.shape[2]
    full = 2 * half
    wide = filter_ref.shape[3]
    border = KSIZE // 2
    kernel_count = filter_ref.shape[0] // 2
    group = prod_ref.shape[2] // (2 * full)

    def arriving(index):
        part = pl.ds(index * kernel_count, kernel_count)
        return pltpu.make_async_copy(filter_hbm.at[part], filter_ref.at[part], sems.at[index])

    def request(index, carry):
        arriving(index).start()
        return carry

    lax.fori_loop(0, 2, request, 0)
    col = lax.axis_index("wide")
    row = lax.axis_index("narrow")
    lane = iota((border, tile), 1)

    def from_neighbour(dw, dz):
        there = (col + dw >= 0) & (col + dw < cols_wide)
        there &= (row + dz >= 0) & (row + dz < rows_narrow)
        place = jnp.where(there, (col + dw) * rows_narrow + row + dz, 0)
        return jnp.where(there, got_ref[place].astype(f32), 0.0)

    def beside(right, right_shift, left, left_shift):
        right = pltpu.roll(right, right_shift % tile, 1)
        left = pltpu.roll(left, left_shift % tile, 1)
        return jnp.where(lane < border, right, jnp.where(lane < 2 * border, left, 0.0)).astype(bf16)

    mask_ref[:tile, :tile] = own_ref[...]
    right = from_neighbour(1, 0)
    left = from_neighbour(-1, 0)
    for low in range(0, tile, border):
        mask_ref[low : low + border, tile:] = beside(right, -low, left, border - low)
    for low, dz in ((tile, 1), (tile + border, -1)):
        mask_ref[low : low + border, :tile] = from_neighbour(0, dz).astype(bf16)
        mask_ref[low : low + border, tile:] = beside(
            from_neighbour(1, dz), 0, from_neighbour(-1, dz), 2 * border
        )
    mask_ref[full:, :] = jnp.zeros((wide - full, wide), bf16)
    for place in range(2):
        for member in range(mid_ref.shape[1]):
            mid_ref[place, member, 1, full:, :] = jnp.zeros((wide - full, wide), bf16)
    mask = mask_ref[...]
    rows = (dot(rows_in_ref[2], mask) + dot(rows_in_ref[1], mask)) + dot(rows_in_ref[0], mask)
    high, middle, low = split3(rows)
    both = dot(low, cols_in_ref[0]) + dot(high, cols_in_ref[2]) + dot(middle, cols_in_ref[1])
    both = (both + dot(middle, cols_in_ref[0]) + dot(high, cols_in_ref[1])) + dot(high, cols_in_ref[0])
    lanes = wide // 2
    spec_ref[0, :, :lanes] = both[:half, :lanes] + both[half:, lanes:]
    spec_ref[0, :, lanes:] = both[:half, :lanes] - both[half:, lanes:]
    spec_ref[1, :, :lanes] = both[half:, :lanes] - both[:half, lanes:]
    spec_ref[1, :, lanes:] = both[half:, :lanes] + both[:half, lanes:]

    extra = (lanes - half) // 2
    column = iota((half, lanes), 1)

    def multiply(index):
        place = prod_ref.at[index % 2]
        for part in range(2 * group):
            ref = filter_ref.at[2 * group * index + part]
            base = part * full
            real = spec_ref[0] * ref[0] - spec_ref[1] * ref[1]
            imag = spec_ref[0] * ref[1] + spec_ref[1] * ref[0]
            pieces = (
                (0, 0, real[:, :lanes] + real[:, lanes:]),
                (0, lanes, imag[:, lanes:] - imag[:, :lanes]),
                (half, 0, imag[:, :lanes] + imag[:, lanes:]),
                (half, lanes, real[:, :lanes] - real[:, lanes:]),
            )
            for down, lane, piece in pieces:
                high, middle, low = split3(piece)
                value = jnp.where(column < half + extra, high.astype(f32), low.astype(f32))
                place[0, base + down : base + down + half, lane : lane + lanes] = value.astype(bf16)
                value = jnp.where(column < half, middle.astype(f32), 0.0)
                place[1, base + down : base + down + half, lane : lane + lanes] = value.astype(bf16)

    def along_cols(index):
        source = prod_ref.at[index % 2]
        table = cols_out_ref[...]
        cols = dot(source[1], table) + dot(source[0], table)
        for part in range(2 * group):
            place = mid_ref.at[index % 2, part // 2]
            base = part * full
            lane = part % 2 * tile
            value = cols[base : base + full, tile:] + cols[base : base + full, :tile]
            high, low = split(value)
            place[0, :full, lane : lane + tile] = high
            place[1, :full, lane : lane + tile] = low
            for order, first in enumerate((0, half)):
                slow = slice(first, first + extra)
                down = full + order * extra
                place[0, down : down + extra, lane : lane + tile] = high[slow]
                rest = split3(value[slow])[2]
                down += 2 * extra
                place[0, down : down + extra, lane : lane + tile] = rest

    def along_rows(index):
        value = None
        for member in range(group):
            source = mid_ref.at[index % 2, member]
            field = dot3((rows_out_ref[0], rows_out_ref[1]), (source[0], source[1]))
            energy = field * field
            term = energy[:, :tile] + energy[:, tile:]
            value = term if value is None else value + term
        if index == 0:
            sum_ref[...] = value
        elif index == kernel_count // group - 1:
            aerial_ref[...] = sum_ref[...] + value
        else:
            sum_ref[...] += value

    for step in range(kernel_count // group + 2):
        if step % (kernel_count // (2 * group)) == 0 and step < kernel_count // group:
            arriving(step // (kernel_count // (2 * group))).wait()
        if step < kernel_count // group:
            multiply(step)
        if 0 <= step - 1 < kernel_count // group:
            along_cols(step - 1)
        if 0 <= step - 2:
            along_rows(step - 2)

    halfway = dot3((rb_ref[0], rb_ref[1]), split(aerial_ref[...]))
    crossed = dot3_t(split(halfway), (cb_ref[0], cb_ref[1]))
    shape = (CAP * KSIG, CAP * KSIG)
    crossed = jnp.where(iota(shape, 0) // KSIG == iota(shape, 1) // KSIG, crossed, 0.0)
    fold = ((iota(shape, 0) & (KSIG - 1)) == (iota(shape, 1) & (KSIG - 1))).astype(f32).astype(bf16)
    high = crossed.astype(bf16)
    middle, low = split(crossed - high.astype(f32))
    spread = (dot(low, fold) + dot(middle, fold)) + dot(high, fold)
    spread = jnp.where((iota(shape, 0) & (KSIG - 1)) == iota(shape, 1) // KSIG, spread, 0.0)
    signature = jnp.sum(spread.reshape(CAP, KSIG, SIGD), axis=1)
    signature = jnp.where(iota(signature.shape, 1) == 0, 0.0, signature)
    mean_square = jnp.mean(signature * signature, axis=1, keepdims=True)
    units = (signature / (KSIG * jnp.sqrt(mean_square + 1e-06))).astype(bf16)
    units_ref[...] = jnp.broadcast_to(units[None], units_ref.shape)


def match_body(
    cols_wide, rows_narrow, tile_ref, gathered_ref, library_ref, out_ref, logits_ref
):
    clip_count = tile_ref.shape[1]
    slot_count = gathered_ref.shape[0]
    device_count = out_ref.shape[0]
    own_count = clip_count // device_count
    row = tile_ref[...].astype(f32)
    peaks = []
    for first in range(0, clip_count, LANES):
        shape = (LANES, clip_count)
        clip = iota(shape, 0) + first
        other = iota(shape, 1)
        spread = jnp.broadcast_to(row, shape)
        column = jnp.sum(jnp.where(clip == other, spread, 0.0), axis=1, keepdims=True)
        before = (spread == column) & (other < clip)
        rank = jnp.sum(before.astype(f32), axis=1, keepdims=True)
        grid_row = jnp.floor((column + 0.5) * (1.0 / cols_wide))
        holder = (column - grid_row * cols_wide) * rows_narrow + grid_row
        place = (holder * CAP + rank).astype(jnp.int32)
        pick = (iota((LANES, slot_count), 1) == place).astype(f32).astype(bf16)
        units = dot(pick, gathered_ref[...]).astype(bf16)
        rows = min(512, library_ref.shape[0])
        steps = library_ref.shape[0] // rows

        def logits_of(step):
            cosine = lax.dot_general(
                library_ref[step * rows : (step + 1) * rows],
                units,
                (((1,), (1,)), ((), ())),
                preferred_element_type=f32,
            )
            return sharpness * (cosine - 1.0)

        peak = None
        for step in range(steps):
            logits = logits_of(step)
            logits_ref[step * rows : (step + 1) * rows] = logits
            local = jnp.max(logits.reshape(rows // 8, 8, LANES), axis=0)
            peak = local if peak is None else jnp.maximum(peak, local)
        peak = jnp.max(peak, axis=0, keepdims=True)
        total = jnp.zeros((8, LANES), f32)
        for step in range(steps):
            logits = logits_ref[step * rows : (step + 1) * rows]
            total += jnp.sum(jnp.exp(logits - peak).reshape(rows // 8, 8, LANES), axis=0)
        total = jnp.sum(total, axis=0, keepdims=True)
        peaks.append(peak + jnp.log(total))
    slab = peaks[0] if len(peaks) == 1 else jnp.concatenate(peaks, axis=1)
    shape = (device_count, clip_count)
    spread = jnp.broadcast_to(slab, shape)
    lane = iota((device_count, LANES), 1)
    sent = jnp.zeros((device_count, LANES), f32)
    for index in range(own_count):
        mine = iota(shape, 1) == iota(shape, 0) * own_count + index
        value = jnp.sum(jnp.where(mine, spread, 0.0), axis=1, keepdims=True)
        sent = jnp.where(lane == index, value, sent)
    out_ref[...] = sent


def call(
    body, out_shape, operands, scratch=(), limit=24, smem=(), hbm=(), out=None, flops=0, name=None
):
    spaces = [
        pltpu.SMEM if index in smem else pltpu.HBM if index in hbm else pltpu.VMEM
        for index in range(len(operands))
    ]
    return pl.pallas_call(
        body,
        out_shape=out_shape,
        in_specs=[pl.BlockSpec(memory_space=space) for space in spaces],
        out_specs=jax.tree.map(lambda _: VMEM_SPEC, out_shape) if out is None else out,
        scratch_shapes=list(scratch),
        compiler_params=pltpu.CompilerParams(vmem_limit_bytes=limit << 20),
        cost_estimate=pl.CostEstimate(flops=flops, bytes_accessed=1 << 20, transcendentals=0),
        name=name,
    )(
        *(
            pltpu.with_memory_space_constraint(value, pltpu.HBM) if index in hbm else value
            for index, value in enumerate(operands)
        )
    )


def per_device(raster, transmission, kernels, kernel_weight, library, clip_tile, clip_corner):
    tile = raster.shape[0]
    border = KSIZE // 2
    full = tile + KSIZE
    half = full // 2
    wide = 2 * ceil_to(half, LANES)
    table = {
        key: jnp.stack([jnp.asarray(part) for part in value])
        if isinstance(value, tuple)
        else jnp.asarray(value)
        for key, value in tables(tile).items()
    }
    cols_wide = lax.axis_size("wide")
    rows_narrow = lax.axis_size("narrow")
    device_count = cols_wide * rows_narrow
    both = ("wide", "narrow")
    clip_count = clip_tile.shape[0]
    real_count = 2 * kernels.shape[0]

    mask, sent = call(
        lambda *refs: edges_body(cols_wide, rows_narrow, *refs),
        (
            jax.ShapeDtypeStruct((tile, tile), bf16),
            pltpu.HBM((device_count, border, tile), bf16),
        ),
        (raster, transmission),
        scratch=(
            pltpu.VMEM((tile, tile), jnp.int32),
            pltpu.VMEM((tile, tile), bf16),
            pltpu.VMEM((4, border, tile), bf16),
            pltpu.SemaphoreType.DMA((2,)),
            pltpu.SemaphoreType.DMA((8,)),
        ),
        out=(VMEM_SPEC, pl.BlockSpec(memory_space=pltpu.HBM)),
        hbm=(0, 1),
        name="edges",
    )
    got = lax.all_to_all(sent, both, 0, 0, tiled=True)

    tile_line = clip_tile.reshape(1, clip_count)
    spectrum = (2, half, wide)
    basis = jax.ShapeDtypeStruct((2, CAP * KSIG, tile), bf16)
    filters, row_basis, col_basis, lib_units = call(
        lambda *refs: filters_body(cols_wide, *refs),
        (
            pltpu.HBM((real_count,) + spectrum, f32),
            basis,
            basis,
            jax.ShapeDtypeStruct(library.shape, bf16),
        ),
        (
            kernel_weight,
            kernels.reshape(real_count, KSIZE, KSIZE),
            table["taps_rows"],
            table["taps_cols"],
            tile_line,
            clip_corner,
            library,
        ),
        scratch=(
            pltpu.VMEM((real_count,) + spectrum, f32),
            pltpu.VMEM((2, full, 6 * KSIZE), bf16),
            pltpu.VMEM((real_count, KSIZE, KSIZE), f32),
            pltpu.VMEM(table["taps_rows"].shape, bf16),
            pltpu.VMEM(table["taps_cols"].shape, bf16),
            pltpu.VMEM((1, clip_count), jnp.int32),
            pltpu.VMEM((2, clip_count), jnp.int32),
            pltpu.VMEM(library.shape, bf16),
            pltpu.SemaphoreType.DMA((5,)),
            pltpu.SemaphoreType.DMA((real_count,)),
            pltpu.SemaphoreType.DMA(()),
        ),
        smem=(0,),
        hbm=(1, 2, 3, 4, 5, 6),
        out=(pl.BlockSpec(memory_space=pltpu.HBM), VMEM_SPEC, VMEM_SPEC, VMEM_SPEC),
        flops=4 << 30,
        name="filters",
    )
    aerial, copies = call(
        lambda *refs: image_body(cols_wide, rows_narrow, *refs),
        (
            jax.ShapeDtypeStruct((tile, tile), f32),
            jax.ShapeDtypeStruct((device_count, CAP, SIGD), bf16),
        ),
        (
            mask,
            got,
            filters,
            row_basis,
            col_basis,
            table["rows_in"],
            table["cols_in"],
            table["cols_out"],
            table["rows_out"],
        ),
        scratch=(
            pltpu.VMEM((wide, wide), bf16),
            pltpu.VMEM(spectrum, f32),
            pltpu.VMEM((2, 2, GROUP * 2 * full, wide), bf16),
            pltpu.VMEM((2, GROUP, 2, wide, wide), bf16),
            pltpu.VMEM((tile, tile), f32),
            pltpu.VMEM((real_count,) + spectrum, f32),
            pltpu.SemaphoreType.DMA((2,)),
        ),
        hbm=(2,),
        flops=6 << 30,
        name="image",
    )
    gathered = lax.all_to_all(copies, both, 0, 0, tiled=True).reshape(device_count * CAP, SIGD)
    slab = call(
        lambda *refs: match_body(cols_wide, rows_narrow, *refs),
        jax.ShapeDtypeStruct((device_count, LANES), f32),
        (tile_line, gathered, lib_units),
        scratch=(pltpu.VMEM((library.shape[0], LANES), f32),),
        limit=40,
        flops=1 << 30,
        name="match",
    )
    slab = lax.all_to_all(slab, both, 0, 0, tiled=True)[:, : clip_count // device_count]
    peak = jnp.max(slab, axis=0)
    total = jnp.sum(jnp.exp(slab - peak[None, :]), axis=0)
    scores = -(peak + jnp.log(total)) / sharpness
    return (aerial, scores)


def solution(mesh):
    placed = (
        P("narrow", "wide"),
        P("narrow", "wide"),
        P(),
        P(),
        P(("wide", "narrow"), None),
        P(),
        P(),
    )
    return jax.shard_map(
        per_device,
        mesh=mesh,
        in_specs=placed,
        out_specs=(P("narrow", "wide"), P(("wide", "narrow"))),
        check_vma=False,
    )
```
